32 devices in a mesh: row: 4 (over z), col: 8 (over y, x, core).
Axes of the slice: x: 2, y: 2, z: 4, core: 2. Of those that a mesh axis runs over, the one named last changes fastest.
Arguments:
- kernel: bfloat16 [2, 2, 2048, 1024], P(None, None, 'col', 'row'), may hold values from -0.09375 to 0.09375
- probes: bfloat16 [256, 2, 2, 2048], P(None, None, None, 'col'), may hold values from -6 to 6
- noise_var: float32 [2, 2048], P(None, 'col'), may hold values from 0.05 to 0.5
- prior_diag: float32 [1024], P('row'), may hold values from 2.2 to 4
Outputs:
- hess_probes: float32 [256, 2, 2, 2048], P('row', None, None, 'col')
The draws below stay inside these ranges and needn't reach their ends.
All inputs are finite; a program needn't handle non-finite values.
Results may differ from the reference program's by a relative error of at most 0.015.
Values may be sent and summed in bfloat16 or wider, within the bound.
No kernel may reach another device: no remote copies, remote signals or barrier semaphores. Data moves between devices by JAX's collectives and lax.ppermute only.
A program may use at most 64 MiB of HBM per device.

```python
import math
import jax
import jax.numpy as jnp

NF = 2
P_DEV = 256
NCOL = 256
NP = 1024
NR = 2048
N_ROW = 4


def block_levels(stream_key, shape, cuts, smallest, top_value):
    def one(axis_at, blocks):
        heights = jax.random.uniform(jax.random.fold_in(jax.random.fold_in(stream_key, 6), axis_at), (blocks,), jnp.float32, smallest / len(cuts), top_value / len(cuts))
        return jnp.repeat(jnp.exp(heights), shape[axis_at] // blocks).reshape((-1,) + (1,) * (len(shape) - axis_at - 1))

    level = one(*cuts[0])
    for cut in cuts[1:]:
        level = level * one(*cut)
    return level


def noise(stream_key, dims, scale, bound, split=(), dtype=jnp.bfloat16):
    array = jax.random.normal(stream_key, dims, jnp.float32) * scale
    if len(split) > 0:
        array = block_levels(stream_key, dims, split, -0.22, 0.18) * array
    return jnp.clip(array, min=-bound, max=bound).astype(dtype)


def setup_inputs(seed: int = 0) -> dict:
    seeds = jax.random.split(jax.random.key(seed), 5)
    return {
        "kernel": noise(seeds[0], (NF, 2, NR, NP), (2 * NR) ** -0.5, 0.09375, ((2, 8), (3, 4))),
        "probes": noise(seeds[1], (NCOL, NF, 2, NR), 1.0, 6.0, ((3, 8),)),
        "noise_var": jnp.clip(jnp.exp(math.log(0.5) - 2.3025851 * jax.random.uniform(seeds[2], (NF, NR), jnp.float32) ** block_levels(seeds[2], (NF, NR), ((1, 8),), -0.2, 0.2)), 0.05, 0.5),
        "prior_diag": jnp.clip(2.2 + 1.8 * jax.random.uniform(seeds[3], (NP,), jnp.float32) ** block_levels(seeds[3], (NP,), ((0, 4),), -0.2, 0.2), 2.2, 4.0),
    }


def sweep(field, coef):
    padded = jnp.pad(field, ((0, 0), (1, 1)))
    return coef * field - padded[:, :-2] - padded[:, 2:]


def reference(kernel, probes, noise_var, prior_diag):
    adjoint = []
    for freq_no in range(NF):
        real_part = probes[:, freq_no, 0, :]
        imag_part = probes[:, freq_no, 1, :]
        upper = jnp.concatenate([real_part, imag_part], axis=1)
        lower = jnp.concatenate([imag_part, -real_part], axis=1)
        stacked = kernel[freq_no].reshape(2 * NR, NP)
        adjoint.append(jnp.dot(jnp.concatenate([upper, lower], axis=0), stacked, preferred_element_type=jnp.float32))
    adjoint = jnp.stack(adjoint).reshape(NF * 2 * NCOL, NP)
    smooth = sweep(sweep(adjoint, prior_diag), prior_diag)
    smooth = smooth.astype(jnp.bfloat16).reshape(NF, 2, NCOL, NP)
    total = jnp.zeros((NCOL, NF, 2, NR), jnp.float32)
    for block in range(N_ROW):
        low = block * P_DEV
        parts = []
        for freq_no in range(NF):
            field = jnp.concatenate([smooth[freq_no, 0, :, low:low + P_DEV], smooth[freq_no, 1, :, low:low + P_DEV]], axis=0)
            stacked = kernel[freq_no, :, :, low:low + P_DEV].reshape(2 * NR, P_DEV)
            prod = jax.lax.dot_general(field, stacked, (((1,), (1,)), ((), ())), preferred_element_type=jnp.float32)
            real_out = prod[:NCOL, :NR] - prod[NCOL:, NR:]
            imag_out = prod[NCOL:, :NR] + prod[:NCOL, NR:]
            parts.append(jnp.stack([real_out, imag_out], axis=1))
        partial_value = jnp.stack(parts, axis=1).astype(jnp.bfloat16)
        total = total + partial_value.astype(jnp.float32)
    return total + noise_var[None, :, None, :] * probes.astype(jnp.float32)
```

```python
import functools

import jax
import jax.numpy as jnp
from jax import lax
from jax.experimental import pallas as pl
from jax.experimental.pallas import tpu as pltpu
from jax.sharding import PartitionSpec as P

BF = jnp.bfloat16
F32 = jnp.float32
LANES = 128
VMEM = pl.BlockSpec(memory_space=pltpu.VMEM)


def call(body, name, ins, outs, scratch=()):
    return pl.pallas_call(
        body,
        name=name,
        in_specs=[VMEM] * len(ins),
        out_specs=[VMEM] * len(outs),
        out_shape=[jax.ShapeDtypeStruct(*o) for o in outs],
        scratch_shapes=list(scratch),
    )(*ins)


def parity():
    return lax.rem(lax.axis_index("col"), 2)


def dot_nt(left, right):
    return lax.dot_general(left, right, (((1,), (1,)), ((), ())), preferred_element_type=F32)


def dot_nn(left, right):
    return jnp.dot(left, right, preferred_element_type=F32)


def pair_perm(axis, step):
    return [(i, i ^ step) for i in range(lax.axis_size(axis))]


def adjoint_body(swap, x_ref, k_ref, o_ref, u_ref):
    rows = x_ref.shape[0] // 4
    width = k_ref.shape[3]
    freq = parity()
    if swap:
        freq = 1 - freq
    x = x_ref[...]
    tiles = width // LANES
    for part in range(2):
        y = dot_nn(x, k_ref[freq, part])
        for t in range(tiles):
            u_ref[part * tiles + t] = y[:, t * LANES:(t + 1) * LANES]
    real = pl.ds(2 * freq, rows, stride=4)
    imag = pl.ds(2 * freq + 1, rows, stride=4)
    for t in range(tiles):
        at = slice(t * LANES, (t + 1) * LANES)
        o_ref[:rows, at] = (u_ref[t, real, :] + u_ref[tiles + t, imag, :]).astype(o_ref.dtype)
        o_ref[rows:, at] = (u_ref[t, imag, :] - u_ref[tiles + t, real, :]).astype(o_ref.dtype)


def edges_body(k_ref, d_ref, low_ref, high_ref):
    freqs, _, rows, width = k_ref.shape
    at = lax.broadcasted_iota(jnp.int32, (8, width), 0)
    place = lax.broadcasted_iota(jnp.int32, (8, width), 1)
    first = jnp.where((at < 2) & (place == at), 1.0, 0.0).astype(BF)
    last = jnp.where((at < 2) & (place == at + width - 2), 1.0, 0.0).astype(BF)
    for f in range(freqs):
        for c in range(2):
            lo = (f * 2 + c) * rows
            low_ref[:, lo:lo + rows] = dot_nt(last, k_ref[f, c]).astype(BF)
            high_ref[:, lo:lo + rows] = dot_nt(first, k_ref[f, c]).astype(BF)
    coef = d_ref[...]
    spot = lax.broadcasted_iota(jnp.int32, coef.shape, 1)
    for ref, where in ((low_ref, width - 1), (high_ref, 0)):
        left = jnp.sum(jnp.where(spot == where, coef, 0.0), axis=1, keepdims=True)
        for row in range(2, 5):
            piece = left.astype(BF)
            ref[row:row + 1, :] = jnp.broadcast_to(piece, (1, ref.shape[1]))
            left = left - piece.astype(F32)


def operator_body(k_ref, d_ref, low_ref, high_ref, o_ref):
    freqs, _, rows, width = k_ref.shape
    at = lax.axis_index("row")
    coef = d_ref[...]
    row_at = lax.broadcasted_iota(jnp.int32, (width, width), 0)
    col_at = lax.broadcasted_iota(jnp.int32, (width, width), 1)
    wide = jnp.broadcast_to(coef, (width, width))
    tall = jnp.sum(jnp.where(row_at == col_at, wide, 0.0), axis=1, keepdims=True)
    gap = jnp.abs(row_at - col_at)
    edge = ((row_at == 0) & (at == 0)) | ((row_at == width - 1) & (at == lax.axis_size("row") - 1))
    centre = wide * wide + jnp.where(edge, 1.0, 2.0)
    stencil = jnp.where(gap == 0, centre, jnp.where(gap == 1, -(wide + tall), jnp.where(gap == 2, 1.0, 0.0)))
    upper = stencil.astype(BF)
    lower = (stencil - upper.astype(F32)).astype(BF)
    low = low_ref[...].astype(F32)
    high = high_ref[...].astype(F32)
    low_coef = low[2:3, :rows] + low[3:4, :rows] + low[4:5, :rows] + coef[:, :1]
    high_coef = high[2:3, :rows] + high[3:4, :rows] + high[4:5, :rows] + coef[:, width - 1:]
    for f in range(freqs):
        for c in range(2):
            block = k_ref[f, c]
            value = dot_nt(upper, block) + dot_nt(lower, block)
            lo = (f * 2 + c) * rows
            before = low[0:2, lo:lo + rows]
            after = high[0:2, lo:lo + rows]
            head = jnp.concatenate(
                [before[0:1] - low_coef * before[1:2], before[1:2]], axis=0
            )
            tail = jnp.concatenate(
                [after[0:1], after[1:2] - high_coef * after[0:1]], axis=0
            )
            value = value + jnp.concatenate(
                [head, jnp.zeros((width - 4, rows), F32), tail], axis=0
            )
            o_ref[f, c] = value.astype(BF)


def split_body(own_ref, got_ref, keep_ref, *send_refs):
    size = keep_ref.shape[0]
    me = lax.div(lax.axis_index("col"), 2)

    def piece(chip):
        rows = pl.ds(pl.multiple_of(chip * size, size), size)
        return own_ref[rows, :] + got_ref[rows, :].astype(F32)

    keep_ref[...] = piece(me)
    for step, ref in enumerate(send_refs):
        ref[...] = piece(jnp.bitwise_xor(me, step + 1)).astype(BF)


def sum_body(keep_ref, *refs):
    total = keep_ref[...]
    for ref in refs[:-1]:
        total = total + ref[...].astype(F32)
    refs[-1][...] = total.astype(BF)


def join_body(mine_ref, *refs):
    size = mine_ref.shape[0]
    me = lax.div(lax.axis_index("col"), 2)
    out = refs[-1]
    for step, ref in enumerate((mine_ref,) + refs[:-1]):
        chip = jnp.bitwise_xor(me, step)
        out[pl.ds(pl.multiple_of(chip * size, size), size), :] = ref[...]


def predict_body(swap, a_ref, k_ref, keep_ref, *refs):
    freq = parity()
    if swap:
        freq = 1 - freq
    probes = a_ref.shape[0] // 2
    size = keep_ref.shape[0] // 2
    me = lax.axis_index("row")
    k_real = k_ref[freq, 0]
    k_imag = k_ref[freq, 1]
    for step in range(len(refs), -1, -1):
        block = jnp.bitwise_xor(me, step)
        start = pl.multiple_of(block * size, size)
        real = a_ref[pl.ds(start, size), :]
        imag = a_ref[pl.ds(pl.multiple_of(probes + start, size), size), :]
        both = jnp.concatenate([real, imag], axis=0)
        by_real = dot_nn(both, k_real)
        by_imag = dot_nn(both, k_imag)
        ref = keep_ref if step == 0 else refs[step - 1]
        ref[:size] = (by_real[:size] - by_imag[size:]).astype(ref.dtype)
        ref[size:] = (by_real[size:] + by_imag[:size]).astype(ref.dtype)


def final_body(peers, x_ref, noise_ref, *refs):
    out_ref, s_ref = refs[-2:]
    rows = out_ref.shape[0]
    size = rows // 4
    me = lax.axis_index("row")
    freq = parity()
    for which in range(2):
        group = refs[which * (peers + 1):(which + 1) * (peers + 1)]
        total = group[0][...]
        for ref in group[1:]:
            total = total + ref[...].astype(F32)
        f = freq if which == 0 else 1 - freq
        for t in range(s_ref.shape[0]):
            at = slice(t * LANES, (t + 1) * LANES)
            s_ref[t, pl.ds(2 * f, size, stride=4), :] = total[:size, at]
            s_ref[t, pl.ds(2 * f + 1, size, stride=4), :] = total[size:, at]
    x = x_ref[pl.ds(pl.multiple_of(me * rows, rows), rows), :].astype(F32)
    kind = lax.rem(lax.broadcasted_iota(jnp.int32, x.shape, 0), 4)
    noise = jnp.where(kind < 2, noise_ref[0:1, :], noise_ref[1:2, :])
    extra = noise * x
    for t in range(s_ref.shape[0]):
        at = slice(t * LANES, (t + 1) * LANES)
        out_ref[:, at] = s_ref[t] + extra[:, at]


def all_sum(x, kernel):
    rows = x.shape[0] // 2
    width = kernel.shape[3]
    count = lax.axis_size("col")
    scratch = (pltpu.VMEM((2 * width // LANES, x.shape[0], LANES), F32),)
    other = call(functools.partial(adjoint_body, True), "adjoint_other", (x, kernel), [((rows, width), BF)], scratch)[0]
    got = lax.ppermute(other, "col", pair_perm("col", 1))
    own = call(functools.partial(adjoint_body, False), "adjoint_own", (x, kernel), [((rows, width), F32)], scratch)[0]
    chips = count // 2
    if chips > 4:
        part = own + got.astype(F32)
        both = jnp.where(parity() == 0, jnp.stack([part, 0 * part]), jnp.stack([0 * part, part]))
        both = lax.psum(both, "col").astype(BF)
        mine = lax.dynamic_index_in_dim(both, parity(), 0, keepdims=False)
        return mine, lax.dynamic_index_in_dim(both, 1 - parity(), 0, keepdims=False)
    size = rows // chips
    keep, *sends = call(
        split_body, "split", (own, got), [((size, width), F32)] + [((size, width), BF)] * (chips - 1)
    )
    got = [lax.ppermute(v, "col", pair_perm("col", 2 * (d + 1))) for d, v in enumerate(sends)]
    mine = call(sum_body, "sum", (keep, *got), [((size, width), BF)])[0]
    got = [lax.ppermute(mine, "col", pair_perm("col", 2 * (d + 1))) for d in range(chips - 1)]
    mine = call(join_body, "join", (mine, *got), [((rows, width), BF)])[0]
    return mine, lax.ppermute(mine, "col", pair_perm("col", 1))


def shards(kernel, probes, noise_var, prior_diag):
    rows_own = kernel.shape[2]
    width = kernel.shape[3]
    count = probes.shape[0]
    blocks = lax.axis_size("row")
    x = probes.reshape(-1, rows_own)
    coef = prior_diag[None, :]
    low, high = call(edges_body, "edges", (kernel, coef), [((8, 4 * rows_own), BF)] * 2)
    low = lax.ppermute(low, "row", [(i, i + 1) for i in range(blocks - 1)])
    high = lax.ppermute(high, "row", [(i + 1, i) for i in range(blocks - 1)])
    mine, other = all_sum(x, kernel)
    operator = call(operator_body, "operator", (kernel, coef, low, high), [((2, 2, width, rows_own), BF)])[0]
    size = count // blocks
    groups = []
    for swap, field in ((False, mine), (True, other)):
        keep, *sends = call(
            functools.partial(predict_body, swap),
            "predict_other" if swap else "predict_own",
            (field, operator),
            [((2 * size, rows_own), F32)] + [((2 * size, rows_own), BF)] * (blocks - 1),
        )
        groups.append(keep)
        groups += [lax.ppermute(v, "row", pair_perm("row", d + 1)) for d, v in enumerate(sends)]
    out = call(
        functools.partial(final_body, blocks - 1),
        "final",
        (x, noise_var, *groups),
        [((4 * size, rows_own), F32)],
        (pltpu.VMEM((rows_own // LANES, 4 * size, LANES), F32),),
    )[0]
    return out.reshape(size, 2, 2, rows_own)


def solution(mesh):
    in_specs = (P(None, None, "col", "row"), P(None, None, None, "col"), P(None, "col"), P("row"))
    out_specs = P("row", None, None, "col")
    return jax.shard_map(shards, mesh=mesh, in_specs=in_specs, out_specs=out_specs, check_vma=False)
```

```python
import functools

import jax
import jax.numpy as jnp
from jax import lax
from jax.experimental import pallas as pl
from jax.experimental.pallas import tpu as pltpu
from jax.sharding import PartitionSpec as P

BF = jnp.bfloat16
F32 = jnp.float32
LANES = 128
VMEM = pl.BlockSpec(memory_space=pltpu.VMEM)


def call(body, name, ins, outs, scratch=()):
    return pl.pallas_call(
        body,
        name=name,
        in_specs=[VMEM] * len(ins),
        out_specs=[VMEM] * len(outs),
        out_shape=[pltpu.VMEM(*o) for o in outs],
        scratch_shapes=list(scratch),
    )(*[pltpu.with_memory_space_constraint(v, pltpu.VMEM) for v in ins])


def parity():
    return lax.rem(lax.axis_index("col"), 2)


def dot_nt(left, right):
    return lax.dot_general(left, right, (((1,), (1,)), ((), ())), preferred_element_type=F32)


def dot_nn(left, right):
    return jnp.dot(left, right, preferred_element_type=F32)


def pair_perm(axis, step):
    return [(i, i ^ step) for i in range(lax.axis_size(axis))]


def adjoint_body(swap, x_ref, k_ref, o_ref, *refs):
    u_ref = refs[-1]
    rows = u_ref.shape[1] // 4
    width = k_ref.shape[3]
    freq = parity()
    if swap:
        freq = 1 - freq
    x = x_ref[...]
    if swap:
        x = x.reshape(refs[0].shape)
        refs[0][...] = x
    tiles = width // LANES
    for part in range(2):
        y = dot_nn(x, k_ref[freq, part])
        for t in range(tiles):
            u_ref[part * tiles + t] = y[:, t * LANES:(t + 1) * LANES]
    real = pl.ds(2 * freq, rows, stride=4)
    imag = pl.ds(2 * freq + 1, rows, stride=4)
    for t in range(tiles):
        at = slice(t * LANES, (t + 1) * LANES)
        o_ref[:rows, at] = (u_ref[t, real, :] + u_ref[tiles + t, imag, :]).astype(o_ref.dtype)
        o_ref[rows:, at] = (u_ref[t, imag, :] - u_ref[tiles + t, real, :]).astype(o_ref.dtype)


def edges_body(k_ref, d_ref, low_ref, high_ref):
    freqs, _, rows, width = k_ref.shape
    at = lax.broadcasted_iota(jnp.int32, (8, width), 0)
    place = lax.broadcasted_iota(jnp.int32, (8, width), 1)
    first = jnp.where((at < 2) & (place == at), 1.0, 0.0).astype(BF)
    last = jnp.where((at < 2) & (place == at + width - 2), 1.0, 0.0).astype(BF)
    for f in range(freqs):
        for c in range(2):
            lo = (f * 2 + c) * rows
            low_ref[:, lo:lo + rows] = dot_nt(last, k_ref[f, c]).astype(BF)
            high_ref[:, lo:lo + rows] = dot_nt(first, k_ref[f, c]).astype(BF)
    coef = d_ref[...]
    spot = lax.broadcasted_iota(jnp.int32, coef.shape, 1)
    for ref, where in ((low_ref, width - 1), (high_ref, 0)):
        left = jnp.sum(jnp.where(spot == where, coef, 0.0), axis=1, keepdims=True)
        for row in range(2, 5):
            piece = left.astype(BF)
            ref[row:row + 1, :] = jnp.broadcast_to(piece, (1, ref.shape[1]))
            left = left - piece.astype(F32)


def operator_body(k_ref, d_ref, low_ref, high_ref, o_ref):
    freqs, _, rows, width = k_ref.shape
    at = lax.axis_index("row")
    coef = d_ref[...]
    row_at = lax.broadcasted_iota(jnp.int32, (width, width), 0)
    col_at = lax.broadcasted_iota(jnp.int32, (width, width), 1)
    wide = jnp.broadcast_to(coef, (width, width))
    tall = jnp.sum(jnp.where(row_at == col_at, wide, 0.0), axis=1, keepdims=True)
    gap = jnp.abs(row_at - col_at)
    edge = ((row_at == 0) & (at == 0)) | ((row_at == width - 1) & (at == lax.axis_size("row") - 1))
    centre = wide * wide + jnp.where(edge, 1.0, 2.0)
    stencil = jnp.where(gap == 0, centre, jnp.where(gap == 1, -(wide + tall), jnp.where(gap == 2, 1.0, 0.0)))
    upper = stencil.astype(BF)
    lower = (stencil - upper.astype(F32)).astype(BF)
    low = low_ref[...].astype(F32)
    high = high_ref[...].astype(F32)
    low_coef = low[2:3, :rows] + low[3:4, :rows] + low[4:5, :rows] + coef[:, :1]
    high_coef = high[2:3, :rows] + high[3:4, :rows] + high[4:5, :rows] + coef[:, width - 1:]
    for f in range(freqs):
        for c in range(2):
            block = k_ref[f, c]
            value = dot_nt(upper, block) + dot_nt(lower, block)
            lo = (f * 2 + c) * rows
            before = low[0:2, lo:lo + rows]
            after = high[0:2, lo:lo + rows]
            head = jnp.concatenate(
                [before[0:1] - low_coef * before[1:2], before[1:2]], axis=0
            )
            tail = jnp.concatenate(
                [after[0:1], after[1:2] - high_coef * after[0:1]], axis=0
            )
            value = value + jnp.concatenate(
                [head, jnp.zeros((width - 4, rows), F32), tail], axis=0
            )
            o_ref[f, c] = value.astype(BF)


def split_body(own_ref, got_ref, keep_ref, *send_refs):
    size = keep_ref.shape[0]
    me = lax.div(lax.axis_index("col"), 2)

    def piece(chip):
        rows = pl.ds(pl.multiple_of(chip * size, size), size)
        return own_ref[rows, :] + got_ref[rows, :].astype(F32)

    keep_ref[...] = piece(me)
    for step, ref in enumerate(send_refs):
        ref[...] = piece(jnp.bitwise_xor(me, step + 1)).astype(BF)


def sum_body(keep_ref, *refs):
    total = keep_ref[...]
    for ref in refs[:-1]:
        total = total + ref[...].astype(F32)
    refs[-1][...] = total.astype(BF)


def join_body(mine_ref, *refs):
    size = mine_ref.shape[0]
    me = lax.div(lax.axis_index("col"), 2)
    out = refs[-1]
    for step, ref in enumerate((mine_ref,) + refs[:-1]):
        chip = jnp.bitwise_xor(me, step)
        out[pl.ds(pl.multiple_of(chip * size, size), size), :] = ref[...]


def predict_body(swap, a_ref, k_ref, keep_ref, *refs):
    freq = parity()
    if swap:
        freq = 1 - freq
    probes = a_ref.shape[0] // 2
    size = keep_ref.shape[0] // 2
    me = lax.axis_index("row")
    k_real = k_ref[freq, 0]
    k_imag = k_ref[freq, 1]
    for step in range(len(refs), -1, -1):
        block = jnp.bitwise_xor(me, step)
        start = pl.multiple_of(block * size, size)
        real = a_ref[pl.ds(start, size), :]
        imag = a_ref[pl.ds(pl.multiple_of(probes + start, size), size), :]
        both = jnp.concatenate([real, imag], axis=0)
        by_real = dot_nn(both, k_real)
        by_imag = dot_nn(both, k_imag)
        ref = keep_ref if step == 0 else refs[step - 1]
        ref[:size] = (by_real[:size] - by_imag[size:]).astype(ref.dtype)
        ref[size:] = (by_real[size:] + by_imag[:size]).astype(ref.dtype)


def final_body(peers, x_ref, noise_ref, *refs):
    out_ref, s_ref = refs[-2:]
    size = out_ref.shape[0]
    rows = 4 * size
    me = lax.axis_index("row")
    freq = parity()
    for which in range(2):
        group = refs[which * (peers + 1):(which + 1) * (peers + 1)]
        total = group[0][...]
        for ref in group[1:]:
            total = total + ref[...].astype(F32)
        f = freq if which == 0 else 1 - freq
        for t in range(s_ref.shape[0]):
            at = slice(t * LANES, (t + 1) * LANES)
            s_ref[t, pl.ds(2 * f, size, stride=4), :] = total[:size, at]
            s_ref[t, pl.ds(2 * f + 1, size, stride=4), :] = total[size:, at]
    x = x_ref[pl.ds(pl.multiple_of(me * rows, rows), rows), :].astype(F32)
    kind = lax.rem(lax.broadcasted_iota(jnp.int32, x.shape, 0), 4)
    noise = jnp.where(kind < 2, noise_ref[0:1, :], noise_ref[1:2, :])
    values = jnp.concatenate([s_ref[t] for t in range(s_ref.shape[0])], axis=1) + noise * x
    out_ref[...] = values.reshape(out_ref.shape)


def all_sum(probes, kernel):
    rows = 2 * probes.shape[0]
    width = kernel.shape[3]
    count = lax.axis_size("col")
    flat = (2 * rows, probes.shape[3])
    scratch = (pltpu.VMEM((2 * width // LANES, 2 * rows, LANES), F32),)
    other, x = call(
        functools.partial(adjoint_body, True),
        "adjoint_other",
        (probes, kernel),
        [((rows, width), BF), (flat, BF)],
        scratch,
    )
    got = lax.ppermute(other, "col", pair_perm("col", 1))
    own = call(functools.partial(adjoint_body, False), "adjoint_own", (x, kernel), [((rows, width), F32)], scratch)[0]
    chips = count // 2
    if chips > 4:
        part = own + got.astype(F32)
        both = jnp.where(parity() == 0, jnp.stack([part, 0 * part]), jnp.stack([0 * part, part]))
        both = lax.psum(both, "col").astype(BF)
        mine = lax.dynamic_index_in_dim(both, parity(), 0, keepdims=False)
        return x, mine, lax.dynamic_index_in_dim(both, 1 - parity(), 0, keepdims=False)
    size = rows // chips
    keep, *sends = call(
        split_body, "split", (own, got), [((size, width), F32)] + [((size, width), BF)] * (chips - 1)
    )
    got = [lax.ppermute(v, "col", pair_perm("col", 2 * (d + 1))) for d, v in enumerate(sends)]
    mine = call(sum_body, "sum", (keep, *got), [((size, width), BF)])[0]
    got = [lax.ppermute(mine, "col", pair_perm("col", 2 * (d + 1))) for d in range(chips - 1)]
    mine = call(join_body, "join", (mine, *got), [((rows, width), BF)])[0]
    return x, mine, lax.ppermute(mine, "col", pair_perm("col", 1))


def shards(kernel, probes, noise_var, prior_diag):
    rows_own = kernel.shape[2]
    width = kernel.shape[3]
    count = probes.shape[0]
    blocks = lax.axis_size("row")
    coef = prior_diag[None, :]
    low, high = call(edges_body, "edges", (kernel, coef), [((8, 4 * rows_own), BF)] * 2)
    low = lax.ppermute(low, "row", [(i, i + 1) for i in range(blocks - 1)])
    high = lax.ppermute(high, "row", [(i + 1, i) for i in range(blocks - 1)])
    x, mine, other = all_sum(probes, kernel)
    operator = call(operator_body, "operator", (kernel, coef, low, high), [((2, 2, width, rows_own), BF)])[0]
    size = count // blocks
    groups = []
    for swap, field in ((False, mine), (True, other)):
        keep, *sends = call(
            functools.partial(predict_body, swap),
            "predict_other" if swap else "predict_own",
            (field, operator),
            [((2 * size, rows_own), F32)] + [((2 * size, rows_own), BF)] * (blocks - 1),
        )
        groups.append(keep)
        groups += [lax.ppermute(v, "row", pair_perm("row", d + 1)) for d, v in enumerate(sends)]
    out = call(
        functools.partial(final_body, blocks - 1),
        "final",
        (x, noise_var, *groups),
        [((size,) + probes.shape[1:3] + (rows_own,), F32)],
        (pltpu.VMEM((rows_own // LANES, 4 * size, LANES), F32),),
    )[0]
    return out


def solution(mesh):
    in_specs = (P(None, None, "col", "row"), P(None, None, None, "col"), P(None, "col"), P("row"))
    out_specs = P("row", None, None, "col")
    return jax.shard_map(shards, mesh=mesh, in_specs=in_specs, out_specs=out_specs, check_vma=False)
```

```python
import functools

import jax
import jax.numpy as jnp
from jax import lax
from jax.experimental import pallas as pl
from jax.experimental.pallas import tpu as pltpu
from jax.sharding import PartitionSpec as P


BF = jnp.bfloat16
F32 = jnp.float32
LANES = 128
VMEM = pl.BlockSpec(memory_space=pltpu.VMEM)


def call(body, ins, outs, scratch=()):
    return pl.pallas_call(
        body,
        in_specs=[VMEM] * len(ins),
        out_specs=[VMEM] * len(outs),
        out_shape=[pltpu.VMEM(*o) for o in outs],
        scratch_shapes=list(scratch),
    )(*[pltpu.with_memory_space_constraint(v, pltpu.VMEM) for v in ins])


def parity():
    return lax.rem(lax.axis_index("col"), 2)


def dot_nt(left, right):
    return lax.dot_general(left, right, (((1,), (1,)), ((), ())), preferred_element_type=F32)


def dot_nn(left, right):
    return jnp.dot(left, right, preferred_element_type=F32)


def pair_perm(axis, step):
    return [(i, i ^ step) for i in range(lax.axis_size(axis))]


def adjoint_body(swap, x_ref, k_ref, o_ref, *refs):
    u_ref = refs[-1]
    rows = u_ref.shape[1] // 4
    width = k_ref.shape[3]
    freq = parity()
    if swap:
        freq = 1 - freq
    x = x_ref[...]
    if swap:
        x = x.reshape(refs[0].shape)
        refs[0][...] = x
    tiles = width // LANES
    for part in range(2):
        y = dot_nn(x, k_ref[freq, part])
        for t in range(tiles):
            u_ref[part * tiles + t] = y[:, t * LANES:(t + 1) * LANES]
    real = pl.ds(2 * freq, rows, stride=4)
    imag = pl.ds(2 * freq + 1, rows, stride=4)
    for t in range(tiles):
        at = slice(t * LANES, (t + 1) * LANES)
        o_ref[:rows, at] = (u_ref[t, real, :] + u_ref[tiles + t, imag, :]).astype(o_ref.dtype)
        o_ref[rows:, at] = (u_ref[t, imag, :] - u_ref[tiles + t, real, :]).astype(o_ref.dtype)


def edges_body(k_ref, d_ref, low_ref, high_ref):
    freqs, _, rows, width = k_ref.shape
    at = lax.broadcasted_iota(jnp.int32, (8, width), 0)
    place = lax.broadcasted_iota(jnp.int32, (8, width), 1)
    first = jnp.where((at < 2) & (place == at), 1.0, 0.0).astype(BF)
    last = jnp.where((at < 2) & (place == at + width - 2), 1.0, 0.0).astype(BF)
    for f in range(freqs):
        for c in range(2):
            lo = (f * 2 + c) * rows
            low_ref[:, lo:lo + rows] = dot_nt(last, k_ref[f, c]).astype(BF)
            high_ref[:, lo:lo + rows] = dot_nt(first, k_ref[f, c]).astype(BF)
    coef = d_ref[...]
    spot = lax.broadcasted_iota(jnp.int32, coef.shape, 1)
    for ref, where in ((low_ref, width - 1), (high_ref, 0)):
        left = jnp.sum(jnp.where(spot == where, coef, 0.0), axis=1, keepdims=True)
        for row in range(2, 5):
            piece = left.astype(BF)
            ref[row:row + 1, :] = jnp.broadcast_to(piece, (1, ref.shape[1]))
            left = left - piece.astype(F32)


def operator_body(k_ref, d_ref, low_ref, high_ref, o_ref):
    freqs, _, rows, width = k_ref.shape
    at = lax.axis_index("row")
    coef = d_ref[...]
    row_at = lax.broadcasted_iota(jnp.int32, (width, width), 0)
    col_at = lax.broadcasted_iota(jnp.int32, (width, width), 1)
    wide = jnp.broadcast_to(coef, (width, width))
    tall = jnp.sum(jnp.where(row_at == col_at, wide, 0.0), axis=1, keepdims=True)
    gap = jnp.abs(row_at - col_at)
    edge = ((row_at == 0) & (at == 0)) | ((row_at == width - 1) & (at == lax.axis_size("row") - 1))
    centre = wide * wide + jnp.where(edge, 1.0, 2.0)
    stencil = jnp.where(gap == 0, centre, jnp.where(gap == 1, -(wide + tall), jnp.where(gap == 2, 1.0, 0.0)))
    upper = stencil.astype(BF)
    lower = (stencil - upper.astype(F32)).astype(BF)
    low = low_ref[...].astype(F32)
    high = high_ref[...].astype(F32)
    low_coef = low[2:3, :rows] + low[3:4, :rows] + low[4:5, :rows] + coef[:, :1]
    high_coef = high[2:3, :rows] + high[3:4, :rows] + high[4:5, :rows] + coef[:, width - 1:]
    for f in range(freqs):
        for c in range(2):
            block = k_ref[f, c]
            value = dot_nt(upper, block) + dot_nt(lower, block)
            lo = (f * 2 + c) * rows
            before = low[0:2, lo:lo + rows]
            after = high[0:2, lo:lo + rows]
            head = jnp.concatenate(
                [before[0:1] - low_coef * before[1:2], before[1:2]], axis=0
            )
            tail = jnp.concatenate(
                [after[0:1], after[1:2] - high_coef * after[0:1]], axis=0
            )
            value = value + jnp.concatenate(
                [head, jnp.zeros((width - 4, rows), F32), tail], axis=0
            )
            o_ref[f, c] = value.astype(BF)


def split_body(own_ref, got_ref, keep_ref, *send_refs):
    size = keep_ref.shape[0]
    me = lax.div(lax.axis_index("col"), 2)

    def piece(chip):
        rows = pl.ds(pl.multiple_of(chip * size, size), size)
        return own_ref[rows, :] + got_ref[rows, :].astype(F32)

    keep_ref[...] = piece(me)
    for step, ref in enumerate(send_refs):
        ref[...] = piece(jnp.bitwise_xor(me, step + 1)).astype(BF)


def fence_body(d_ref, o_ref):
    o_ref[...] = jnp.zeros_like(o_ref)


def sum_body(keep_ref, fence_ref, *refs):
    total = keep_ref[...]
    for ref in refs[:-1]:
        total = total + ref[...].astype(F32)
    refs[-1][...] = total.astype(BF)


def join_body(mine_ref, *refs):
    size = mine_ref.shape[0]
    me = lax.div(lax.axis_index("col"), 2)
    out = refs[-1]
    for step, ref in enumerate((mine_ref,) + refs[:-1]):
        chip = jnp.bitwise_xor(me, step)
        out[pl.ds(pl.multiple_of(chip * size, size), size), :] = ref[...]


def predict_body(swap, a_ref, k_ref, keep_ref, *refs):
    freq = parity()
    if swap:
        freq = 1 - freq
    probes = a_ref.shape[0] // 2
    size = keep_ref.shape[0] // 2
    me = lax.axis_index("row")
    k_real = k_ref[freq, 0]
    k_imag = k_ref[freq, 1]
    for step in range(len(refs), -1, -1):
        block = jnp.bitwise_xor(me, step)
        start = pl.multiple_of(block * size, size)
        real = a_ref[pl.ds(start, size), :]
        imag = a_ref[pl.ds(pl.multiple_of(probes + start, size), size), :]
        both = jnp.concatenate([real, imag], axis=0)
        by_real = dot_nn(both, k_real)
        by_imag = dot_nn(both, k_imag)
        ref = keep_ref if step == 0 else refs[step - 1]
        ref[:size] = (by_real[:size] - by_imag[size:]).astype(ref.dtype)
        ref[size:] = (by_real[size:] + by_imag[:size]).astype(ref.dtype)


def final_body(peers, x_ref, noise_ref, *refs):
    out_ref, s_ref = refs[-2:]
    size = out_ref.shape[0]
    rows = 4 * size
    me = lax.axis_index("row")
    freq = parity()
    for which in range(2):
        group = refs[which * (peers + 1):(which + 1) * (peers + 1)]
        total = group[0][...]
        for ref in group[1:]:
            total = total + ref[...].astype(F32)
        f = freq if which == 0 else 1 - freq
        for t in range(s_ref.shape[0]):
            at = slice(t * LANES, (t + 1) * LANES)
            s_ref[t, pl.ds(2 * f, size, stride=4), :] = total[:size, at]
            s_ref[t, pl.ds(2 * f + 1, size, stride=4), :] = total[size:, at]
    x = x_ref[pl.ds(pl.multiple_of(me * rows, rows), rows), :].astype(F32)
    kind = lax.rem(lax.broadcasted_iota(jnp.int32, x.shape, 0), 4)
    noise = jnp.where(kind < 2, noise_ref[0:1, :], noise_ref[1:2, :])
    values = jnp.concatenate([s_ref[t] for t in range(s_ref.shape[0])], axis=1) + noise * x
    out_ref[...] = values.reshape(out_ref.shape)


def all_sum(probes, kernel, coef):
    rows = 2 * probes.shape[0]
    width = kernel.shape[3]
    count = lax.axis_size("col")
    flat = (2 * rows, probes.shape[3])
    scratch = (pltpu.VMEM((2 * width // LANES, 2 * rows, LANES), F32),)
    other, x = call(functools.partial(adjoint_body, True), (probes, kernel), [((rows, width), BF), (flat, BF)], scratch)
    got = lax.ppermute(other, "col", pair_perm("col", 1))
    own = call(functools.partial(adjoint_body, False), (x, kernel), [((rows, width), F32)], scratch)[0]
    chips = count // 2
    if chips > 4:
        part = own + got.astype(F32)
        both = jnp.where(parity() == 0, jnp.stack([part, 0 * part]), jnp.stack([0 * part, part]))
        both = lax.psum(both, "col").astype(BF)
        mine = lax.dynamic_index_in_dim(both, parity(), 0, keepdims=False)
        return x, mine, lax.dynamic_index_in_dim(both, 1 - parity(), 0, keepdims=False)
    size = rows // chips
    keep, *sends = call(split_body, (own, got), [((size, width), F32)] + [((size, width), BF)] * (chips - 1))
    got = [lax.ppermute(v, "col", pair_perm("col", 2 * (d + 1))) for d, v in enumerate(sends)]
    fence = call(fence_body, (coef,), [((8, LANES), F32)])[0]
    mine = call(sum_body, (keep, fence, *got), [((size, width), BF)])[0]
    got = [lax.ppermute(mine, "col", pair_perm("col", 2 * (d + 1))) for d in range(chips - 1)]
    mine = call(join_body, (mine, *got), [((rows, width), BF)])[0]
    return x, mine, lax.ppermute(mine, "col", pair_perm("col", 1))


def apply(kernel, probes, noise_var, prior_diag):
    rows_own = kernel.shape[2]
    width = kernel.shape[3]
    count = probes.shape[0]
    blocks = lax.axis_size("row")
    coef = prior_diag[None, :]
    low, high = call(edges_body, (kernel, coef), [((8, 4 * rows_own), BF)] * 2)
    low = lax.ppermute(low, "row", [(i, i + 1) for i in range(blocks - 1)])
    high = lax.ppermute(high, "row", [(i + 1, i) for i in range(blocks - 1)])
    x, mine, other = all_sum(probes, kernel, coef)
    operator = call(operator_body, (kernel, coef, low, high), [((2, 2, width, rows_own), BF)])[0]
    size = count // blocks
    groups = []
    for swap, field in ((False, mine), (True, other)):
        keep, *sends = call(
            functools.partial(predict_body, swap),
            (field, operator),
            [((2 * size, rows_own), F32)] + [((2 * size, rows_own), BF)] * (blocks - 1),
        )
        groups.append(keep)
        groups += [lax.ppermute(v, "row", pair_perm("row", d + 1)) for d, v in enumerate(sends)]
    out = call(
        functools.partial(final_body, blocks - 1),
        (x, noise_var, *groups),
        [((size,) + probes.shape[1:3] + (rows_own,), F32)],
        (pltpu.VMEM((rows_own // LANES, 4 * size, LANES), F32),),
    )[0]
    return out


def solution(mesh):
    in_specs = (P(None, None, "col", "row"), P(None, None, None, "col"), P(None, "col"), P("row"))
    out_specs = P("row", None, None, "col")
    return jax.shard_map(apply, mesh=mesh, in_specs=in_specs, out_specs=out_specs, check_vma=False)
```

```python
import functools

import jax
import jax.numpy as jnp
from jax import lax
from jax.experimental import pallas as pl
from jax.experimental.pallas import tpu as pltpu
from jax.sharding import PartitionSpec as P


BF = jnp.bfloat16
F32 = jnp.float32
LANES = 128
VMEM = pl.BlockSpec(memory_space=pltpu.VMEM)
HBM = pl.BlockSpec(memory_space=pl.ANY)


def call(body, ins, outs, scratch=(), raw=()):
    return pl.pallas_call(
        body,
        in_specs=[HBM] * len(raw) + [VMEM] * len(ins),
        out_specs=[VMEM] * len(outs),
        out_shape=[pltpu.VMEM(*o) for o in outs],
        scratch_shapes=list(scratch),
    )(*raw, *[pltpu.with_memory_space_constraint(v, pltpu.VMEM) for v in ins])


def move(value, axis, perm):
    return lax.ppermute(value, axis, perm)


def pair_perm(axis, step):
    return [(i, i ^ step) for i in range(lax.axis_size(axis))]


def parity():
    return lax.rem(lax.axis_index("col"), 2)


def xor(a, b):
    return jnp.bitwise_xor(a, b)


def part(start, size):
    return pl.ds(pl.multiple_of(start, size), size)


def dot_nt(left, right):
    return lax.dot_general(left, right, (((1,), (1,)), ((), ())), preferred_element_type=F32)


def dot_nn(left, right):
    return jnp.dot(left, right, preferred_element_type=F32)


def three(value):
    pieces = []
    for _ in range(3):
        pieces.append(value.astype(BF))
        value = value - pieces[-1].astype(F32)
    return pieces


def adjoint(freq, x, k_ref, o_ref, u_ref):
    rows = x.shape[0] // 4
    width = k_ref.shape[3]
    tiles = width // LANES
    for c in range(2):
        y = dot_nn(x, k_ref[freq, c])
        for t in range(tiles):
            u_ref[c * tiles + t] = y[:, t * LANES:(t + 1) * LANES]
    real = pl.ds(2 * freq, rows, stride=4)
    imag = pl.ds(2 * freq + 1, rows, stride=4)
    for t in range(tiles):
        at = slice(t * LANES, (t + 1) * LANES)
        o_ref[:rows, at] = (u_ref[t, real, :] + u_ref[tiles + t, imag, :]).astype(o_ref.dtype)
        o_ref[rows:, at] = (u_ref[t, imag, :] - u_ref[tiles + t, real, :]).astype(o_ref.dtype)


def adjoint_other_body(v_hbm, k_hbm, o_ref, x_ref, k_ref, v_ref, u_ref, sems):
    freq = 1 - parity()
    copies = [
        pltpu.make_async_copy(v_hbm, v_ref, sems.at[0]),
        pltpu.make_async_copy(k_hbm.at[freq], k_ref.at[freq], sems.at[1]),
        pltpu.make_async_copy(k_hbm.at[1 - freq], k_ref.at[1 - freq], sems.at[2]),
    ]
    for copy in copies:
        copy.start()
    copies[0].wait()
    x = v_ref[...].reshape(x_ref.shape)
    x_ref[...] = x
    copies[1].wait()
    adjoint(freq, x, k_ref, o_ref, u_ref)
    copies[2].wait()


def adjoint_own_body(x_ref, k_ref, o_ref, u_ref):
    adjoint(parity(), x_ref[...], k_ref, o_ref, u_ref)


def seam_body(k_ref, d_ref, o_ref):
    freqs, _, rows, width = k_ref.shape
    odd = lax.rem(lax.axis_index("row"), 2)
    at = lax.broadcasted_iota(jnp.int32, (8, width), 0)
    place = lax.broadcasted_iota(jnp.int32, (8, width), 1)
    pick = jnp.where((at < 2) & (place == at + odd * (width - 2)), 1.0, 0.0).astype(BF)
    for f in range(freqs):
        for c in range(2):
            lo = (f * 2 + c) * rows
            o_ref[:, lo:lo + rows] = dot_nt(pick, k_ref[f, c]).astype(BF)
    coef = d_ref[...]
    spot = lax.broadcasted_iota(jnp.int32, coef.shape, 1)
    edge = jnp.sum(jnp.where(spot == odd * (width - 1), coef, 0.0), axis=1, keepdims=True)
    for n, piece in enumerate(three(edge)):
        o_ref[2 + n:3 + n, :] = jnp.broadcast_to(piece, (1, o_ref.shape[1]))


def fence_body(d_ref, o_ref):
    o_ref[...] = jnp.zeros_like(o_ref)


def stencil_matrix(coef, block):
    width = coef.shape[1]
    row_at = lax.broadcasted_iota(jnp.int32, (width, width), 0)
    col_at = lax.broadcasted_iota(jnp.int32, (width, width), 1)
    wide = jnp.broadcast_to(coef, (width, width))
    tall = jnp.sum(jnp.where(row_at == col_at, wide, 0.0), axis=1, keepdims=True)
    gap = jnp.abs(row_at - col_at)
    first = (row_at == 0) & (block == 0)
    last = (row_at == width - 1) & (block == lax.axis_size("row") - 1)
    centre = wide * wide + jnp.where(first | last, 1.0, 2.0)
    matrix = jnp.where(gap == 0, centre, jnp.where(gap == 1, -(wide + tall), jnp.where(gap == 2, 1.0, 0.0)))
    upper = matrix.astype(BF)
    return upper, (matrix - upper.astype(F32)).astype(BF)


def operator_body(k_ref, mate_ref, d_ref, got_ref, near_ref, far_ref, o_ref):
    freqs, _, rows, width = k_ref.shape
    me = lax.axis_index("row")
    odd = lax.rem(me, 2)
    is_odd = odd == 1
    at = lax.broadcasted_iota(jnp.int32, (8, width), 0)
    place = lax.broadcasted_iota(jnp.int32, (8, width), 1)
    own_pick = jnp.where((at < 2) & (place == at + (1 - odd) * (width - 2)), 1.0, 0.0).astype(BF)
    mate_pick = jnp.where((at < 2) & (place == at + odd * (width - 2)), 1.0, 0.0).astype(BF)
    coef = d_ref[...]
    tail = got_ref[got_ref.shape[0] - 16:, :].astype(F32)
    mate_coef = tail[0:1] + tail[1:2] + tail[2:3]

    def last_or_first(value, last):
        return jnp.where(last, value[:, width - 1:], value[:, :1])

    def outer(ref):
        full = ref[...].astype(F32)
        return full[0:2], full[2:3, :1] + full[3:4, :1] + full[4:5, :1]

    near, near_coef = outer(near_ref)
    far, far_coef = outer(far_ref)
    sides = (
        (k_ref, coef, me, near, near_coef, mate_ref, mate_pick, last_or_first(mate_coef, is_odd), is_odd),
        (mate_ref, mate_coef, xor(me, 1), far, far_coef, k_ref, own_pick, last_or_first(coef, ~is_odd), ~is_odd),
    )
    for n, (ref, c_block, block, outside, outside_coef, inner_ref, pick, inside_coef, inner_left) in enumerate(sides):
        upper, lower = stencil_matrix(c_block, block)
        left_coef = jnp.where(inner_left, inside_coef, outside_coef) + c_block[:, :1]
        right_coef = jnp.where(inner_left, outside_coef, inside_coef) + c_block[:, width - 1:]
        for f in range(freqs):
            for c in range(2):
                own = ref[f, c]
                value = dot_nt(upper, own) + dot_nt(lower, own)
                inside = dot_nt(pick, inner_ref[f, c])[0:2]
                lo = (f * 2 + c) * rows
                beyond = outside[:, lo:lo + rows]
                left = jnp.where(inner_left, inside, beyond)
                right = jnp.where(inner_left, beyond, inside)
                extra = jnp.concatenate(
                    [
                        left[0:1] - left_coef * left[1:2],
                        left[1:2],
                        jnp.zeros((width - 4, rows), F32),
                        right[0:1],
                        right[1:2] - right_coef * right[0:1],
                    ],
                    axis=0,
                )
                o_ref[f, c, n * width:(n + 1) * width] = (value + extra).astype(BF)


def split_body(own_ref, got_ref, keep_ref, *send_refs):
    chips = len(send_refs) + 1
    blocks = lax.axis_size("row")
    probes = own_ref.shape[0] // 2
    block = probes // blocks
    size = block // chips
    chip = lax.div(lax.axis_index("col"), 2)
    me = lax.axis_index("row")
    for step, ref in enumerate((keep_ref,) + send_refs):
        target = xor(chip, step)
        at = 0
        for mate in range(2):
            for slot in range(blocks // 2):
                for c in range(2):
                    lo = c * probes + xor(me, mate + 2 * slot) * block + target * size
                    rows = part(lo, size)
                    ref[at:at + size] = (own_ref[rows, :] + got_ref[rows, :].astype(F32)).astype(ref.dtype)
                    at += size


def sum_body(keep_ref, d_ref, fence_ref, *refs):
    stay_ref, give_ref = refs[-2:]
    size = stay_ref.shape[0]
    total = keep_ref[...]
    for ref in refs[:-2]:
        total = total + ref[...].astype(F32)
    stay_ref[...] = total[:size].astype(BF)
    give_ref[:size] = total[size:].astype(BF)
    pad = jnp.zeros((13, d_ref.shape[1]), BF)
    give_ref[size:] = jnp.concatenate(three(d_ref[...]) + [pad], axis=0)


def pack_body(stay_ref, got_ref, fence_ref, o_ref):
    size = stay_ref.shape[0]
    o_ref[:size] = stay_ref[...]
    o_ref[size:] = got_ref[:size]


def join_body(mine_ref, *refs):
    out_ref = refs[-1]
    pieces = (mine_ref,) + refs[:-1]
    chips = len(pieces)
    groups = 2 * lax.axis_size("row")
    size = mine_ref.shape[0] // groups
    chip = lax.div(lax.axis_index("col"), 2)
    for step, ref in enumerate(pieces):
        source = xor(chip, step)
        for n in range(groups):
            lo = n * chips * size + source * size
            out_ref[part(lo, size), :] = ref[n * size:(n + 1) * size]


def predict_body(swap, a_ref, k_ref, keep_ref, *refs):
    freq = parity()
    if swap:
        freq = 1 - freq
    half = a_ref.shape[0] // 2
    width = a_ref.shape[1]
    size = keep_ref.shape[0] // 2
    total = []
    for c in range(2):
        value = dot_nn(a_ref[:half], k_ref[freq, c, :width])
        total.append(value + dot_nn(a_ref[half:], k_ref[freq, c, width:]))
    by_real, by_imag = total
    for slot, ref in enumerate((keep_ref,) + refs):
        lo = 2 * slot * size
        mid = lo + size
        hi = mid + size
        ref[:size] = (by_real[lo:mid] - by_imag[mid:hi]).astype(ref.dtype)
        ref[size:] = (by_real[mid:hi] + by_imag[lo:mid]).astype(ref.dtype)


def final_body(peers, x_ref, noise_ref, *refs):
    out_ref, s_ref = refs[-2:]
    size = out_ref.shape[0]
    rows = 4 * size
    me = lax.axis_index("row")
    freq = parity()
    for which in range(2):
        group = refs[which * (peers + 1):(which + 1) * (peers + 1)]
        total = group[0][...]
        for ref in group[1:]:
            total = total + ref[...].astype(F32)
        f = freq if which == 0 else 1 - freq
        for t in range(s_ref.shape[0]):
            at = slice(t * LANES, (t + 1) * LANES)
            s_ref[t, pl.ds(2 * f, size, stride=4), :] = total[:size, at]
            s_ref[t, pl.ds(2 * f + 1, size, stride=4), :] = total[size:, at]
    x = x_ref[part(me * rows, rows), :].astype(F32)
    kind = lax.rem(lax.broadcasted_iota(jnp.int32, x.shape, 0), 4)
    noise = jnp.where(kind < 2, noise_ref[0:1, :], noise_ref[1:2, :])
    values = jnp.concatenate([s_ref[t] for t in range(s_ref.shape[0])], axis=1) + noise * x
    out_ref[...] = values.reshape(out_ref.shape)


def wide_sum(own, got, coef, blocks):
    rows, width = own.shape
    a = parity()
    value = own + got.astype(F32)
    both = jnp.where(a == 0, jnp.stack([value, 0 * value]), jnp.stack([0 * value, value]))
    both = lax.psum(both, "col").astype(BF).reshape(2, 2, blocks, -1, width)
    slots = 2 * jnp.arange(blocks // 2)
    me = lax.axis_index("row")

    def chosen(freq, mate):
        value = lax.dynamic_index_in_dim(both, freq, 0, keepdims=False)
        value = jnp.take(value, xor(me, mate + slots), axis=1)
        return value.transpose(1, 0, 2, 3).reshape(-1, width)

    tail = jnp.concatenate(three(coef) + [jnp.zeros((13, width), BF)], axis=0)
    give = jnp.concatenate([chosen(1 - a, 1), chosen(a, 1), tail], axis=0)
    give = move(give, "row", pair_perm("row", 1))
    half = rows // 2
    mine = jnp.concatenate([chosen(a, 0), give[half:rows]], axis=0)
    other = jnp.concatenate([chosen(1 - a, 0), give[:half]], axis=0)
    return mine, other, give


def chip_sum(own, got, coef, chips):
    rows, width = own.shape
    size = rows // chips
    keep, *sends = call(split_body, (own, got), [((size, width), F32)] + [((size, width), BF)] * (chips - 1))
    fence = call(fence_body, (coef,), [((8, LANES), F32)])[0]
    got = [move(v, "col", pair_perm("col", 2 * (d + 1))) for d, v in enumerate(sends)]
    stay, give = call(sum_body, (keep, coef, fence, *got), [((size // 2, width), BF), ((size // 2 + 16, width), BF)])
    fence = call(fence_body, (coef,), [((8, LANES), F32)])[0]
    give = move(give, "row", pair_perm("row", 1))
    mine = call(pack_body, (stay, give, fence), [((size, width), BF)])[0]
    got = [move(mine, "col", pair_perm("col", 2 * (d + 1))) for d in range(chips - 1)]
    mine = call(join_body, (mine, *got), [((rows, width), BF)])[0]
    return mine, move(mine, "col", pair_perm("col", 1)), give


def apply(kernel, probes, noise_var, prior_diag):
    count = probes.shape[0]
    rows, width = kernel.shape[2:]
    blocks = lax.axis_size("row")
    chips = lax.axis_size("col") // 2
    coef = prior_diag[None, :]
    flat = (4 * count, rows)
    scratch = pltpu.VMEM((2 * width // LANES, 4 * count, LANES), F32)
    mate = move(kernel, "row", pair_perm("row", 1))
    other, x, kernel = call(
        adjoint_other_body,
        (),
        [((2 * count, width), BF), (flat, BF), (kernel.shape, BF)],
        (pltpu.VMEM(probes.shape, BF), scratch, pltpu.SemaphoreType.DMA((3,))),
        raw=(probes, kernel),
    )
    got = move(other, "col", pair_perm("col", 1))
    own = call(adjoint_own_body, (x, kernel), [((2 * count, width), F32)], (scratch,))[0]
    seam = call(seam_body, (kernel, coef), [((8, 4 * rows), BF)])[0]
    odd = [i for i in range(blocks) if i % 2]
    even = [i for i in range(blocks) if i % 2 == 0]
    near = [(i, i + 1) for i in odd if i + 1 < blocks] + [(i, i - 1) for i in even if i]
    far = [(i, i + 2) for i in odd if i + 2 < blocks] + [(i, i - 2) for i in even if i]
    near = move(seam, "row", near)
    far = move(seam, "row", far)
    if chips > 4:
        mine, other, give = wide_sum(own, got, coef, blocks)
    else:
        mine, other, give = chip_sum(own, got, coef, chips)
    operator = call(operator_body, (kernel, mate, coef, give, near, far), [((2, 2, 2 * width, rows), BF)])[0]
    size = count // blocks
    peers = blocks // 2 - 1
    groups = []
    for swap, field in ((False, mine), (True, other)):
        keep, *sends = call(
            functools.partial(predict_body, swap),
            (field, operator),
            [((2 * size, rows), F32)] + [((2 * size, rows), BF)] * peers,
        )
        groups.append(keep)
        groups += [move(v, "row", pair_perm("row", 2 * (d + 1))) for d, v in enumerate(sends)]
    return call(
        functools.partial(final_body, peers),
        (x, noise_var, *groups),
        [((size,) + probes.shape[1:3] + (rows,), F32)],
        (pltpu.VMEM((rows // LANES, 4 * size, LANES), F32),),
    )[0]


def solution(mesh):
    in_specs = (P(None, None, "col", "row"), P(None, None, None, "col"), P(None, "col"), P("row"))
    out_specs = P("row", None, None, "col")
    return jax.shard_map(apply, mesh=mesh, in_specs=in_specs, out_specs=out_specs, check_vma=False)
```

```python
import functools

import jax
import jax.numpy as jnp
from jax import lax
from jax.experimental import pallas as pl
from jax.experimental.pallas import tpu as pltpu
from jax.sharding import PartitionSpec as P


BF = jnp.bfloat16
F32 = jnp.float32
LANES = 128
LIMIT = 24 * 2**20
VMEM = pl.BlockSpec(memory_space=pltpu.VMEM)
HBM = pl.BlockSpec(memory_space=pltpu.HBM)


def call(body, ins, outs, scratch=(), raw=()):
    return pl.pallas_call(
        body,
        in_specs=[HBM] * len(raw) + [VMEM] * len(ins),
        out_specs=[VMEM] * len(outs),
        out_shape=[pltpu.VMEM(*o) for o in outs],
        scratch_shapes=list(scratch),
        compiler_params=pltpu.CompilerParams(vmem_limit_bytes=LIMIT),
    )(*[pltpu.with_memory_space_constraint(v, pltpu.HBM) for v in raw], *[pltpu.with_memory_space_constraint(v, pltpu.VMEM) for v in ins])


def pair_perm(axis, step):
    return [(i, i ^ step) for i in range(lax.axis_size(axis))]


def parity():
    return lax.rem(lax.axis_index("col"), 2)


def xor(a, b):
    return jnp.bitwise_xor(a, b)


def part(start, size):
    return pl.ds(pl.multiple_of(start, size), size)


def dot_nt(left, right):
    return lax.dot_general(left, right, (((1,), (1,)), ((), ())), preferred_element_type=F32)


def dot_nn(left, right):
    return jnp.dot(left, right, preferred_element_type=F32)


def three(value):
    pieces = []
    for _ in range(3):
        pieces.append(value.astype(BF))
        value = value - pieces[-1].astype(F32)
    return pieces


def adjoint(freq, x, k_ref, o_ref, u_ref):
    rows = x.shape[0] // 4
    width = k_ref.shape[3]
    tiles = width // LANES
    for c in range(2):
        y = dot_nn(x, k_ref[freq, c])
        for t in range(tiles):
            u_ref[c * tiles + t] = y[:, t * LANES:(t + 1) * LANES]
    real = pl.ds(2 * freq, rows, stride=4)
    imag = pl.ds(2 * freq + 1, rows, stride=4)
    for t in range(tiles):
        at = slice(t * LANES, (t + 1) * LANES)
        o_ref[:rows, at] = (u_ref[t, real, :] + u_ref[tiles + t, imag, :]).astype(o_ref.dtype)
        o_ref[rows:, at] = (u_ref[t, imag, :] - u_ref[tiles + t, real, :]).astype(o_ref.dtype)


def adjoint_other_body(v_hbm, k_hbm, d_hbm, n_hbm, o_ref, x_ref, k_ref, d_ref, n_ref, v_ref, u_ref, sems):
    freq = 1 - parity()
    copies = [
        pltpu.make_async_copy(v_hbm, v_ref, sems.at[0]),
        pltpu.make_async_copy(k_hbm.at[freq], k_ref.at[freq], sems.at[1]),
        pltpu.make_async_copy(k_hbm.at[1 - freq], k_ref.at[1 - freq], sems.at[2]),
        pltpu.make_async_copy(d_hbm, d_ref, sems.at[3]),
        pltpu.make_async_copy(n_hbm, n_ref, sems.at[4]),
    ]
    for copy in copies:
        copy.start()
    copies[0].wait()
    x = v_ref[...].reshape(x_ref.shape)
    x_ref[...] = x
    copies[1].wait()
    adjoint(freq, x, k_ref, o_ref, u_ref)
    for copy in copies[2:]:
        copy.wait()


def adjoint_own_body(x_ref, k_ref, o_ref, u_ref):
    adjoint(parity(), x_ref[...], k_ref, o_ref, u_ref)


def seam_body(k_ref, d_ref, o_ref):
    freqs, _, rows, width = k_ref.shape
    odd = lax.rem(lax.axis_index("row"), 2)
    at = lax.broadcasted_iota(jnp.int32, (8, width), 0)
    place = lax.broadcasted_iota(jnp.int32, (8, width), 1)
    pick = jnp.where((at < 2) & (place == at + odd * (width - 2)), 1.0, 0.0).astype(BF)
    for f in range(freqs):
        for c in range(2):
            lo = (f * 2 + c) * rows
            o_ref[:, lo:lo + rows] = dot_nt(pick, k_ref[f, c]).astype(BF)
    coef = d_ref[...]
    spot = lax.broadcasted_iota(jnp.int32, coef.shape, 1)
    edge = jnp.sum(jnp.where(spot == odd * (width - 1), coef, 0.0), axis=1, keepdims=True)
    for n, piece in enumerate(three(edge)):
        o_ref[2 + n:3 + n, :] = jnp.broadcast_to(piece, (1, o_ref.shape[1]))


def fence_body(d_ref, o_ref):
    o_ref[...] = jnp.zeros_like(o_ref)


def stencil_matrix(coef, block):
    width = coef.shape[1]
    row_at = lax.broadcasted_iota(jnp.int32, (width, width), 0)
    col_at = lax.broadcasted_iota(jnp.int32, (width, width), 1)
    wide = jnp.broadcast_to(coef, (width, width))
    tall = jnp.sum(jnp.where(row_at == col_at, wide, 0.0), axis=1, keepdims=True)
    gap = jnp.abs(row_at - col_at)
    first = (row_at == 0) & (block == 0)
    last = (row_at == width - 1) & (block == lax.axis_size("row") - 1)
    centre = wide * wide + jnp.where(first | last, 1.0, 2.0)
    matrix = jnp.where(gap == 0, centre, jnp.where(gap == 1, -(wide + tall), jnp.where(gap == 2, 1.0, 0.0)))
    upper = matrix.astype(BF)
    return upper, (matrix - upper.astype(F32)).astype(BF)


def operator_body(k_ref, mate_ref, d_ref, got_ref, near_ref, far_ref, o_ref):
    freqs, _, rows, width = k_ref.shape
    me = lax.axis_index("row")
    odd = lax.rem(me, 2)
    is_odd = odd == 1
    at = lax.broadcasted_iota(jnp.int32, (8, width), 0)
    place = lax.broadcasted_iota(jnp.int32, (8, width), 1)
    own_pick = jnp.where((at < 2) & (place == at + (1 - odd) * (width - 2)), 1.0, 0.0).astype(BF)
    mate_pick = jnp.where((at < 2) & (place == at + odd * (width - 2)), 1.0, 0.0).astype(BF)
    coef = d_ref[...]
    tail = got_ref[got_ref.shape[0] - 16:, :].astype(F32)
    mate_coef = tail[0:1] + tail[1:2] + tail[2:3]

    def last_or_first(value, last):
        return jnp.where(last, value[:, width - 1:], value[:, :1])

    def outer(ref):
        full = ref[...].astype(F32)
        return full[0:2], full[2:3, :1] + full[3:4, :1] + full[4:5, :1]

    near, near_coef = outer(near_ref)
    far, far_coef = outer(far_ref)
    sides = (
        (k_ref, coef, me, near, near_coef, mate_ref, mate_pick, last_or_first(mate_coef, is_odd), is_odd),
        (mate_ref, mate_coef, xor(me, 1), far, far_coef, k_ref, own_pick, last_or_first(coef, ~is_odd), ~is_odd),
    )
    for n, (ref, c_block, block, outside, outside_coef, inner_ref, pick, inside_coef, inner_left) in enumerate(sides):
        upper, lower = stencil_matrix(c_block, block)
        left_coef = jnp.where(inner_left, inside_coef, outside_coef) + c_block[:, :1]
        right_coef = jnp.where(inner_left, outside_coef, inside_coef) + c_block[:, width - 1:]
        for f in range(freqs):
            for c in range(2):
                own = ref[f, c]
                value = dot_nt(upper, own) + dot_nt(lower, own)
                inside = dot_nt(pick, inner_ref[f, c])[0:2]
                lo = (f * 2 + c) * rows
                beyond = outside[:, lo:lo + rows]
                left = jnp.where(inner_left, inside, beyond)
                right = jnp.where(inner_left, beyond, inside)
                extra = jnp.concatenate(
                    [
                        left[0:1] - left_coef * left[1:2],
                        left[1:2],
                        jnp.zeros((width - 4, rows), F32),
                        right[0:1],
                        right[1:2] - right_coef * right[0:1],
                    ],
                    axis=0,
                )
                o_ref[f, c, n * width:(n + 1) * width] = (value + extra).astype(BF)


def split_body(own_ref, got_ref, keep_ref, *send_refs):
    chips = len(send_refs) + 1
    blocks = lax.axis_size("row")
    probes = own_ref.shape[0] // 2
    block = probes // blocks
    size = block // chips
    chip = lax.div(lax.axis_index("col"), 2)
    me = lax.axis_index("row")
    for step, ref in enumerate((keep_ref,) + send_refs):
        target = xor(chip, step)
        at = 0
        for mate in range(2):
            for slot in range(blocks // 2):
                for c in range(2):
                    lo = c * probes + xor(me, mate + 2 * slot) * block + target * size
                    rows = part(lo, size)
                    ref[at:at + size] = (own_ref[rows, :] + got_ref[rows, :].astype(F32)).astype(ref.dtype)
                    at += size


def sum_body(keep_ref, d_ref, fence_ref, *refs):
    stay_ref, give_ref = refs[-2:]
    size = stay_ref.shape[0]
    total = keep_ref[...]
    for ref in refs[:-2]:
        total = total + ref[...].astype(F32)
    stay_ref[...] = total[:size].astype(BF)
    give_ref[:size] = total[size:].astype(BF)
    pad = jnp.zeros((13, d_ref.shape[1]), BF)
    give_ref[size:] = jnp.concatenate(three(d_ref[...]) + [pad], axis=0)


def pack_body(stay_ref, got_ref, fence_ref, o_ref):
    size = stay_ref.shape[0]
    o_ref[:size] = stay_ref[...]
    o_ref[size:] = got_ref[:size]


def join_body(mine_ref, *refs):
    out_ref = refs[-1]
    pieces = (mine_ref,) + refs[:-1]
    chips = len(pieces)
    groups = 2 * lax.axis_size("row")
    size = mine_ref.shape[0] // groups
    chip = lax.div(lax.axis_index("col"), 2)
    for step, ref in enumerate(pieces):
        source = xor(chip, step)
        for n in range(groups):
            lo = n * chips * size + source * size
            out_ref[part(lo, size), :] = ref[n * size:(n + 1) * size]


def predict_body(swap, a_ref, k_ref, keep_ref, *refs):
    freq = parity()
    if swap:
        freq = 1 - freq
    half = a_ref.shape[0] // 2
    width = a_ref.shape[1]
    size = keep_ref.shape[0] // 2
    total = []
    for c in range(2):
        value = dot_nn(a_ref[:half], k_ref[freq, c, :width])
        total.append(value + dot_nn(a_ref[half:], k_ref[freq, c, width:]))
    by_real, by_imag = total
    for slot, ref in enumerate((keep_ref,) + refs):
        lo = 2 * slot * size
        mid = lo + size
        hi = mid + size
        ref[:size] = (by_real[lo:mid] - by_imag[mid:hi]).astype(ref.dtype)
        ref[size:] = (by_real[mid:hi] + by_imag[lo:mid]).astype(ref.dtype)


def final_body(peers, x_ref, noise_ref, *refs):
    out_ref, s_ref = refs[-2:]
    size = out_ref.shape[0]
    rows = 4 * size
    me = lax.axis_index("row")
    freq = parity()
    for which in range(2):
        group = refs[which * (peers + 1):(which + 1) * (peers + 1)]
        total = group[0][...]
        for ref in group[1:]:
            total = total + ref[...].astype(F32)
        f = freq if which == 0 else 1 - freq
        for t in range(s_ref.shape[0]):
            at = slice(t * LANES, (t + 1) * LANES)
            s_ref[t, pl.ds(2 * f, size, stride=4), :] = total[:size, at]
            s_ref[t, pl.ds(2 * f + 1, size, stride=4), :] = total[size:, at]
    x = x_ref[part(me * rows, rows), :].astype(F32)
    kind = lax.rem(lax.broadcasted_iota(jnp.int32, x.shape, 0), 4)
    noise = jnp.where(kind < 2, noise_ref[0:1, :], noise_ref[1:2, :])
    values = jnp.concatenate([s_ref[t] for t in range(s_ref.shape[0])], axis=1) + noise * x
    out_ref[...] = values.reshape(out_ref.shape)


def wide_sum(own, got, coef, blocks):
    rows, width = own.shape
    a = parity()
    value = own + got.astype(F32)
    both = jnp.where(a == 0, jnp.stack([value, 0 * value]), jnp.stack([0 * value, value]))
    both = lax.psum(both, "col").astype(BF).reshape(2, 2, blocks, -1, width)
    slots = 2 * jnp.arange(blocks // 2)
    me = lax.axis_index("row")

    def chosen(freq, mate):
        value = lax.dynamic_index_in_dim(both, freq, 0, keepdims=False)
        value = jnp.take(value, xor(me, mate + slots), axis=1)
        return value.transpose(1, 0, 2, 3).reshape(-1, width)

    tail = jnp.concatenate(three(coef) + [jnp.zeros((13, width), BF)], axis=0)
    give = jnp.concatenate([chosen(1 - a, 1), chosen(a, 1), tail], axis=0)
    give = lax.ppermute(give, "row", pair_perm("row", 1))
    half = rows // 2
    mine = jnp.concatenate([chosen(a, 0), give[half:rows]], axis=0)
    other = jnp.concatenate([chosen(1 - a, 0), give[:half]], axis=0)
    return mine, other, give


def chip_sum(own, got, coef, chips):
    rows, width = own.shape
    size = rows // chips
    keep, *sends = call(split_body, (own, got), [((size, width), F32)] + [((size, width), BF)] * (chips - 1))
    fence = call(fence_body, (coef,), [((8, LANES), F32)])[0]
    got = [lax.ppermute(v, "col", pair_perm("col", 2 * (d + 1))) for d, v in enumerate(sends)]
    stay, give = call(sum_body, (keep, coef, fence, *got), [((size // 2, width), BF), ((size // 2 + 16, width), BF)])
    fence = call(fence_body, (coef,), [((8, LANES), F32)])[0]
    give = lax.ppermute(give, "row", pair_perm("row", 1))
    mine = call(pack_body, (stay, give, fence), [((size, width), BF)])[0]
    got = [lax.ppermute(mine, "col", pair_perm("col", 2 * (d + 1))) for d in range(chips - 1)]
    mine = call(join_body, (mine, *got), [((rows, width), BF)])[0]
    return mine, lax.ppermute(mine, "col", pair_perm("col", 1)), give


def apply(kernel, probes, noise_var, prior_diag):
    count = probes.shape[0]
    rows, width = kernel.shape[2:]
    blocks = lax.axis_size("row")
    chips = lax.axis_size("col") // 2
    coef = prior_diag[None, :]
    flat = (4 * count, rows)
    scratch = pltpu.VMEM((2 * width // LANES, 4 * count, LANES), F32)
    mate = lax.ppermute(kernel, "row", pair_perm("row", 1))
    other, x, kernel, coef, noise = call(
        adjoint_other_body,
        (),
        [((2 * count, width), BF), (flat, BF), (kernel.shape, BF), (coef.shape, F32), (noise_var.shape, F32)],
        (pltpu.VMEM(probes.shape, BF), scratch, pltpu.SemaphoreType.DMA((5,))),
        raw=(probes, kernel, coef, noise_var),
    )
    got = lax.ppermute(other, "col", pair_perm("col", 1))
    own = call(adjoint_own_body, (x, kernel), [((2 * count, width), F32)], (scratch,))[0]
    seam = call(seam_body, (kernel, coef), [((8, 4 * rows), BF)])[0]
    odd = [i for i in range(blocks) if i % 2]
    even = [i for i in range(blocks) if i % 2 == 0]
    near = [(i, i + 1) for i in odd if i + 1 < blocks] + [(i, i - 1) for i in even if i]
    far = [(i, i + 2) for i in odd if i + 2 < blocks] + [(i, i - 2) for i in even if i]
    near = lax.ppermute(seam, "row", near)
    far = lax.ppermute(seam, "row", far)
    if chips > 4:
        mine, other, give = wide_sum(own, got, coef, blocks)
    else:
        mine, other, give = chip_sum(own, got, coef, chips)
    operator = call(operator_body, (kernel, mate, coef, give, near, far), [((2, 2, 2 * width, rows), BF)])[0]
    size = count // blocks
    peers = blocks // 2 - 1
    groups = []
    for swap, field in ((False, mine), (True, other)):
        keep, *sends = call(
            functools.partial(predict_body, swap),
            (field, operator),
            [((2 * size, rows), F32)] + [((2 * size, rows), BF)] * peers,
        )
        groups.append(keep)
        groups += [lax.ppermute(v, "row", pair_perm("row", 2 * (d + 1))) for d, v in enumerate(sends)]
    return call(
        functools.partial(final_body, peers),
        (x, noise, *groups),
        [((size,) + probes.shape[1:3] + (rows,), F32)],
        (pltpu.VMEM((rows // LANES, 4 * size, LANES), F32),),
    )[0]


def solution(mesh):
    in_specs = (P(None, None, "col", "row"), P(None, None, None, "col"), P(None, "col"), P("row"))
    out_specs = P("row", None, None, "col")
    return jax.shard_map(apply, mesh=mesh, in_specs=in_specs, out_specs=out_specs, check_vma=False)
```

```python
import functools

import jax
import jax.numpy as jnp
from jax import lax
from jax.experimental import pallas as pl
from jax.experimental.pallas import tpu as pltpu
from jax.sharding import PartitionSpec as P


BF = jnp.bfloat16
F32 = jnp.float32
LANES = 128
LIMIT = 24 * 2**20
TAIL = 48
VMEM = pl.BlockSpec(memory_space=pltpu.VMEM)
HBM = pl.BlockSpec(memory_space=pltpu.HBM)


def call(body, ins, outs, scratch=(), raw=()):
    return pl.pallas_call(
        body,
        in_specs=[HBM] * len(raw) + [VMEM] * len(ins),
        out_specs=[VMEM] * len(outs),
        out_shape=[pltpu.VMEM(*o) for o in outs],
        scratch_shapes=list(scratch),
        compiler_params=pltpu.CompilerParams(vmem_limit_bytes=LIMIT),
    )(*[pltpu.with_memory_space_constraint(v, pltpu.HBM) for v in raw], *[pltpu.with_memory_space_constraint(v, pltpu.VMEM) for v in ins])


def pair_perm(axis, step):
    return [(i, i ^ step) for i in range(lax.axis_size(axis))]


def parity():
    return lax.rem(lax.axis_index("col"), 2)


def xor(a, b):
    return jnp.bitwise_xor(a, b)


def part(start, size):
    return pl.ds(pl.multiple_of(start, size), size)


def dot_nt(left, right):
    return lax.dot_general(left, right, (((1,), (1,)), ((), ())), preferred_element_type=F32)


def dot_nn(left, right):
    return jnp.dot(left, right, preferred_element_type=F32)


def three(value):
    pieces = []
    for _ in range(3):
        pieces.append(value.astype(BF))
        value = value - pieces[-1].astype(F32)
    return pieces


def adjoint(freq, x, k_ref, o_ref, u_ref):
    rows = x.shape[0] // 4
    width = k_ref.shape[3]
    tiles = width // LANES
    for c in range(2):
        y = dot_nn(x, k_ref[freq, c])
        for t in range(tiles):
            u_ref[c * tiles + t] = y[:, t * LANES:(t + 1) * LANES]
    real = pl.ds(2 * freq, rows, stride=4)
    imag = pl.ds(2 * freq + 1, rows, stride=4)
    for t in range(tiles):
        at = slice(t * LANES, (t + 1) * LANES)
        o_ref[:rows, at] = (u_ref[t, real, :] + u_ref[tiles + t, imag, :]).astype(o_ref.dtype)
        o_ref[rows:, at] = (u_ref[t, imag, :] - u_ref[tiles + t, real, :]).astype(o_ref.dtype)


def adjoint_other_body(v_hbm, k_hbm, d_hbm, n_hbm, o_ref, x_ref, k_ref, d_ref, n_ref, v_ref, u_ref, sems):
    freq = 1 - parity()
    copies = [
        pltpu.make_async_copy(v_hbm, v_ref, sems.at[0]),
        pltpu.make_async_copy(k_hbm.at[freq], k_ref.at[freq], sems.at[1]),
        pltpu.make_async_copy(k_hbm.at[1 - freq], k_ref.at[1 - freq], sems.at[2]),
        pltpu.make_async_copy(d_hbm, d_ref, sems.at[3]),
        pltpu.make_async_copy(n_hbm, n_ref, sems.at[4]),
    ]
    for copy in copies:
        copy.start()
    copies[0].wait()
    x = v_ref[...].reshape(x_ref.shape)
    x_ref[...] = x
    copies[1].wait()
    adjoint(freq, x, k_ref, o_ref, u_ref)
    for copy in copies[2:]:
        copy.wait()


def adjoint_own_body(x_ref, k_ref, o_ref, u_ref):
    adjoint(parity(), x_ref[...], k_ref, o_ref, u_ref)


def seam_body(k_ref, d_ref, o_ref):
    freqs, _, rows, width = k_ref.shape
    odd = lax.rem(lax.axis_index("row"), 2)
    at = lax.broadcasted_iota(jnp.int32, (8, width), 0)
    place = lax.broadcasted_iota(jnp.int32, (8, width), 1)
    pick = jnp.where((at < 2) & (place == at + odd * (width - 2)), 1.0, 0.0).astype(BF)
    for f in range(freqs):
        for c in range(2):
            lo = (f * 2 + c) * rows
            o_ref[:, lo:lo + rows] = dot_nt(pick, k_ref[f, c]).astype(BF)
    coef = d_ref[...]
    spot = lax.broadcasted_iota(jnp.int32, coef.shape, 1)
    edge = jnp.sum(jnp.where(spot == odd * (width - 1), coef, 0.0), axis=1, keepdims=True)
    for n, piece in enumerate(three(edge)):
        o_ref[2 + n:3 + n, :] = jnp.broadcast_to(piece, (1, o_ref.shape[1]))


def fence_body(d_ref, o_ref):
    o_ref[...] = jnp.zeros_like(o_ref)


def stencil_matrix(coef, block):
    width = coef.shape[1]
    row_at = lax.broadcasted_iota(jnp.int32, (width, width), 0)
    col_at = lax.broadcasted_iota(jnp.int32, (width, width), 1)
    wide = jnp.broadcast_to(coef, (width, width))
    tall = jnp.sum(jnp.where(row_at == col_at, wide, 0.0), axis=1, keepdims=True)
    gap = jnp.abs(row_at - col_at)
    first = (row_at == 0) & (block == 0)
    last = (row_at == width - 1) & (block == lax.axis_size("row") - 1)
    centre = wide * wide + jnp.where(first | last, 1.0, 2.0)
    matrix = jnp.where(gap == 0, centre, jnp.where(gap == 1, -(wide + tall), jnp.where(gap == 2, 1.0, 0.0)))
    upper = matrix.astype(BF)
    return upper, (matrix - upper.astype(F32)).astype(BF)


def operator_body(k_ref, mate_ref, d_ref, got_ref, near_ref, o_ref):
    freqs, _, rows, width = k_ref.shape
    me = lax.axis_index("row")
    odd = lax.rem(me, 2)
    is_odd = odd == 1
    at = lax.broadcasted_iota(jnp.int32, (8, width), 0)
    place = lax.broadcasted_iota(jnp.int32, (8, width), 1)
    own_pick = jnp.where((at < 2) & (place == at + (1 - odd) * (width - 2)), 1.0, 0.0).astype(BF)
    mate_pick = jnp.where((at < 2) & (place == at + odd * (width - 2)), 1.0, 0.0).astype(BF)
    coef = d_ref[...]
    base = got_ref.shape[0] - TAIL
    tail = got_ref[base:, :].astype(F32)
    mate_coef = tail[0:1] + tail[1:2] + tail[2:3]

    def last_or_first(value, last):
        return jnp.where(last, value[:, width - 1:], value[:, :1])

    def outer(full):
        return full, full[2:3, :1] + full[3:4, :1] + full[4:5, :1]

    def beyond_of(full, block):
        last = lax.axis_size("row") - 1
        there = jnp.where(lax.rem(block, 2) == 1, block < last, block > 0)
        return jnp.where(there, full, 0.0)

    near, near_coef = outer(near_ref[...].astype(F32))
    far = jnp.concatenate([tail[16 + 8 * n:24 + 8 * n] for n in range(2 * freqs)], axis=1)
    far, far_coef = outer(far)
    sides = (
        (k_ref, coef, me, near, near_coef, mate_ref, mate_pick, last_or_first(mate_coef, is_odd), is_odd),
        (mate_ref, mate_coef, xor(me, 1), far, far_coef, k_ref, own_pick, last_or_first(coef, ~is_odd), ~is_odd),
    )
    for n, (ref, c_block, block, outside, outside_coef, inner_ref, pick, inside_coef, inner_left) in enumerate(sides):
        upper, lower = stencil_matrix(c_block, block)
        left_coef = jnp.where(inner_left, inside_coef, outside_coef) + c_block[:, :1]
        right_coef = jnp.where(inner_left, outside_coef, inside_coef) + c_block[:, width - 1:]
        for f in range(freqs):
            for c in range(2):
                own = ref[f, c]
                value = dot_nt(upper, own) + dot_nt(lower, own)
                inside = dot_nt(pick, inner_ref[f, c])[0:2]
                lo = (f * 2 + c) * rows
                beyond = beyond_of(outside[0:2, lo:lo + rows], block)
                left = jnp.where(inner_left, inside, beyond)
                right = jnp.where(inner_left, beyond, inside)
                extra = jnp.concatenate(
                    [
                        left[0:1] - left_coef * left[1:2],
                        left[1:2],
                        jnp.zeros((width - 4, rows), F32),
                        right[0:1],
                        right[1:2] - right_coef * right[0:1],
                    ],
                    axis=0,
                )
                o_ref[f, c, n * width:(n + 1) * width] = (value + extra).astype(BF)


def split_body(own_ref, got_ref, fence_ref, keep_ref, *send_refs):
    chips = len(send_refs) + 1
    blocks = lax.axis_size("row")
    probes = own_ref.shape[0] // 2
    block = probes // blocks
    size = block // chips
    chip = lax.div(lax.axis_index("col"), 2)
    me = lax.axis_index("row")
    for step, ref in enumerate((keep_ref,) + send_refs):
        target = xor(chip, step)
        at = 0
        for mate in range(2):
            for slot in range(blocks // 2):
                for c in range(2):
                    lo = c * probes + xor(me, mate + 2 * slot) * block + target * size
                    rows = part(lo, size)
                    ref[at:at + size] = (own_ref[rows, :] + got_ref[rows, :].astype(F32)).astype(ref.dtype)
                    at += size


def sum_body(keep_ref, d_ref, near_ref, *refs):
    stay_ref, give_ref, long_ref = refs[-3:]
    size, width = stay_ref.shape
    total = keep_ref[...]
    for ref in refs[:-3]:
        total = total + ref[...].astype(F32)
    stay_ref[...] = total[:size].astype(BF)
    give = total[size:].astype(BF)
    give_ref[...] = give
    long_ref[:size] = give
    pad = jnp.zeros((13, width), BF)
    long_ref[size:size + 16] = jnp.concatenate(three(d_ref[...]) + [pad], axis=0)
    for n in range(4):
        lo = size + 16 + 8 * n
        long_ref[lo:lo + 8] = near_ref[:, n * width:(n + 1) * width]


def join_body(*refs):
    out_ref = refs[-1]
    chips = len(refs) // 2
    groups = lax.axis_size("row")
    size = refs[0].shape[0] // groups
    chip = lax.div(lax.axis_index("col"), 2)
    for n, ref in enumerate(refs[:-1]):
        source = xor(chip, n % chips)
        for g in range(groups):
            lo = (n // chips * groups + g) * chips * size + source * size
            out_ref[part(lo, size), :] = ref[g * size:(g + 1) * size]


def predict_body(swap, a_ref, k_ref, keep_ref, *refs):
    freq = parity()
    if swap:
        freq = 1 - freq
    half = a_ref.shape[0] // 2
    width = a_ref.shape[1]
    size = keep_ref.shape[0] // 2
    total = []
    for c in range(2):
        value = dot_nn(a_ref[:half], k_ref[freq, c, :width])
        total.append(value + dot_nn(a_ref[half:], k_ref[freq, c, width:]))
    by_real, by_imag = total
    for slot, ref in enumerate((keep_ref,) + refs):
        lo = 2 * slot * size
        mid = lo + size
        hi = mid + size
        ref[:size] = (by_real[lo:mid] - by_imag[mid:hi]).astype(ref.dtype)
        ref[size:] = (by_real[mid:hi] + by_imag[lo:mid]).astype(ref.dtype)


def final_body(peers, x_ref, noise_ref, *refs):
    out_ref, s_ref = refs[-2:]
    size = out_ref.shape[0]
    rows = 4 * size
    me = lax.axis_index("row")
    freq = parity()
    for which in range(2):
        group = refs[which * (peers + 1):(which + 1) * (peers + 1)]
        total = group[0][...]
        for ref in group[1:]:
            total = total + ref[...].astype(F32)
        f = freq if which == 0 else 1 - freq
        for t in range(s_ref.shape[0]):
            at = slice(t * LANES, (t + 1) * LANES)
            s_ref[t, pl.ds(2 * f, size, stride=4), :] = total[:size, at]
            s_ref[t, pl.ds(2 * f + 1, size, stride=4), :] = total[size:, at]
    x = x_ref[part(me * rows, rows), :].astype(F32)
    kind = lax.rem(lax.broadcasted_iota(jnp.int32, x.shape, 0), 4)
    noise = jnp.where(kind < 2, noise_ref[0:1, :], noise_ref[1:2, :])
    values = jnp.concatenate([s_ref[t] for t in range(s_ref.shape[0])], axis=1) + noise * x
    out_ref[...] = values.reshape(out_ref.shape)


def wide_sum(own, got, coef, near, blocks):
    rows, width = own.shape
    a = parity()
    value = own + got.astype(F32)
    both = jnp.where(a == 0, jnp.stack([value, 0 * value]), jnp.stack([0 * value, value]))
    both = lax.psum(both, "col").astype(BF).reshape(2, 2, blocks, -1, width)
    slots = 2 * jnp.arange(blocks // 2)
    me = lax.axis_index("row")

    def chosen(freq, mate):
        value = lax.dynamic_index_in_dim(both, freq, 0, keepdims=False)
        value = jnp.take(value, xor(me, mate + slots), axis=1)
        return value.transpose(1, 0, 2, 3).reshape(-1, width)

    tail = three(coef) + [jnp.zeros((13, width), BF)]
    tail += [near[:, n * width:(n + 1) * width] for n in range(4)]
    give = jnp.concatenate([chosen(1 - a, 1), chosen(a, 1)] + tail, axis=0)
    give = lax.ppermute(give, "row", pair_perm("row", 1))
    half = rows // 2
    mine = jnp.concatenate([chosen(a, 0), give[half:rows]], axis=0)
    other = jnp.concatenate([chosen(1 - a, 0), give[:half]], axis=0)
    return mine, other, give


def cross_perm(step):
    cols = lax.axis_size("col")
    return [(i * cols + j, (i ^ 1) * cols + (j ^ step)) for i in range(lax.axis_size("row")) for j in range(cols)]


def chip_sum(own, got, coef, near, chips):
    rows, width = own.shape
    size = rows // chips
    half = size // 2
    fence = call(fence_body, (coef,), [((8, LANES), F32)])[0]
    keep, *sends = call(split_body, (own, got, fence), [((size, width), F32)] + [((size, width), BF)] * (chips - 1))
    got = [lax.ppermute(v, "col", pair_perm("col", 2 * (d + 1))) for d, v in enumerate(sends)]
    stay, give, long = call(
        sum_body, (keep, coef, near, *got), [((half, width), BF), ((half, width), BF), ((half + TAIL, width), BF)]
    )
    long = lax.ppermute(long, "row", pair_perm("row", 1))
    pieces = [stay]
    pieces += [lax.ppermute(stay, "col", pair_perm("col", 2 * (d + 1))) for d in range(chips - 1)]
    pieces.append(long)
    pieces += [lax.ppermute(give, ("row", "col"), cross_perm(2 * (d + 1))) for d in range(chips - 1)]
    mine = call(join_body, pieces, [((rows, width), BF)])[0]
    return mine, lax.ppermute(mine, "col", pair_perm("col", 1)), long


def apply(kernel, probes, noise_var, prior_diag):
    count = probes.shape[0]
    rows, width = kernel.shape[2:]
    blocks = lax.axis_size("row")
    chips = lax.axis_size("col") // 2
    coef = prior_diag[None, :]
    flat = (4 * count, rows)
    scratch = pltpu.VMEM((2 * width // LANES, 4 * count, LANES), F32)
    mate = lax.ppermute(kernel, "row", pair_perm("row", 1))
    other, x, kernel, coef, noise = call(
        adjoint_other_body,
        (),
        [((2 * count, width), BF), (flat, BF), (kernel.shape, BF), (coef.shape, F32), (noise_var.shape, F32)],
        (pltpu.VMEM(probes.shape, BF), scratch, pltpu.SemaphoreType.DMA((5,))),
        raw=(probes, kernel, coef, noise_var),
    )
    got = lax.ppermute(other, "col", pair_perm("col", 1))
    own = call(adjoint_own_body, (x, kernel), [((2 * count, width), F32)], (scratch,))[0]
    seam = call(seam_body, (kernel, coef), [((8, 4 * rows), BF)])[0]
    odd = [i for i in range(blocks) if i % 2]
    even = [i for i in range(blocks) if i % 2 == 0]
    near = [(i, min(i + 1, blocks - 1)) for i in odd] + [(i, max(i - 1, 0)) for i in even]
    near = lax.ppermute(seam, "row", near)
    if chips > 4:
        mine, other, give = wide_sum(own, got, coef, near, blocks)
    else:
        mine, other, give = chip_sum(own, got, coef, near, chips)
    operator = call(operator_body, (kernel, mate, coef, give, near), [((2, 2, 2 * width, rows), BF)])[0]
    size = count // blocks
    peers = blocks // 2 - 1
    groups = []
    for swap, field in ((False, mine), (True, other)):
        keep, *sends = call(
            functools.partial(predict_body, swap),
            (field, operator),
            [((2 * size, rows), F32)] + [((2 * size, rows), BF)] * peers,
        )
        groups.append(keep)
        groups += [lax.ppermute(v, "row", pair_perm("row", 2 * (d + 1))) for d, v in enumerate(sends)]
    return call(
        functools.partial(final_body, peers),
        (x, noise, *groups),
        [((size,) + probes.shape[1:3] + (rows,), F32)],
        (pltpu.VMEM((rows // LANES, 4 * size, LANES), F32),),
    )[0]


def solution(mesh):
    in_specs = (P(None, None, "col", "row"), P(None, None, None, "col"), P(None, "col"), P("row"))
    out_specs = P("row", None, None, "col")
    return jax.shard_map(apply, mesh=mesh, in_specs=in_specs, out_specs=out_specs, check_vma=False)
```

```python
import functools

import jax
import jax.numpy as jnp
from jax import lax
from jax.experimental import pallas as pl
from jax.experimental.pallas import tpu as pltpu
from jax.sharding import PartitionSpec as P


BF = jnp.bfloat16
F32 = jnp.float32
LANES = 128
LIMIT = 24 * 2**20
TAIL = 48
CHUNKS = 4
VMEM = pl.BlockSpec(memory_space=pltpu.VMEM)
HBM = pl.BlockSpec(memory_space=pltpu.HBM)


def call(body, ins, outs, scratch=(), raw=()):
    return pl.pallas_call(
        body,
        in_specs=[HBM] * len(raw) + [VMEM] * len(ins),
        out_specs=[VMEM] * len(outs),
        out_shape=[pltpu.VMEM(*o) for o in outs],
        scratch_shapes=list(scratch),
        compiler_params=pltpu.CompilerParams(vmem_limit_bytes=LIMIT),
    )(*[pltpu.with_memory_space_constraint(v, pltpu.HBM) for v in raw], *[pltpu.with_memory_space_constraint(v, pltpu.VMEM) for v in ins])


def pair_perm(axis, step):
    return [(i, i ^ step) for i in range(lax.axis_size(axis))]


def parity():
    return lax.rem(lax.axis_index("col"), 2)


def xor(a, b):
    return jnp.bitwise_xor(a, b)


def part(start, size):
    return pl.ds(pl.multiple_of(start, size), size)


def dot_nt(left, right):
    return lax.dot_general(left, right, (((1,), (1,)), ((), ())), preferred_element_type=F32)


def dot_nn(left, right):
    return jnp.dot(left, right, preferred_element_type=F32)


def three(value):
    pieces = []
    for _ in range(3):
        pieces.append(value.astype(BF))
        value = value - pieces[-1].astype(F32)
    return pieces


def products(freq, x, k_ref, u_ref, start):
    tiles = u_ref.shape[0] // 2
    for c in range(2):
        y = dot_nn(x, k_ref[freq, c])
        for t in range(tiles):
            u_ref[c * tiles + t, start:start + x.shape[0]] = y[:, t * LANES:(t + 1) * LANES]


def combine(freq, o_ref, u_ref):
    rows = o_ref.shape[0] // 2
    tiles = u_ref.shape[0] // 2
    real = pl.ds(2 * freq, rows, stride=4)
    imag = pl.ds(2 * freq + 1, rows, stride=4)
    for t in range(tiles):
        at = slice(t * LANES, (t + 1) * LANES)
        o_ref[:rows, at] = (u_ref[t, real, :] + u_ref[tiles + t, imag, :]).astype(o_ref.dtype)
        o_ref[rows:, at] = (u_ref[t, imag, :] - u_ref[tiles + t, real, :]).astype(o_ref.dtype)


def adjoint_other_body(v_hbm, k_hbm, d_hbm, n_hbm, o_ref, x_ref, k_ref, d_ref, n_ref, v_ref, u_ref, sems):
    freq = 1 - parity()
    size = v_ref.shape[0] // CHUNKS
    rows = x_ref.shape[0] // CHUNKS
    first = pltpu.make_async_copy(k_hbm.at[freq], k_ref.at[freq], sems.at[0])
    first.start()
    copies = []
    for n in range(CHUNKS):
        at = pl.ds(n * size, size)
        copies.append(pltpu.make_async_copy(v_hbm.at[at], v_ref.at[at], sems.at[n + 1]))
    rest = (
        (k_hbm.at[1 - freq], k_ref.at[1 - freq]),
        (d_hbm, d_ref),
        (n_hbm, n_ref),
    )
    others = [pltpu.make_async_copy(*pair, sems.at[CHUNKS + 1 + n]) for n, pair in enumerate(rest)]
    for copy in copies + others:
        copy.start()
    first.wait()
    for n, copy in enumerate(copies):
        copy.wait()
        x = v_ref[n * size:(n + 1) * size].reshape(rows, x_ref.shape[1])
        x_ref[n * rows:(n + 1) * rows] = x
        products(freq, x, k_ref, u_ref, n * rows)
    combine(freq, o_ref, u_ref)
    for copy in others:
        copy.wait()


def adjoint_own_body(x_ref, k_ref, o_ref, u_ref):
    products(parity(), x_ref[...], k_ref, u_ref, 0)
    combine(parity(), o_ref, u_ref)


def seam_body(k_ref, d_ref, o_ref):
    freqs, _, rows, width = k_ref.shape
    odd = lax.rem(lax.axis_index("row"), 2)
    at = lax.broadcasted_iota(jnp.int32, (8, width), 0)
    place = lax.broadcasted_iota(jnp.int32, (8, width), 1)
    pick = jnp.where((at < 2) & (place == at + odd * (width - 2)), 1.0, 0.0).astype(BF)
    for f in range(freqs):
        for c in range(2):
            lo = (f * 2 + c) * rows
            o_ref[:, lo:lo + rows] = dot_nt(pick, k_ref[f, c]).astype(BF)
    coef = d_ref[...]
    spot = lax.broadcasted_iota(jnp.int32, coef.shape, 1)
    edge = jnp.sum(jnp.where(spot == odd * (width - 1), coef, 0.0), axis=1, keepdims=True)
    for n, piece in enumerate(three(edge)):
        o_ref[2 + n:3 + n, :] = jnp.broadcast_to(piece, (1, o_ref.shape[1]))


def fence_body(d_ref, o_ref):
    o_ref[...] = jnp.zeros_like(o_ref)


def stencil_matrix(coef, block):
    width = coef.shape[1]
    row_at = lax.broadcasted_iota(jnp.int32, (width, width), 0)
    col_at = lax.broadcasted_iota(jnp.int32, (width, width), 1)
    wide = jnp.broadcast_to(coef, (width, width))
    tall = jnp.sum(jnp.where(row_at == col_at, wide, 0.0), axis=1, keepdims=True)
    gap = jnp.abs(row_at - col_at)
    first = (row_at == 0) & (block == 0)
    last = (row_at == width - 1) & (block == lax.axis_size("row") - 1)
    centre = wide * wide + jnp.where(first | last, 1.0, 2.0)
    matrix = jnp.where(gap == 0, centre, jnp.where(gap == 1, -(wide + tall), jnp.where(gap == 2, 1.0, 0.0)))
    upper = matrix.astype(BF)
    return upper, (matrix - upper.astype(F32)).astype(BF)


def operator_body(k_ref, mate_ref, d_ref, got_ref, near_ref, o_ref):
    freqs, _, rows, width = k_ref.shape
    me = lax.axis_index("row")
    odd = lax.rem(me, 2)
    is_odd = odd == 1
    at = lax.broadcasted_iota(jnp.int32, (8, width), 0)
    place = lax.broadcasted_iota(jnp.int32, (8, width), 1)
    own_pick = jnp.where((at < 2) & (place == at + (1 - odd) * (width - 2)), 1.0, 0.0).astype(BF)
    mate_pick = jnp.where((at < 2) & (place == at + odd * (width - 2)), 1.0, 0.0).astype(BF)
    coef = d_ref[...]
    base = got_ref.shape[0] - TAIL
    tail = got_ref[base:, :].astype(F32)
    mate_coef = tail[0:1] + tail[1:2] + tail[2:3]

    def last_or_first(value, last):
        return jnp.where(last, value[:, width - 1:], value[:, :1])

    def outer(full):
        return full, full[2:3, :1] + full[3:4, :1] + full[4:5, :1]

    def beyond_of(full, block):
        last = lax.axis_size("row") - 1
        there = jnp.where(lax.rem(block, 2) == 1, block < last, block > 0)
        return jnp.where(there, full, 0.0)

    near, near_coef = outer(near_ref[...].astype(F32))
    far = jnp.concatenate([tail[16 + 8 * n:24 + 8 * n] for n in range(2 * freqs)], axis=1)
    far, far_coef = outer(far)
    sides = (
        (k_ref, coef, me, near, near_coef, mate_ref, mate_pick, last_or_first(mate_coef, is_odd), is_odd),
        (mate_ref, mate_coef, xor(me, 1), far, far_coef, k_ref, own_pick, last_or_first(coef, ~is_odd), ~is_odd),
    )
    for n, (ref, c_block, block, outside, outside_coef, inner_ref, pick, inside_coef, inner_left) in enumerate(sides):
        upper, lower = stencil_matrix(c_block, block)
        left_coef = jnp.where(inner_left, inside_coef, outside_coef) + c_block[:, :1]
        right_coef = jnp.where(inner_left, outside_coef, inside_coef) + c_block[:, width - 1:]
        for f in range(freqs):
            for c in range(2):
                own = ref[f, c]
                value = dot_nt(upper, own) + dot_nt(lower, own)
                inside = dot_nt(pick, inner_ref[f, c])[0:2]
                lo = (f * 2 + c) * rows
                beyond = beyond_of(outside[0:2, lo:lo + rows], block)
                left = jnp.where(inner_left, inside, beyond)
                right = jnp.where(inner_left, beyond, inside)
                extra = jnp.concatenate(
                    [
                        left[0:1] - left_coef * left[1:2],
                        left[1:2],
                        jnp.zeros((width - 4, rows), F32),
                        right[0:1],
                        right[1:2] - right_coef * right[0:1],
                    ],
                    axis=0,
                )
                o_ref[f, c, n * width:(n + 1) * width] = (value + extra).astype(BF)


def split_body(own_ref, got_ref, keep_ref, *send_refs):
    chips = len(send_refs) + 1
    blocks = lax.axis_size("row")
    probes = own_ref.shape[0] // 2
    block = probes // blocks
    size = block // chips
    chip = lax.div(lax.axis_index("col"), 2)
    me = lax.axis_index("row")
    for step, ref in enumerate((keep_ref,) + send_refs):
        target = xor(chip, step)
        at = 0
        for mate in range(2):
            for slot in range(blocks // 2):
                for c in range(2):
                    lo = c * probes + xor(me, mate + 2 * slot) * block + target * size
                    rows = part(lo, size)
                    ref[at:at + size] = (own_ref[rows, :] + got_ref[rows, :].astype(F32)).astype(ref.dtype)
                    at += size


def sum_body(keep_ref, d_ref, near_ref, fence_ref, *refs):
    stay_ref, long_ref = refs[-2:]
    size, width = stay_ref.shape
    total = keep_ref[...]
    for ref in refs[:-2]:
        total = total + ref[...].astype(F32)
    stay_ref[...] = total[:size].astype(BF)
    long_ref[:size] = total[size:].astype(BF)
    pad = jnp.zeros((13, width), BF)
    long_ref[size:size + 16] = jnp.concatenate(three(d_ref[...]) + [pad], axis=0)
    for n in range(4):
        lo = size + 16 + 8 * n
        long_ref[lo:lo + 8] = near_ref[:, n * width:(n + 1) * width]


def pack_body(got_ref, fence_ref, o_ref):
    o_ref[...] = got_ref[:o_ref.shape[0]]


def join_body(*refs):
    out_ref = refs[-1]
    chips = len(refs) // 2
    groups = lax.axis_size("row")
    size = refs[0].shape[0] // groups
    chip = lax.div(lax.axis_index("col"), 2)
    for n, ref in enumerate(refs[:-1]):
        source = xor(chip, n % chips)
        for g in range(groups):
            lo = (n // chips * groups + g) * chips * size + source * size
            out_ref[part(lo, size), :] = ref[g * size:(g + 1) * size]


def predict_body(swap, a_ref, k_ref, keep_ref, *refs):
    freq = parity()
    if swap:
        freq = 1 - freq
    half = a_ref.shape[0] // 2
    width = a_ref.shape[1]
    size = keep_ref.shape[0] // 2
    total = []
    for c in range(2):
        value = dot_nn(a_ref[:half], k_ref[freq, c, :width])
        total.append(value + dot_nn(a_ref[half:], k_ref[freq, c, width:]))
    by_real, by_imag = total
    for slot, ref in enumerate((keep_ref,) + refs):
        lo = 2 * slot * size
        mid = lo + size
        hi = mid + size
        ref[:size] = (by_real[lo:mid] - by_imag[mid:hi]).astype(ref.dtype)
        ref[size:] = (by_real[mid:hi] + by_imag[lo:mid]).astype(ref.dtype)


def final_body(slot, keeps, peers, x_ref, noise_ref, *refs):
    out_hbm, v_ref, s_ref, w_ref, sem = refs[-5:]
    keep_refs = refs[:keeps]
    got_refs = refs[keeps:keeps + peers]
    odd = lax.rem(lax.axis_index("row"), 2)

    def write(keep_ref, freq):
        size = v_ref.shape[0]
        me = lax.axis_index("row")
        total = keep_ref[...]
        for ref in got_refs:
            total = total + ref[...].astype(F32)
        x = x_ref[part(me * 4 * size, 4 * size), :].astype(F32)
        noise = noise_ref[pl.ds(freq, 1), :]
        tiles = s_ref.shape[0]
        for t in range(tiles):
            at = slice(t * LANES, (t + 1) * LANES)
            w_ref[t] = x[:, at]
            for c in range(2):
                probe = w_ref[t, pl.ds(2 * freq + c, size, stride=4), :]
                s_ref[t, pl.ds(c, size, stride=2), :] = total[c * size:(c + 1) * size, at] + noise[:, at] * probe
        values = jnp.concatenate([s_ref[t] for t in range(tiles)], axis=1)
        v_ref[...] = values.reshape(v_ref.shape)
        copy = pltpu.make_async_copy(v_ref, out_hbm.at[:, freq], sem)
        copy.start()
        copy.wait()

    if slot < 2:

        @pl.when(odd == 0)
        def _():
            write(keep_refs[-1] if slot else keep_refs[0], 1 - parity() if slot else parity())

    if slot > 0:

        @pl.when(odd == 1)
        def _():
            write(keep_refs[0], parity() if slot == 1 else 1 - parity())


def finish(slot, shape, x, noise, keeps, got, before=()):
    size, _, parts, rows = shape
    ins = [pltpu.with_memory_space_constraint(v, pltpu.VMEM) for v in (x, noise, *keeps, *got)]
    return pl.pallas_call(
        functools.partial(final_body, slot, len(keeps), len(got)),
        in_specs=[VMEM] * len(ins) + [HBM] * len(before),
        out_specs=HBM,
        out_shape=jax.ShapeDtypeStruct(shape, F32),
        input_output_aliases={len(ins): 0} if before else {},
        scratch_shapes=[
            pltpu.VMEM((size, parts, rows), F32),
            pltpu.VMEM((rows // LANES, 2 * size, LANES), F32),
            pltpu.VMEM((rows // LANES, 4 * size, LANES), F32),
            pltpu.SemaphoreType.DMA,
        ],
        compiler_params=pltpu.CompilerParams(vmem_limit_bytes=LIMIT),
    )(*ins, *before)


def choose_body(own_ref, other_ref, o_ref):
    odd = lax.rem(lax.axis_index("row"), 2)

    @pl.when(odd == 1)
    def _():
        o_ref[...] = own_ref[...]

    @pl.when(odd == 0)
    def _():
        o_ref[...] = other_ref[...]


def wide_sum(own, got, coef, near, blocks):
    rows, width = own.shape
    a = parity()
    value = own + got.astype(F32)
    both = jnp.where(a == 0, jnp.stack([value, 0 * value]), jnp.stack([0 * value, value]))
    both = lax.psum(both, "col").astype(BF).reshape(2, 2, blocks, -1, width)
    slots = 2 * jnp.arange(blocks // 2)
    me = lax.axis_index("row")

    def chosen(freq, mate):
        value = lax.dynamic_index_in_dim(both, freq, 0, keepdims=False)
        value = jnp.take(value, xor(me, mate + slots), axis=1)
        return value.transpose(1, 0, 2, 3).reshape(-1, width)

    tail = three(coef) + [jnp.zeros((13, width), BF)]
    tail += [near[:, n * width:(n + 1) * width] for n in range(4)]
    give = jnp.concatenate([chosen(1 - a, 1), chosen(a, 1)] + tail, axis=0)
    give = lax.ppermute(give, "row", pair_perm("row", 1))
    half = rows // 2
    mine = jnp.concatenate([chosen(a, 0), give[half:rows]], axis=0)
    other = jnp.concatenate([chosen(1 - a, 0), give[:half]], axis=0)
    return mine, other, give


def chip_sum(own, got, coef, near, chips):
    rows, width = own.shape
    size = rows // chips
    half = size // 2
    keep, *sends = call(split_body, (own, got), [((size, width), F32)] + [((size, width), BF)] * (chips - 1))
    fence = call(fence_body, (coef,), [((8, LANES), F32)])[0]
    got = [lax.ppermute(v, "col", pair_perm("col", 2 * (d + 1))) for d, v in enumerate(sends)]
    stay, long = call(sum_body, (keep, coef, near, fence, *got), [((half, width), BF), ((half + TAIL, width), BF)])
    fence = call(fence_body, (coef,), [((8, LANES), F32)])[0]
    pieces = [stay]
    pieces += [lax.ppermute(stay, "col", pair_perm("col", 2 * (d + 1))) for d in range(chips - 1)]
    long = lax.ppermute(long, "row", pair_perm("row", 1))
    give = call(pack_body, (long, fence), [((half, width), BF)])[0]
    pieces.append(give)
    pieces += [lax.ppermute(give, "col", pair_perm("col", 2 * (d + 1))) for d in range(chips - 1)]
    mine = call(join_body, pieces, [((rows, width), BF)])[0]
    return mine, lax.ppermute(mine, "col", pair_perm("col", 1)), long


def apply(kernel, probes, noise_var, prior_diag):
    count = probes.shape[0]
    rows, width = kernel.shape[2:]
    blocks = lax.axis_size("row")
    chips = lax.axis_size("col") // 2
    coef = prior_diag[None, :]
    flat = (4 * count, rows)
    scratch = pltpu.VMEM((2 * width // LANES, 4 * count, LANES), F32)
    mate = lax.ppermute(kernel, "row", pair_perm("row", 1))
    other, x, kernel, coef, noise = call(
        adjoint_other_body,
        (),
        [((2 * count, width), BF), (flat, BF), (kernel.shape, BF), (coef.shape, F32), (noise_var.shape, F32)],
        (pltpu.VMEM(probes.shape, BF), scratch, pltpu.SemaphoreType.DMA((CHUNKS + 4,))),
        raw=(probes, kernel, coef, noise_var),
    )
    got = lax.ppermute(other, "col", pair_perm("col", 1))
    own = call(adjoint_own_body, (x, kernel), [((2 * count, width), F32)], (scratch,))[0]
    seam = call(seam_body, (kernel, coef), [((8, 4 * rows), BF)])[0]
    odd = [i for i in range(blocks) if i % 2]
    even = [i for i in range(blocks) if i % 2 == 0]
    near = [(i, min(i + 1, blocks - 1)) for i in odd] + [(i, max(i - 1, 0)) for i in even]
    near = lax.ppermute(seam, "row", near)
    if chips > 4:
        mine, other, give = wide_sum(own, got, coef, near, blocks)
    else:
        mine, other, give = chip_sum(own, got, coef, near, chips)
    operator = call(operator_body, (kernel, mate, coef, give, near), [((2, 2, 2 * width, rows), BF)])[0]
    size = count // blocks
    peers = blocks // 2 - 1
    keeps, sends = [], []
    for swap, field in ((False, mine), (True, other)):
        keep, *send = call(
            functools.partial(predict_body, swap),
            (field, operator),
            [((2 * size, rows), F32)] + [((2 * size, rows), BF)] * peers,
        )
        keeps.append(keep)
        sends.append(send)
    shape = (size,) + probes.shape[1:3] + (rows,)
    got = [[], [], []]
    for d in range(peers):
        step = 2 * (d + 1)
        evens = [(i, i if i % 2 else i ^ step) for i in range(blocks)]
        odds = [(i, i ^ step if i % 2 else i) for i in range(blocks)]
        own, other = sends[0][d], sends[1][d]
        middle = call(choose_body, (own, other), [(own.shape, BF)])[0]
        got[0].append(lax.ppermute(own, "row", evens))
        got[1].append(lax.ppermute(middle, "row", pair_perm("row", step)))
        got[2].append(lax.ppermute(other, "row", odds))
    out = finish(0, shape, x, noise, keeps[:1], got[0])
    out = finish(1, shape, x, noise, keeps, got[1], (out,))
    return finish(2, shape, x, noise, keeps[1:], got[2], (out,))


def solution(mesh):
    in_specs = (P(None, None, "col", "row"), P(None, None, None, "col"), P(None, "col"), P("row"))
    out_specs = P("row", None, None, "col")
    return jax.shard_map(apply, mesh=mesh, in_specs=in_specs, out_specs=out_specs, check_vma=False)
```

```python
import functools

import jax
import jax.numpy as jnp
from jax import lax
from jax.experimental import pallas as pl
from jax.experimental.pallas import tpu as pltpu
from jax.sharding import PartitionSpec as P


BF = jnp.bfloat16
F32 = jnp.float32
LANES = 128
LIMIT = 24 * 2**20
VMEM = pl.BlockSpec(memory_space=pltpu.VMEM)
HBM = pl.BlockSpec(memory_space=pltpu.HBM)


def call(body, ins, outs, scratch=(), raw=()):
    return pl.pallas_call(
        body,
        in_specs=[HBM] * len(raw) + [VMEM] * len(ins),
        out_specs=[VMEM] * len(outs),
        out_shape=[pltpu.VMEM(*o) for o in outs],
        scratch_shapes=list(scratch),
        compiler_params=pltpu.CompilerParams(vmem_limit_bytes=LIMIT),
    )(*[pltpu.with_memory_space_constraint(v, pltpu.HBM) for v in raw], *[pltpu.with_memory_space_constraint(v, pltpu.VMEM) for v in ins])


def pair_perm(axis, step):
    return [(i, i ^ step) for i in range(lax.axis_size(axis))]


def parity():
    return lax.rem(lax.axis_index("col"), 2)


def xor(a, b):
    return jnp.bitwise_xor(a, b)


def part(start, size):
    return pl.ds(pl.multiple_of(start, size), size)


def dot_nt(left, right):
    return lax.dot_general(left, right, (((1,), (1,)), ((), ())), preferred_element_type=F32)


def dot_nn(left, right):
    return jnp.dot(left, right, preferred_element_type=F32)


def three(value):
    pieces = []
    for _ in range(3):
        pieces.append(value.astype(BF))
        value = value - pieces[-1].astype(F32)
    return pieces


def adjoint(freq, x, k_ref, o_ref, u_ref):
    rows = x.shape[0] // 4
    width = k_ref.shape[3]
    tiles = width // LANES
    for c in range(2):
        y = dot_nn(x, k_ref[freq, c])
        for t in range(tiles):
            u_ref[c * tiles + t] = y[:, t * LANES:(t + 1) * LANES]
    real = pl.ds(2 * freq, rows, stride=4)
    imag = pl.ds(2 * freq + 1, rows, stride=4)
    for t in range(tiles):
        at = slice(t * LANES, (t + 1) * LANES)
        o_ref[:rows, at] = (u_ref[t, real, :] + u_ref[tiles + t, imag, :]).astype(o_ref.dtype)
        o_ref[rows:, at] = (u_ref[t, imag, :] - u_ref[tiles + t, real, :]).astype(o_ref.dtype)


def adjoint_other_body(v_hbm, k_hbm, d_hbm, n_hbm, o_ref, x_ref, k_ref, d_ref, n_ref, v_ref, u_ref, sems):
    freq = 1 - parity()
    copies = [
        pltpu.make_async_copy(v_hbm, v_ref, sems.at[0]),
        pltpu.make_async_copy(k_hbm.at[freq], k_ref.at[freq], sems.at[1]),
        pltpu.make_async_copy(k_hbm.at[1 - freq], k_ref.at[1 - freq], sems.at[2]),
        pltpu.make_async_copy(d_hbm, d_ref, sems.at[3]),
        pltpu.make_async_copy(n_hbm, n_ref, sems.at[4]),
    ]
    for copy in copies[:2]:
        copy.start()
    copies[0].wait()
    x = v_ref[...].reshape(x_ref.shape)
    x_ref[...] = x
    copies[1].wait()
    for copy in copies[2:]:
        copy.start()
    adjoint(freq, x, k_ref, o_ref, u_ref)
    for copy in copies[2:]:
        copy.wait()


def adjoint_own_body(x_ref, k_ref, o_ref, u_ref):
    adjoint(parity(), x_ref[...], k_ref, o_ref, u_ref)


def seam_body(k_ref, d_ref, o_ref):
    freqs, _, rows, width = k_ref.shape
    odd = lax.rem(lax.axis_index("row"), 2)
    at = lax.broadcasted_iota(jnp.int32, (8, width), 0)
    place = lax.broadcasted_iota(jnp.int32, (8, width), 1)
    pick = jnp.where((at < 2) & (place == at + odd * (width - 2)), 1.0, 0.0).astype(BF)
    for f in range(freqs):
        for c in range(2):
            lo = (f * 2 + c) * rows
            o_ref[:, lo:lo + rows] = dot_nt(pick, k_ref[f, c]).astype(BF)
    coef = d_ref[...]
    spot = lax.broadcasted_iota(jnp.int32, coef.shape, 1)
    edge = jnp.sum(jnp.where(spot == odd * (width - 1), coef, 0.0), axis=1, keepdims=True)
    for n, piece in enumerate(three(edge)):
        o_ref[2 + n:3 + n, :] = jnp.broadcast_to(piece, (1, o_ref.shape[1]))


def fence_body(d_ref, o_ref):
    o_ref[...] = jnp.zeros_like(o_ref)


def stencil_matrix(coef, block):
    width = coef.shape[1]
    row_at = lax.broadcasted_iota(jnp.int32, (width, width), 0)
    col_at = lax.broadcasted_iota(jnp.int32, (width, width), 1)
    wide = jnp.broadcast_to(coef, (width, width))
    tall = jnp.sum(jnp.where(row_at == col_at, wide, 0.0), axis=1, keepdims=True)
    gap = jnp.abs(row_at - col_at)
    first = (row_at == 0) & (block == 0)
    last = (row_at == width - 1) & (block == lax.axis_size("row") - 1)
    centre = wide * wide + jnp.where(first | last, 1.0, 2.0)
    matrix = jnp.where(gap == 0, centre, jnp.where(gap == 1, -(wide + tall), jnp.where(gap == 2, 1.0, 0.0)))
    upper = matrix.astype(BF)
    return upper, (matrix - upper.astype(F32)).astype(BF)


def operator_body(k_ref, mate_ref, d_ref, got_ref, near_ref, far_ref, o_ref):
    freqs, _, rows, width = k_ref.shape
    me = lax.axis_index("row")
    odd = lax.rem(me, 2)
    is_odd = odd == 1
    at = lax.broadcasted_iota(jnp.int32, (8, width), 0)
    place = lax.broadcasted_iota(jnp.int32, (8, width), 1)
    own_pick = jnp.where((at < 2) & (place == at + (1 - odd) * (width - 2)), 1.0, 0.0).astype(BF)
    mate_pick = jnp.where((at < 2) & (place == at + odd * (width - 2)), 1.0, 0.0).astype(BF)
    coef = d_ref[...]
    tail = got_ref[got_ref.shape[0] - 16:, :].astype(F32)
    mate_coef = tail[0:1] + tail[1:2] + tail[2:3]

    def last_or_first(value, last):
        return jnp.where(last, value[:, width - 1:], value[:, :1])

    def outer(ref, block):
        last = lax.axis_size("row") - 1
        there = jnp.where(lax.rem(block, 2) == 1, block < last, block > 0)
        full = jnp.where(there, ref[...].astype(F32), 0.0)
        return full[0:2], full[2:3, :1] + full[3:4, :1] + full[4:5, :1]

    near, near_coef = outer(near_ref, me)
    far, far_coef = outer(far_ref, xor(me, 1))
    sides = (
        (k_ref, coef, me, near, near_coef, mate_ref, mate_pick, last_or_first(mate_coef, is_odd), is_odd),
        (mate_ref, mate_coef, xor(me, 1), far, far_coef, k_ref, own_pick, last_or_first(coef, ~is_odd), ~is_odd),
    )
    for n, (ref, c_block, block, outside, outside_coef, inner_ref, pick, inside_coef, inner_left) in enumerate(sides):
        upper, lower = stencil_matrix(c_block, block)
        left_coef = jnp.where(inner_left, inside_coef, outside_coef) + c_block[:, :1]
        right_coef = jnp.where(inner_left, outside_coef, inside_coef) + c_block[:, width - 1:]
        for f in range(freqs):
            for c in range(2):
                own = ref[f, c]
                value = dot_nt(upper, own) + dot_nt(lower, own)
                inside = dot_nt(pick, inner_ref[f, c])[0:2]
                lo = (f * 2 + c) * rows
                beyond = outside[:, lo:lo + rows]
                left = jnp.where(inner_left, inside, beyond)
                right = jnp.where(inner_left, beyond, inside)
                extra = jnp.concatenate(
                    [
                        left[0:1] - left_coef * left[1:2],
                        left[1:2],
                        jnp.zeros((width - 4, rows), F32),
                        right[0:1],
                        right[1:2] - right_coef * right[0:1],
                    ],
                    axis=0,
                )
                o_ref[f, c, n * width:(n + 1) * width] = (value + extra).astype(BF)


def split_body(own_ref, got_ref, keep_ref, *send_refs):
    chips = len(send_refs) + 1
    blocks = lax.axis_size("row")
    probes = own_ref.shape[0] // 2
    block = probes // blocks
    size = block // chips
    chip = lax.div(lax.axis_index("col"), 2)
    me = lax.axis_index("row")
    for step, ref in enumerate((keep_ref,) + send_refs):
        target = xor(chip, step)
        at = 0
        for mate in range(2):
            for slot in range(blocks // 2):
                for c in range(2):
                    lo = c * probes + xor(me, mate + 2 * slot) * block + target * size
                    rows = part(lo, size)
                    ref[at:at + size] = (own_ref[rows, :] + got_ref[rows, :].astype(F32)).astype(ref.dtype)
                    at += size


def sum_body(keep_ref, d_ref, fence_ref, *refs):
    stay_ref, give_ref = refs[-2:]
    size = stay_ref.shape[0]
    total = keep_ref[...]
    for ref in refs[:-2]:
        total = total + ref[...].astype(F32)
    stay_ref[...] = total[:size].astype(BF)
    give_ref[:size] = total[size:].astype(BF)
    pad = jnp.zeros((13, d_ref.shape[1]), BF)
    give_ref[size:] = jnp.concatenate(three(d_ref[...]) + [pad], axis=0)


def pack_body(stay_ref, got_ref, fence_ref, o_ref):
    size = stay_ref.shape[0]
    o_ref[:size] = stay_ref[...]
    o_ref[size:] = got_ref[:size]


def join_body(mine_ref, *refs):
    out_ref = refs[-1]
    pieces = (mine_ref,) + refs[:-1]
    chips = len(pieces)
    groups = 2 * lax.axis_size("row")
    size = mine_ref.shape[0] // groups
    chip = lax.div(lax.axis_index("col"), 2)
    for step, ref in enumerate(pieces):
        source = xor(chip, step)
        for n in range(groups):
            lo = n * chips * size + source * size
            out_ref[part(lo, size), :] = ref[n * size:(n + 1) * size]


def predict_body(swap, a_ref, k_ref, keep_ref, *refs):
    freq = parity()
    if swap:
        freq = 1 - freq
    half = a_ref.shape[0] // 2
    width = a_ref.shape[1]
    size = keep_ref.shape[0] // 2
    total = []
    for c in range(2):
        value = dot_nn(a_ref[:half], k_ref[freq, c, :width])
        total.append(value + dot_nn(a_ref[half:], k_ref[freq, c, width:]))
    by_real, by_imag = total
    for slot, ref in enumerate((keep_ref,) + refs):
        lo = 2 * slot * size
        mid = lo + size
        hi = mid + size
        ref[:size] = (by_real[lo:mid] - by_imag[mid:hi]).astype(ref.dtype)
        ref[size:] = (by_real[mid:hi] + by_imag[lo:mid]).astype(ref.dtype)


def final_body(peers, x_ref, noise_ref, *refs):
    out_ref, s_ref = refs[-2:]
    size = out_ref.shape[0]
    rows = 4 * size
    me = lax.axis_index("row")
    freq = parity()
    for which in range(2):
        group = refs[which * (peers + 1):(which + 1) * (peers + 1)]
        total = group[0][...]
        for ref in group[1:]:
            total = total + ref[...].astype(F32)
        f = freq if which == 0 else 1 - freq
        for t in range(s_ref.shape[0]):
            at = slice(t * LANES, (t + 1) * LANES)
            s_ref[t, pl.ds(2 * f, size, stride=4), :] = total[:size, at]
            s_ref[t, pl.ds(2 * f + 1, size, stride=4), :] = total[size:, at]
    x = x_ref[part(me * rows, rows), :].astype(F32)
    kind = lax.rem(lax.broadcasted_iota(jnp.int32, x.shape, 0), 4)
    noise = jnp.where(kind < 2, noise_ref[0:1, :], noise_ref[1:2, :])
    values = jnp.concatenate([s_ref[t] for t in range(s_ref.shape[0])], axis=1) + noise * x
    out_ref[...] = values.reshape(out_ref.shape)


def wide_sum(own, got, coef, blocks):
    rows, width = own.shape
    a = parity()
    value = own + got.astype(F32)
    both = jnp.where(a == 0, jnp.stack([value, 0 * value]), jnp.stack([0 * value, value]))
    both = lax.psum(both, "col").astype(BF).reshape(2, 2, blocks, -1, width)
    slots = 2 * jnp.arange(blocks // 2)
    me = lax.axis_index("row")

    def chosen(freq, mate):
        value = lax.dynamic_index_in_dim(both, freq, 0, keepdims=False)
        value = jnp.take(value, xor(me, mate + slots), axis=1)
        return value.transpose(1, 0, 2, 3).reshape(-1, width)

    tail = jnp.concatenate(three(coef) + [jnp.zeros((13, width), BF)], axis=0)
    give = jnp.concatenate([chosen(1 - a, 1), chosen(a, 1), tail], axis=0)
    give = lax.ppermute(give, "row", pair_perm("row", 1))
    half = rows // 2
    mine = jnp.concatenate([chosen(a, 0), give[half:rows]], axis=0)
    other = jnp.concatenate([chosen(1 - a, 0), give[:half]], axis=0)
    return mine, other, give


def chip_sum(own, got, coef, chips):
    rows, width = own.shape
    size = rows // chips
    keep, *sends = call(split_body, (own, got), [((size, width), F32)] + [((size, width), BF)] * (chips - 1))
    fence = call(fence_body, (coef,), [((8, LANES), F32)])[0]
    got = [lax.ppermute(v, "col", pair_perm("col", 2 * (d + 1))) for d, v in enumerate(sends)]
    stay, give = call(sum_body, (keep, coef, fence, *got), [((size // 2, width), BF), ((size // 2 + 16, width), BF)])
    fence = call(fence_body, (coef,), [((8, LANES), F32)])[0]
    give = lax.ppermute(give, "row", pair_perm("row", 1))
    mine = call(pack_body, (stay, give, fence), [((size, width), BF)])[0]
    got = [lax.ppermute(mine, "col", pair_perm("col", 2 * (d + 1))) for d in range(chips - 1)]
    mine = call(join_body, (mine, *got), [((rows, width), BF)])[0]
    return mine, lax.ppermute(mine, "col", pair_perm("col", 1)), give


def apply(kernel, probes, noise_var, prior_diag):
    count = probes.shape[0]
    rows, width = kernel.shape[2:]
    blocks = lax.axis_size("row")
    chips = lax.axis_size("col") // 2
    coef = prior_diag[None, :]
    flat = (4 * count, rows)
    scratch = pltpu.VMEM((2 * width // LANES, 4 * count, LANES), F32)
    mate = lax.ppermute(kernel, "row", pair_perm("row", 1))
    other, x, kernel, coef, noise = call(
        adjoint_other_body,
        (),
        [((2 * count, width), BF), (flat, BF), (kernel.shape, BF), (coef.shape, F32), (noise_var.shape, F32)],
        (pltpu.VMEM(probes.shape, BF), scratch, pltpu.SemaphoreType.DMA((5,))),
        raw=(probes, kernel, coef, noise_var),
    )
    got = lax.ppermute(other, "col", pair_perm("col", 1))
    own = call(adjoint_own_body, (x, kernel), [((2 * count, width), F32)], (scratch,))[0]
    seam = call(seam_body, (kernel, coef), [((8, 4 * rows), BF)])[0]
    odd = [i for i in range(blocks) if i % 2]
    even = [i for i in range(blocks) if i % 2 == 0]
    near = [(i, i + 1) for i in odd if i + 1 < blocks] + [(i, i - 1) for i in even if i]
    far = [(i, i + 2 if i + 2 < blocks else 1) for i in odd] + [(i, i - 2 if i else blocks - 2) for i in even]
    near = lax.ppermute(seam, "row", near)
    far = lax.ppermute(seam, "row", far)
    if chips > 4:
        mine, other, give = wide_sum(own, got, coef, blocks)
    else:
        mine, other, give = chip_sum(own, got, coef, chips)
    operator = call(operator_body, (kernel, mate, coef, give, near, far), [((2, 2, 2 * width, rows), BF)])[0]
    size = count // blocks
    peers = blocks // 2 - 1
    groups = []
    for swap, field in ((False, mine), (True, other)):
        keep, *sends = call(
            functools.partial(predict_body, swap),
            (field, operator),
            [((2 * size, rows), F32)] + [((2 * size, rows), BF)] * peers,
        )
        groups.append(keep)
        groups += [lax.ppermute(v, "row", pair_perm("row", 2 * (d + 1))) for d, v in enumerate(sends)]
    return call(
        functools.partial(final_body, peers),
        (x, noise, *groups),
        [((size,) + probes.shape[1:3] + (rows,), F32)],
        (pltpu.VMEM((rows // LANES, 4 * size, LANES), F32),),
    )[0]


def solution(mesh):
    in_specs = (P(None, None, "col", "row"), P(None, None, None, "col"), P(None, "col"), P("row"))
    out_specs = P("row", None, None, "col")
    return jax.shard_map(apply, mesh=mesh, in_specs=in_specs, out_specs=out_specs, check_vma=False)
```

```python
import functools

import jax
import jax.numpy as jnp
from jax import lax
from jax.experimental import pallas as pl
from jax.experimental.pallas import tpu as pltpu
from jax.sharding import PartitionSpec as P


BF = jnp.bfloat16
F32 = jnp.float32
LANES = 128
LIMIT = 24 * 2**20
VMEM = pl.BlockSpec(memory_space=pltpu.VMEM)
HBM = pl.BlockSpec(memory_space=pltpu.HBM)


def call(body, ins, outs, scratch=(), raw=()):
    return pl.pallas_call(
        body,
        in_specs=[HBM] * len(raw) + [VMEM] * len(ins),
        out_specs=[VMEM] * len(outs),
        out_shape=[pltpu.VMEM(*o) for o in outs],
        scratch_shapes=list(scratch),
        compiler_params=pltpu.CompilerParams(vmem_limit_bytes=LIMIT),
    )(*[pltpu.with_memory_space_constraint(v, pltpu.HBM) for v in raw], *[pltpu.with_memory_space_constraint(v, pltpu.VMEM) for v in ins])


def pair_perm(axis, step):
    return [(i, i ^ step) for i in range(lax.axis_size(axis))]


def parity():
    return lax.rem(lax.axis_index("col"), 2)


def xor(a, b):
    return jnp.bitwise_xor(a, b)


def part(start, size):
    return pl.ds(pl.multiple_of(start, size), size)


def dot_nt(left, right):
    return lax.dot_general(left, right, (((1,), (1,)), ((), ())), preferred_element_type=F32)


def dot_nn(left, right):
    return jnp.dot(left, right, preferred_element_type=F32)


def three(value):
    pieces = []
    for _ in range(3):
        pieces.append(value.astype(BF))
        value = value - pieces[-1].astype(F32)
    return pieces


def adjoint(freq, x, k_ref, o_ref, u_ref):
    rows = x.shape[0] // 4
    width = k_ref.shape[3]
    tiles = width // LANES
    for c in range(2):
        y = dot_nn(x, k_ref[freq, c])
        for t in range(tiles):
            u_ref[c * tiles + t] = y[:, t * LANES:(t + 1) * LANES]
    real = pl.ds(2 * freq, rows, stride=4)
    imag = pl.ds(2 * freq + 1, rows, stride=4)
    for t in range(tiles):
        at = slice(t * LANES, (t + 1) * LANES)
        o_ref[:rows, at] = (u_ref[t, real, :] + u_ref[tiles + t, imag, :]).astype(o_ref.dtype)
        o_ref[rows:, at] = (u_ref[t, imag, :] - u_ref[tiles + t, real, :]).astype(o_ref.dtype)


def adjoint_other_body(v_hbm, k_hbm, d_hbm, n_hbm, o_ref, x_ref, k_ref, d_ref, n_ref, v_ref, u_ref, sems):
    freq = 1 - parity()
    copies = [
        pltpu.make_async_copy(v_hbm, v_ref, sems.at[0]),
        pltpu.make_async_copy(k_hbm.at[freq], k_ref.at[freq], sems.at[1]),
        pltpu.make_async_copy(k_hbm.at[1 - freq], k_ref.at[1 - freq], sems.at[2]),
        pltpu.make_async_copy(d_hbm, d_ref, sems.at[3]),
        pltpu.make_async_copy(n_hbm, n_ref, sems.at[4]),
    ]
    for copy in copies:
        copy.start()
    copies[0].wait()
    x = v_ref[...].reshape(x_ref.shape)
    x_ref[...] = x
    copies[1].wait()
    adjoint(freq, x, k_ref, o_ref, u_ref)
    for copy in copies[2:]:
        copy.wait()


def adjoint_own_body(x_ref, k_ref, o_ref, u_ref):
    adjoint(parity(), x_ref[...], k_ref, o_ref, u_ref)


def seam_body(k_ref, d_ref, o_ref):
    freqs, _, rows, width = k_ref.shape
    odd = lax.rem(lax.axis_index("row"), 2)
    at = lax.broadcasted_iota(jnp.int32, (8, width), 0)
    place = lax.broadcasted_iota(jnp.int32, (8, width), 1)
    pick = jnp.where((at < 2) & (place == at + odd * (width - 2)), 1.0, 0.0).astype(BF)
    for f in range(freqs):
        for c in range(2):
            lo = (f * 2 + c) * rows
            o_ref[:, lo:lo + rows] = dot_nt(pick, k_ref[f, c]).astype(BF)
    coef = d_ref[...]
    spot = lax.broadcasted_iota(jnp.int32, coef.shape, 1)
    edge = jnp.sum(jnp.where(spot == odd * (width - 1), coef, 0.0), axis=1, keepdims=True)
    for n, piece in enumerate(three(edge)):
        o_ref[2 + n:3 + n, :] = jnp.broadcast_to(piece, (1, o_ref.shape[1]))


def fence_body(d_ref, o_ref):
    o_ref[...] = jnp.zeros_like(o_ref)


def stencil_matrix(coef, block):
    width = coef.shape[1]
    row_at = lax.broadcasted_iota(jnp.int32, (width, width), 0)
    col_at = lax.broadcasted_iota(jnp.int32, (width, width), 1)
    wide = jnp.broadcast_to(coef, (width, width))
    tall = jnp.sum(jnp.where(row_at == col_at, wide, 0.0), axis=1, keepdims=True)
    gap = jnp.abs(row_at - col_at)
    first = (row_at == 0) & (block == 0)
    last = (row_at == width - 1) & (block == lax.axis_size("row") - 1)
    centre = wide * wide + jnp.where(first | last, 1.0, 2.0)
    matrix = jnp.where(gap == 0, centre, jnp.where(gap == 1, -(wide + tall), jnp.where(gap == 2, 1.0, 0.0)))
    upper = matrix.astype(BF)
    return upper, (matrix - upper.astype(F32)).astype(BF)


def operator_body(k_ref, mate_ref, d_ref, got_ref, near_ref, far_ref, o_ref):
    freqs, _, rows, width = k_ref.shape
    me = lax.axis_index("row")
    odd = lax.rem(me, 2)
    is_odd = odd == 1
    at = lax.broadcasted_iota(jnp.int32, (8, width), 0)
    place = lax.broadcasted_iota(jnp.int32, (8, width), 1)
    own_pick = jnp.where((at < 2) & (place == at + (1 - odd) * (width - 2)), 1.0, 0.0).astype(BF)
    mate_pick = jnp.where((at < 2) & (place == at + odd * (width - 2)), 1.0, 0.0).astype(BF)
    coef = d_ref[...]
    tail = got_ref[got_ref.shape[0] - 16:, :].astype(F32)
    mate_coef = tail[0:1] + tail[1:2] + tail[2:3]

    def last_or_first(value, last):
        return jnp.where(last, value[:, width - 1:], value[:, :1])

    def outer(ref, block):
        last = lax.axis_size("row") - 1
        there = jnp.where(lax.rem(block, 2) == 1, block < last, block > 0)
        full = jnp.where(there, ref[...].astype(F32), 0.0)
        return full[0:2], full[2:3, :1] + full[3:4, :1] + full[4:5, :1]

    near, near_coef = outer(near_ref, me)
    far, far_coef = outer(far_ref, xor(me, 1))
    sides = (
        (k_ref, coef, me, near, near_coef, mate_ref, mate_pick, last_or_first(mate_coef, is_odd), is_odd),
        (mate_ref, mate_coef, xor(me, 1), far, far_coef, k_ref, own_pick, last_or_first(coef, ~is_odd), ~is_odd),
    )
    for n, (ref, c_block, block, outside, outside_coef, inner_ref, pick, inside_coef, inner_left) in enumerate(sides):
        upper, lower = stencil_matrix(c_block, block)
        left_coef = jnp.where(inner_left, inside_coef, outside_coef) + c_block[:, :1]
        right_coef = jnp.where(inner_left, outside_coef, inside_coef) + c_block[:, width - 1:]
        for f in range(freqs):
            for c in range(2):
                own = ref[f, c]
                value = dot_nt(upper, own) + dot_nt(lower, own)
                inside = dot_nt(pick, inner_ref[f, c])[0:2]
                lo = (f * 2 + c) * rows
                beyond = outside[:, lo:lo + rows]
                left = jnp.where(inner_left, inside, beyond)
                right = jnp.where(inner_left, beyond, inside)
                extra = jnp.concatenate(
                    [
                        left[0:1] - left_coef * left[1:2],
                        left[1:2],
                        jnp.zeros((width - 4, rows), F32),
                        right[0:1],
                        right[1:2] - right_coef * right[0:1],
                    ],
                    axis=0,
                )
                o_ref[f, c, n * width:(n + 1) * width] = (value + extra).astype(BF)


def split_body(own_ref, got_ref, keep_ref, *send_refs):
    chips = len(send_refs) + 1
    blocks = lax.axis_size("row")
    probes = own_ref.shape[0] // 2
    block = probes // blocks
    size = block // chips
    chip = lax.div(lax.axis_index("col"), 2)
    me = lax.axis_index("row")
    for step, ref in enumerate((keep_ref,) + send_refs):
        target = xor(chip, step)
        at = 0
        for mate in range(2):
            for slot in range(blocks // 2):
                for c in range(2):
                    lo = c * probes + xor(me, mate + 2 * slot) * block + target * size
                    rows = part(lo, size)
                    ref[at:at + size] = (own_ref[rows, :] + got_ref[rows, :].astype(F32)).astype(ref.dtype)
                    at += size


def sum_body(keep_ref, d_ref, fence_ref, *refs):
    stay_ref, give_ref = refs[-2:]
    size = stay_ref.shape[0]
    total = keep_ref[...]
    for ref in refs[:-2]:
        total = total + ref[...].astype(F32)
    stay_ref[...] = total[:size].astype(BF)
    give_ref[:size] = total[size:].astype(BF)
    pad = jnp.zeros((13, d_ref.shape[1]), BF)
    give_ref[size:] = jnp.concatenate(three(d_ref[...]) + [pad], axis=0)


def pack_body(stay_ref, got_ref, fence_ref, o_ref):
    size = stay_ref.shape[0]
    o_ref[:size] = stay_ref[...]
    o_ref[size:] = got_ref[:size]


def join_body(mine_ref, *refs):
    out_ref = refs[-1]
    pieces = (mine_ref,) + refs[:-1]
    chips = len(pieces)
    groups = 2 * lax.axis_size("row")
    size = mine_ref.shape[0] // groups
    chip = lax.div(lax.axis_index("col"), 2)
    for step, ref in enumerate(pieces):
        source = xor(chip, step)
        for n in range(groups):
            lo = n * chips * size + source * size
            out_ref[part(lo, size), :] = ref[n * size:(n + 1) * size]


def predict(freq, a_ref, k_ref, targets):
    half = a_ref.shape[0] // 2
    width = a_ref.shape[1]
    size = targets[0].shape[0] // 2
    total = []
    for c in range(2):
        value = dot_nn(a_ref[:half], k_ref[freq, c, :width])
        total.append(value + dot_nn(a_ref[half:], k_ref[freq, c, width:]))
    by_real, by_imag = total
    for slot, ref in enumerate(targets):
        lo = 2 * slot * size
        mid = lo + size
        hi = mid + size
        ref[:size] = (by_real[lo:mid] - by_imag[mid:hi]).astype(ref.dtype)
        ref[size:] = (by_real[mid:hi] + by_imag[lo:mid]).astype(ref.dtype)


def predict_own_body(a_ref, k_ref, *outs):
    predict(parity(), a_ref, k_ref, outs)


def predict_other_body(peers, a_ref, k_ref, *refs):
    owns, keep_ref, sends = refs[:peers], refs[peers], refs[peers + 1:]
    size = keep_ref.shape[0]
    for own, send in zip(owns, sends):
        send[:size] = own[...]
    predict(1 - parity(), a_ref, k_ref, (keep_ref,) + tuple(send.at[size:] for send in sends))


def final_body(x_ref, noise_ref, own_ref, other_ref, *refs):
    out_ref, s_ref = refs[-2:]
    size = out_ref.shape[0]
    rows = 4 * size
    half = 2 * size
    me = lax.axis_index("row")
    freq = parity()
    for which, keep_ref in enumerate((own_ref, other_ref)):
        total = keep_ref[...]
        for ref in refs[:-2]:
            total = total + ref[which * half:(which + 1) * half].astype(F32)
        f = freq if which == 0 else 1 - freq
        for t in range(s_ref.shape[0]):
            at = slice(t * LANES, (t + 1) * LANES)
            s_ref[t, pl.ds(2 * f, size, stride=4), :] = total[:size, at]
            s_ref[t, pl.ds(2 * f + 1, size, stride=4), :] = total[size:, at]
    x = x_ref[part(me * rows, rows), :].astype(F32)
    kind = lax.rem(lax.broadcasted_iota(jnp.int32, x.shape, 0), 4)
    noise = jnp.where(kind < 2, noise_ref[0:1, :], noise_ref[1:2, :])
    values = jnp.concatenate([s_ref[t] for t in range(s_ref.shape[0])], axis=1) + noise * x
    out_ref[...] = values.reshape(out_ref.shape)


def wide_sum(own, got, coef, blocks):
    rows, width = own.shape
    a = parity()
    value = own + got.astype(F32)
    both = jnp.where(a == 0, jnp.stack([value, 0 * value]), jnp.stack([0 * value, value]))
    both = lax.psum(both, "col").astype(BF).reshape(2, 2, blocks, -1, width)
    slots = 2 * jnp.arange(blocks // 2)
    me = lax.axis_index("row")

    def chosen(freq, mate):
        value = lax.dynamic_index_in_dim(both, freq, 0, keepdims=False)
        value = jnp.take(value, xor(me, mate + slots), axis=1)
        return value.transpose(1, 0, 2, 3).reshape(-1, width)

    tail = jnp.concatenate(three(coef) + [jnp.zeros((13, width), BF)], axis=0)
    give = jnp.concatenate([chosen(1 - a, 1), chosen(a, 1), tail], axis=0)
    give = lax.ppermute(give, "row", pair_perm("row", 1))
    half = rows // 2
    mine = jnp.concatenate([chosen(a, 0), give[half:rows]], axis=0)
    other = jnp.concatenate([chosen(1 - a, 0), give[:half]], axis=0)
    return mine, other, give


def chip_sum(own, got, coef, chips):
    rows, width = own.shape
    size = rows // chips
    keep, *sends = call(split_body, (own, got), [((size, width), F32)] + [((size, width), BF)] * (chips - 1))
    fence = call(fence_body, (coef,), [((8, LANES), F32)])[0]
    got = [lax.ppermute(v, "col", pair_perm("col", 2 * (d + 1))) for d, v in enumerate(sends)]
    stay, give = call(sum_body, (keep, coef, fence, *got), [((size // 2, width), BF), ((size // 2 + 16, width), BF)])
    fence = call(fence_body, (coef,), [((8, LANES), F32)])[0]
    give = lax.ppermute(give, "row", pair_perm("row", 1))
    mine = call(pack_body, (stay, give, fence), [((size, width), BF)])[0]
    got = [lax.ppermute(mine, "col", pair_perm("col", 2 * (d + 1))) for d in range(chips - 1)]
    mine = call(join_body, (mine, *got), [((rows, width), BF)])[0]
    return mine, lax.ppermute(mine, "col", pair_perm("col", 1)), give


def apply(kernel, probes, noise_var, prior_diag):
    count = probes.shape[0]
    rows, width = kernel.shape[2:]
    blocks = lax.axis_size("row")
    chips = lax.axis_size("col") // 2
    coef = prior_diag[None, :]
    flat = (4 * count, rows)
    scratch = pltpu.VMEM((2 * width // LANES, 4 * count, LANES), F32)
    mate = lax.ppermute(kernel, "row", pair_perm("row", 1))
    other, x, kernel, coef, noise = call(
        adjoint_other_body,
        (),
        [((2 * count, width), BF), (flat, BF), (kernel.shape, BF), (coef.shape, F32), (noise_var.shape, F32)],
        (pltpu.VMEM(probes.shape, BF), scratch, pltpu.SemaphoreType.DMA((5,))),
        raw=(probes, kernel, coef, noise_var),
    )
    got = lax.ppermute(other, "col", pair_perm("col", 1))
    own = call(adjoint_own_body, (x, kernel), [((2 * count, width), F32)], (scratch,))[0]
    seam = call(seam_body, (kernel, coef), [((8, 4 * rows), BF)])[0]
    odd = [i for i in range(blocks) if i % 2]
    even = [i for i in range(blocks) if i % 2 == 0]
    near = [(i, i + 1) for i in odd if i + 1 < blocks] + [(i, i - 1) for i in even if i]
    far = [(i, i + 2 if i + 2 < blocks else 1) for i in odd] + [(i, i - 2 if i else blocks - 2) for i in even]
    near = lax.ppermute(seam, "row", near)
    far = lax.ppermute(seam, "row", far)
    if chips > 4:
        mine, other, give = wide_sum(own, got, coef, blocks)
    else:
        mine, other, give = chip_sum(own, got, coef, chips)
    operator = call(operator_body, (kernel, mate, coef, give, near, far), [((2, 2, 2 * width, rows), BF)])[0]
    size = count // blocks
    peers = blocks // 2 - 1
    half = (2 * size, rows)
    keep_own, *owns = call(predict_own_body, (mine, operator), [(half, F32)] + [(half, BF)] * peers)
    keep_other, *sends = call(
        functools.partial(predict_other_body, peers),
        (other, operator, *owns),
        [(half, F32)] + [((4 * size, rows), BF)] * peers,
    )
    got = [lax.ppermute(v, "row", pair_perm("row", 2 * (d + 1))) for d, v in enumerate(sends)]
    return call(
        final_body,
        (x, noise, keep_own, keep_other, *got),
        [((size,) + probes.shape[1:3] + (rows,), F32)],
        (pltpu.VMEM((rows // LANES, 4 * size, LANES), F32),),
    )[0]


def solution(mesh):
    in_specs = (P(None, None, "col", "row"), P(None, None, None, "col"), P(None, "col"), P("row"))
    out_specs = P("row", None, None, "col")
    return jax.shard_map(apply, mesh=mesh, in_specs=in_specs, out_specs=out_specs, check_vma=False)
```

```python
import functools

import jax
import jax.numpy as jnp
from jax import lax
from jax.experimental import pallas as pl
from jax.experimental.pallas import tpu as pltpu
from jax.sharding import PartitionSpec as P


BF = jnp.bfloat16
F32 = jnp.float32
LANES = 128
LIMIT = 24 * 2**20
VMEM = pl.BlockSpec(memory_space=pltpu.VMEM)
HBM = pl.BlockSpec(memory_space=pltpu.HBM)


def call(body, ins, outs, scratch=(), raw=()):
    return pl.pallas_call(
        body,
        in_specs=[HBM] * len(raw) + [VMEM] * len(ins),
        out_specs=[VMEM] * len(outs),
        out_shape=[pltpu.VMEM(*o) for o in outs],
        scratch_shapes=list(scratch),
        compiler_params=pltpu.CompilerParams(vmem_limit_bytes=LIMIT),
    )(*[pltpu.with_memory_space_constraint(v, pltpu.HBM) for v in raw], *[pltpu.with_memory_space_constraint(v, pltpu.VMEM) for v in ins])


def pair_perm(axis, step):
    return [(i, i ^ step) for i in range(lax.axis_size(axis))]


def parity():
    return lax.rem(lax.axis_index("col"), 2)


def xor(a, b):
    return jnp.bitwise_xor(a, b)


def cross(slot):
    return 2 * slot + 1 if slot else 0


def part(start, size):
    return pl.ds(pl.multiple_of(start, size), size)


def dot_nt(left, right):
    return lax.dot_general(left, right, (((1,), (1,)), ((), ())), preferred_element_type=F32)


def dot_nn(left, right):
    return jnp.dot(left, right, preferred_element_type=F32)


def three(value):
    pieces = []
    for _ in range(3):
        pieces.append(value.astype(BF))
        value = value - pieces[-1].astype(F32)
    return pieces


def adjoint(freq, x, k_ref, o_ref, u_ref):
    rows = x.shape[0] // 4
    width = k_ref.shape[3]
    tiles = width // LANES
    for c in range(2):
        y = dot_nn(x, k_ref[freq, c])
        for t in range(tiles):
            u_ref[c * tiles + t] = y[:, t * LANES:(t + 1) * LANES]
    real = pl.ds(2 * freq, rows, stride=4)
    imag = pl.ds(2 * freq + 1, rows, stride=4)
    for t in range(tiles):
        at = slice(t * LANES, (t + 1) * LANES)
        o_ref[:rows, at] = (u_ref[t, real, :] + u_ref[tiles + t, imag, :]).astype(o_ref.dtype)
        o_ref[rows:, at] = (u_ref[t, imag, :] - u_ref[tiles + t, real, :]).astype(o_ref.dtype)


def adjoint_other_body(v_hbm, k_hbm, d_hbm, n_hbm, o_ref, x_ref, k_ref, d_ref, n_ref, v_ref, u_ref, sems):
    freq = 1 - parity()
    copies = [
        pltpu.make_async_copy(v_hbm, v_ref, sems.at[0]),
        pltpu.make_async_copy(k_hbm.at[freq], k_ref.at[freq], sems.at[1]),
        pltpu.make_async_copy(k_hbm.at[1 - freq], k_ref.at[1 - freq], sems.at[2]),
        pltpu.make_async_copy(d_hbm, d_ref, sems.at[3]),
        pltpu.make_async_copy(n_hbm, n_ref, sems.at[4]),
    ]
    for copy in copies:
        copy.start()
    copies[0].wait()
    x = v_ref[...].reshape(x_ref.shape)
    x_ref[...] = x
    copies[1].wait()
    adjoint(freq, x, k_ref, o_ref, u_ref)
    for copy in copies[2:]:
        copy.wait()


def adjoint_own_body(x_ref, k_ref, o_ref, u_ref):
    adjoint(parity(), x_ref[...], k_ref, o_ref, u_ref)


def seam_body(k_ref, d_ref, o_ref):
    freqs, _, rows, width = k_ref.shape
    odd = lax.rem(lax.axis_index("row"), 2)
    at = lax.broadcasted_iota(jnp.int32, (8, width), 0)
    place = lax.broadcasted_iota(jnp.int32, (8, width), 1)
    pick = jnp.where((at < 2) & (place == at + odd * (width - 2)), 1.0, 0.0).astype(BF)
    for f in range(freqs):
        for c in range(2):
            lo = (f * 2 + c) * rows
            o_ref[:, lo:lo + rows] = dot_nt(pick, k_ref[f, c]).astype(BF)
    coef = d_ref[...]
    spot = lax.broadcasted_iota(jnp.int32, coef.shape, 1)
    edge = jnp.sum(jnp.where(spot == odd * (width - 1), coef, 0.0), axis=1, keepdims=True)
    for n, piece in enumerate(three(edge)):
        o_ref[2 + n:3 + n, :] = jnp.broadcast_to(piece, (1, o_ref.shape[1]))


def fence_body(d_ref, o_ref):
    o_ref[...] = jnp.zeros_like(o_ref)


def stencil_matrix(coef, block):
    width = coef.shape[1]
    row_at = lax.broadcasted_iota(jnp.int32, (width, width), 0)
    col_at = lax.broadcasted_iota(jnp.int32, (width, width), 1)
    wide = jnp.broadcast_to(coef, (width, width))
    tall = jnp.sum(jnp.where(row_at == col_at, wide, 0.0), axis=1, keepdims=True)
    gap = jnp.abs(row_at - col_at)
    first = (row_at == 0) & (block == 0)
    last = (row_at == width - 1) & (block == lax.axis_size("row") - 1)
    centre = wide * wide + jnp.where(first | last, 1.0, 2.0)
    matrix = jnp.where(gap == 0, centre, jnp.where(gap == 1, -(wide + tall), jnp.where(gap == 2, 1.0, 0.0)))
    upper = matrix.astype(BF)
    return upper, (matrix - upper.astype(F32)).astype(BF)


def operator_body(k_ref, mate_ref, d_ref, got_ref, near_ref, far_ref, o_ref):
    freqs, _, rows, width = k_ref.shape
    me = lax.axis_index("row")
    odd = lax.rem(me, 2)
    is_odd = odd == 1
    at = lax.broadcasted_iota(jnp.int32, (8, width), 0)
    place = lax.broadcasted_iota(jnp.int32, (8, width), 1)
    own_pick = jnp.where((at < 2) & (place == at + (1 - odd) * (width - 2)), 1.0, 0.0).astype(BF)
    mate_pick = jnp.where((at < 2) & (place == at + odd * (width - 2)), 1.0, 0.0).astype(BF)
    coef = d_ref[...]
    tail = got_ref[got_ref.shape[0] - 16:, :].astype(F32)
    mate_coef = tail[0:1] + tail[1:2] + tail[2:3]

    def last_or_first(value, last):
        return jnp.where(last, value[:, width - 1:], value[:, :1])

    def outer(ref, block):
        last = lax.axis_size("row") - 1
        there = jnp.where(lax.rem(block, 2) == 1, block < last, block > 0)
        full = jnp.where(there, ref[...].astype(F32), 0.0)
        return full[0:2], full[2:3, :1] + full[3:4, :1] + full[4:5, :1]

    near, near_coef = outer(near_ref, me)
    far, far_coef = outer(far_ref, xor(me, 1))
    sides = (
        (k_ref, coef, me, near, near_coef, mate_ref, mate_pick, last_or_first(mate_coef, is_odd), is_odd),
        (mate_ref, mate_coef, xor(me, 1), far, far_coef, k_ref, own_pick, last_or_first(coef, ~is_odd), ~is_odd),
    )
    for n, (ref, c_block, block, outside, outside_coef, inner_ref, pick, inside_coef, inner_left) in enumerate(sides):
        upper, lower = stencil_matrix(c_block, block)
        left_coef = jnp.where(inner_left, inside_coef, outside_coef) + c_block[:, :1]
        right_coef = jnp.where(inner_left, outside_coef, inside_coef) + c_block[:, width - 1:]
        for f in range(freqs):
            for c in range(2):
                own = ref[f, c]
                value = dot_nt(upper, own) + dot_nt(lower, own)
                inside = dot_nt(pick, inner_ref[f, c])[0:2]
                lo = (f * 2 + c) * rows
                beyond = outside[:, lo:lo + rows]
                left = jnp.where(inner_left, inside, beyond)
                right = jnp.where(inner_left, beyond, inside)
                extra = jnp.concatenate(
                    [
                        left[0:1] - left_coef * left[1:2],
                        left[1:2],
                        jnp.zeros((width - 4, rows), F32),
                        right[0:1],
                        right[1:2] - right_coef * right[0:1],
                    ],
                    axis=0,
                )
                o_ref[f, c, n * width:(n + 1) * width] = (value + extra).astype(BF)


def split_body(own_ref, got_ref, keep_ref, *send_refs):
    chips = len(send_refs) + 1
    blocks = lax.axis_size("row")
    probes = own_ref.shape[0] // 2
    block = probes // blocks
    size = block // chips
    chip = lax.div(lax.axis_index("col"), 2)
    me = lax.axis_index("row")
    for step, ref in enumerate((keep_ref,) + send_refs):
        target = xor(chip, step)
        at = 0
        for mate in range(2):
            for slot in range(blocks // 2):
                for c in range(2):
                    lo = c * probes + xor(me, mate ^ cross(slot)) * block + target * size
                    rows = part(lo, size)
                    ref[at:at + size] = (own_ref[rows, :] + got_ref[rows, :].astype(F32)).astype(ref.dtype)
                    at += size


def sum_body(keep_ref, d_ref, fence_ref, *refs):
    stay_ref, give_ref = refs[-2:]
    size = stay_ref.shape[0]
    total = keep_ref[...]
    for ref in refs[:-2]:
        total = total + ref[...].astype(F32)
    stay_ref[...] = total[:size].astype(BF)
    give_ref[:size] = total[size:].astype(BF)
    pad = jnp.zeros((13, d_ref.shape[1]), BF)
    give_ref[size:] = jnp.concatenate(three(d_ref[...]) + [pad], axis=0)


def pack_body(stay_ref, got_ref, fence_ref, o_ref):
    size = stay_ref.shape[0]
    o_ref[:size] = stay_ref[...]
    o_ref[size:] = got_ref[:size]


def join_body(mine_ref, *refs):
    out_ref = refs[-1]
    pieces = (mine_ref,) + refs[:-1]
    chips = len(pieces)
    groups = 2 * lax.axis_size("row")
    size = mine_ref.shape[0] // groups
    chip = lax.div(lax.axis_index("col"), 2)
    for step, ref in enumerate(pieces):
        source = xor(chip, step)
        for n in range(groups):
            lo = n * chips * size + source * size
            out_ref[part(lo, size), :] = ref[n * size:(n + 1) * size]


def predict(freq, a_ref, k_ref, targets):
    half = a_ref.shape[0] // 2
    width = a_ref.shape[1]
    size = targets[0].shape[0] // 2
    total = []
    for c in range(2):
        value = dot_nn(a_ref[:half], k_ref[freq, c, :width])
        total.append(value + dot_nn(a_ref[half:], k_ref[freq, c, width:]))
    by_real, by_imag = total
    for slot, ref in enumerate(targets):
        lo = 2 * slot * size
        mid = lo + size
        hi = mid + size
        ref[:size] = (by_real[lo:mid] - by_imag[mid:hi]).astype(ref.dtype)
        ref[size:] = (by_real[mid:hi] + by_imag[lo:mid]).astype(ref.dtype)


def predict_own_body(a_ref, k_ref, *outs):
    predict(parity(), a_ref, k_ref, outs)


def predict_other_body(peers, a_ref, k_ref, *refs):
    owns, keep_ref, sends = refs[:peers], refs[peers], refs[peers + 1:]
    size = keep_ref.shape[0]
    for own, send in zip(owns, sends):
        send[:size] = own[...]
    predict(1 - parity(), a_ref, k_ref, (keep_ref,) + tuple(send.at[size:] for send in sends))


def final_body(x_ref, noise_ref, own_ref, other_ref, *refs):
    out_ref, s_ref = refs[-2:]
    size = out_ref.shape[0]
    rows = 4 * size
    half = 2 * size
    me = lax.axis_index("row")
    freq = parity()
    for which, keep_ref in enumerate((own_ref, other_ref)):
        total = keep_ref[...]
        for ref in refs[:-2]:
            total = total + ref[which * half:(which + 1) * half].astype(F32)
        f = freq if which == 0 else 1 - freq
        for t in range(s_ref.shape[0]):
            at = slice(t * LANES, (t + 1) * LANES)
            s_ref[t, pl.ds(2 * f, size, stride=4), :] = total[:size, at]
            s_ref[t, pl.ds(2 * f + 1, size, stride=4), :] = total[size:, at]
    x = x_ref[part(me * rows, rows), :].astype(F32)
    kind = lax.rem(lax.broadcasted_iota(jnp.int32, x.shape, 0), 4)
    noise = jnp.where(kind < 2, noise_ref[0:1, :], noise_ref[1:2, :])
    values = jnp.concatenate([s_ref[t] for t in range(s_ref.shape[0])], axis=1) + noise * x
    out_ref[...] = values.reshape(out_ref.shape)


def wide_sum(own, got, coef, blocks):
    rows, width = own.shape
    a = parity()
    value = own + got.astype(F32)
    both = jnp.where(a == 0, jnp.stack([value, 0 * value]), jnp.stack([0 * value, value]))
    both = lax.psum(both, "col").astype(BF).reshape(2, 2, blocks, -1, width)
    slots = jnp.array([cross(slot) for slot in range(blocks // 2)])
    me = lax.axis_index("row")

    def chosen(freq, mate):
        value = lax.dynamic_index_in_dim(both, freq, 0, keepdims=False)
        value = jnp.take(value, xor(me, xor(mate, slots)), axis=1)
        return value.transpose(1, 0, 2, 3).reshape(-1, width)

    tail = jnp.concatenate(three(coef) + [jnp.zeros((13, width), BF)], axis=0)
    give = jnp.concatenate([chosen(1 - a, 1), chosen(a, 1), tail], axis=0)
    give = lax.ppermute(give, "row", pair_perm("row", 1))
    half = rows // 2
    mine = jnp.concatenate([chosen(a, 0), give[half:rows]], axis=0)
    other = jnp.concatenate([chosen(1 - a, 0), give[:half]], axis=0)
    return mine, other, give


def chip_sum(own, got, coef, chips):
    rows, width = own.shape
    size = rows // chips
    keep, *sends = call(split_body, (own, got), [((size, width), F32)] + [((size, width), BF)] * (chips - 1))
    fence = call(fence_body, (coef,), [((8, LANES), F32)])[0]
    got = [lax.ppermute(v, "col", pair_perm("col", 2 * (d + 1))) for d, v in enumerate(sends)]
    stay, give = call(sum_body, (keep, coef, fence, *got), [((size // 2, width), BF), ((size // 2 + 16, width), BF)])
    fence = call(fence_body, (coef,), [((8, LANES), F32)])[0]
    give = lax.ppermute(give, "row", pair_perm("row", 1))
    mine = call(pack_body, (stay, give, fence), [((size, width), BF)])[0]
    got = [lax.ppermute(mine, "col", pair_perm("col", 2 * (d + 1))) for d in range(chips - 1)]
    mine = call(join_body, (mine, *got), [((rows, width), BF)])[0]
    return mine, lax.ppermute(mine, "col", pair_perm("col", 1)), give


def apply(kernel, probes, noise_var, prior_diag):
    count = probes.shape[0]
    rows, width = kernel.shape[2:]
    blocks = lax.axis_size("row")
    chips = lax.axis_size("col") // 2
    coef = prior_diag[None, :]
    flat = (4 * count, rows)
    scratch = pltpu.VMEM((2 * width // LANES, 4 * count, LANES), F32)
    mate = lax.ppermute(kernel, "row", pair_perm("row", 1))
    other, x, kernel, coef, noise = call(
        adjoint_other_body,
        (),
        [((2 * count, width), BF), (flat, BF), (kernel.shape, BF), (coef.shape, F32), (noise_var.shape, F32)],
        (pltpu.VMEM(probes.shape, BF), scratch, pltpu.SemaphoreType.DMA((5,))),
        raw=(probes, kernel, coef, noise_var),
    )
    got = lax.ppermute(other, "col", pair_perm("col", 1))
    own = call(adjoint_own_body, (x, kernel), [((2 * count, width), F32)], (scratch,))[0]
    seam = call(seam_body, (kernel, coef), [((8, 4 * rows), BF)])[0]
    odd = [i for i in range(blocks) if i % 2]
    even = [i for i in range(blocks) if i % 2 == 0]
    near = [(i, i + 1) for i in odd if i + 1 < blocks] + [(i, i - 1) for i in even if i]
    far = [(i, i + 2 if i + 2 < blocks else 1) for i in odd] + [(i, i - 2 if i else blocks - 2) for i in even]
    near = lax.ppermute(seam, "row", near)
    far = lax.ppermute(seam, "row", far)
    if chips > 4:
        mine, other, give = wide_sum(own, got, coef, blocks)
    else:
        mine, other, give = chip_sum(own, got, coef, chips)
    operator = call(operator_body, (kernel, mate, coef, give, near, far), [((2, 2, 2 * width, rows), BF)])[0]
    size = count // blocks
    peers = blocks // 2 - 1
    half = (2 * size, rows)
    keep_own, *owns = call(predict_own_body, (mine, operator), [(half, F32)] + [(half, BF)] * peers)
    keep_other, *sends = call(
        functools.partial(predict_other_body, peers),
        (other, operator, *owns),
        [(half, F32)] + [((4 * size, rows), BF)] * peers,
    )
    got = [lax.ppermute(v, "row", pair_perm("row", cross(d + 1))) for d, v in enumerate(sends)]
    return call(
        final_body,
        (x, noise, keep_own, keep_other, *got),
        [((size,) + probes.shape[1:3] + (rows,), F32)],
        (pltpu.VMEM((rows // LANES, 4 * size, LANES), F32),),
    )[0]


def solution(mesh):
    in_specs = (P(None, None, "col", "row"), P(None, None, None, "col"), P(None, "col"), P("row"))
    out_specs = P("row", None, None, "col")
    return jax.shard_map(apply, mesh=mesh, in_specs=in_specs, out_specs=out_specs, check_vma=False)
```

```python
import functools

import jax
import jax.numpy as jnp
from jax import lax
from jax.experimental import pallas as pl
from jax.experimental.pallas import tpu as pltpu
from jax.sharding import PartitionSpec as P


BF = jnp.bfloat16
F32 = jnp.float32
LANES = 128
LIMIT = 24 * 2**20
VMEM = pl.BlockSpec(memory_space=pltpu.VMEM)
HBM = pl.BlockSpec(memory_space=pltpu.HBM)


def call(body, ins, outs, scratch=(), raw=()):
    return pl.pallas_call(
        body,
        in_specs=[HBM] * len(raw) + [VMEM] * len(ins),
        out_specs=[VMEM] * len(outs),
        out_shape=[pltpu.VMEM(*o) for o in outs],
        scratch_shapes=list(scratch),
        compiler_params=pltpu.CompilerParams(vmem_limit_bytes=LIMIT),
    )(*[pltpu.with_memory_space_constraint(v, pltpu.HBM) for v in raw], *[pltpu.with_memory_space_constraint(v, pltpu.VMEM) for v in ins])


def pair_perm(axis, step):
    return [(i, i ^ step) for i in range(lax.axis_size(axis))]


def parity():
    value = lax.axis_index("col")
    for shift in range(1, lax.axis_size("col").bit_length()):
        value = xor(value, lax.shift_right_logical(lax.axis_index("col"), jnp.int32(shift)))
    return lax.rem(xor(value, lax.axis_index("row")), 2)


def hop(step):
    return 2 * step + step.bit_count() % 2


def mate_perm():
    cols = lax.axis_size("col")
    return [(i * cols + j, (i ^ 1) * cols + (j ^ 1)) for i in range(lax.axis_size("row")) for j in range(cols)]


def xor(a, b):
    return jnp.bitwise_xor(a, b)


def cross(slot):
    return 2 * slot + 1 if slot else 0


def part(start, size):
    return pl.ds(pl.multiple_of(start, size), size)


def dot_nt(left, right):
    return lax.dot_general(left, right, (((1,), (1,)), ((), ())), preferred_element_type=F32)


def dot_nn(left, right):
    return jnp.dot(left, right, preferred_element_type=F32)


def three(value):
    pieces = []
    for _ in range(3):
        pieces.append(value.astype(BF))
        value = value - pieces[-1].astype(F32)
    return pieces


def adjoint(freq, x, k_ref, o_ref, u_ref):
    rows = x.shape[0] // 4
    width = k_ref.shape[3]
    tiles = width // LANES
    for c in range(2):
        y = dot_nn(x, k_ref[freq, c])
        for t in range(tiles):
            u_ref[c * tiles + t] = y[:, t * LANES:(t + 1) * LANES]
    real = pl.ds(2 * freq, rows, stride=4)
    imag = pl.ds(2 * freq + 1, rows, stride=4)
    for t in range(tiles):
        at = slice(t * LANES, (t + 1) * LANES)
        o_ref[:rows, at] = (u_ref[t, real, :] + u_ref[tiles + t, imag, :]).astype(o_ref.dtype)
        o_ref[rows:, at] = (u_ref[t, imag, :] - u_ref[tiles + t, real, :]).astype(o_ref.dtype)


def adjoint_other_body(v_hbm, k_hbm, d_hbm, n_hbm, o_ref, x_ref, k_ref, d_ref, n_ref, v_ref, u_ref, sems):
    freq = 1 - parity()
    copies = [
        pltpu.make_async_copy(v_hbm, v_ref, sems.at[0]),
        pltpu.make_async_copy(k_hbm.at[freq], k_ref.at[freq], sems.at[1]),
        pltpu.make_async_copy(k_hbm.at[1 - freq], k_ref.at[1 - freq], sems.at[2]),
        pltpu.make_async_copy(d_hbm, d_ref, sems.at[3]),
        pltpu.make_async_copy(n_hbm, n_ref, sems.at[4]),
    ]
    for copy in copies:
        copy.start()
    copies[0].wait()
    x = v_ref[...].reshape(x_ref.shape)
    x_ref[...] = x
    copies[1].wait()
    adjoint(freq, x, k_ref, o_ref, u_ref)
    for copy in copies[2:]:
        copy.wait()


def adjoint_own_body(x_ref, k_ref, o_ref, u_ref):
    adjoint(parity(), x_ref[...], k_ref, o_ref, u_ref)


def seam_body(k_ref, d_ref, o_ref):
    freqs, _, rows, width = k_ref.shape
    odd = lax.rem(lax.axis_index("row"), 2)
    at = lax.broadcasted_iota(jnp.int32, (8, width), 0)
    place = lax.broadcasted_iota(jnp.int32, (8, width), 1)
    pick = jnp.where((at < 2) & (place == at + odd * (width - 2)), 1.0, 0.0).astype(BF)
    for f in range(freqs):
        for c in range(2):
            lo = (f * 2 + c) * rows
            o_ref[:, lo:lo + rows] = dot_nt(pick, k_ref[f, c]).astype(BF)
    coef = d_ref[...]
    spot = lax.broadcasted_iota(jnp.int32, coef.shape, 1)
    edge = jnp.sum(jnp.where(spot == odd * (width - 1), coef, 0.0), axis=1, keepdims=True)
    for n, piece in enumerate(three(edge)):
        o_ref[2 + n:3 + n, :] = jnp.broadcast_to(piece, (1, o_ref.shape[1]))


def fence_body(d_ref, o_ref):
    o_ref[...] = jnp.zeros_like(o_ref)


def stencil_matrix(coef, block):
    width = coef.shape[1]
    row_at = lax.broadcasted_iota(jnp.int32, (width, width), 0)
    col_at = lax.broadcasted_iota(jnp.int32, (width, width), 1)
    wide = jnp.broadcast_to(coef, (width, width))
    tall = jnp.sum(jnp.where(row_at == col_at, wide, 0.0), axis=1, keepdims=True)
    gap = jnp.abs(row_at - col_at)
    first = (row_at == 0) & (block == 0)
    last = (row_at == width - 1) & (block == lax.axis_size("row") - 1)
    centre = wide * wide + jnp.where(first | last, 1.0, 2.0)
    matrix = jnp.where(gap == 0, centre, jnp.where(gap == 1, -(wide + tall), jnp.where(gap == 2, 1.0, 0.0)))
    upper = matrix.astype(BF)
    return upper, (matrix - upper.astype(F32)).astype(BF)


def operator_body(k_ref, mate_ref, d_ref, got_ref, near_ref, far_ref, o_ref):
    freqs, _, rows, width = k_ref.shape
    me = lax.axis_index("row")
    odd = lax.rem(me, 2)
    is_odd = odd == 1
    at = lax.broadcasted_iota(jnp.int32, (8, width), 0)
    place = lax.broadcasted_iota(jnp.int32, (8, width), 1)
    own_pick = jnp.where((at < 2) & (place == at + (1 - odd) * (width - 2)), 1.0, 0.0).astype(BF)
    mate_pick = jnp.where((at < 2) & (place == at + odd * (width - 2)), 1.0, 0.0).astype(BF)
    coef = d_ref[...]
    tail = got_ref[got_ref.shape[0] - 16:, :].astype(F32)
    mate_coef = tail[0:1] + tail[1:2] + tail[2:3]

    def last_or_first(value, last):
        return jnp.where(last, value[:, width - 1:], value[:, :1])

    def outer(ref, block):
        last = lax.axis_size("row") - 1
        there = jnp.where(lax.rem(block, 2) == 1, block < last, block > 0)
        full = jnp.where(there, ref[...].astype(F32), 0.0)
        return full[0:2], full[2:3, :1] + full[3:4, :1] + full[4:5, :1]

    near, near_coef = outer(near_ref, me)
    far, far_coef = outer(far_ref, xor(me, 1))
    sides = (
        (k_ref, coef, me, near, near_coef, mate_ref, mate_pick, last_or_first(mate_coef, is_odd), is_odd),
        (mate_ref, mate_coef, xor(me, 1), far, far_coef, k_ref, own_pick, last_or_first(coef, ~is_odd), ~is_odd),
    )
    for n, (ref, c_block, block, outside, outside_coef, inner_ref, pick, inside_coef, inner_left) in enumerate(sides):
        upper, lower = stencil_matrix(c_block, block)
        left_coef = jnp.where(inner_left, inside_coef, outside_coef) + c_block[:, :1]
        right_coef = jnp.where(inner_left, outside_coef, inside_coef) + c_block[:, width - 1:]
        for f in range(freqs):
            for c in range(2):
                own = ref[f, c]
                value = dot_nt(upper, own) + dot_nt(lower, own)
                inside = dot_nt(pick, inner_ref[f, c])[0:2]
                lo = (f * 2 + c) * rows
                beyond = outside[:, lo:lo + rows]
                left = jnp.where(inner_left, inside, beyond)
                right = jnp.where(inner_left, beyond, inside)
                extra = jnp.concatenate(
                    [
                        left[0:1] - left_coef * left[1:2],
                        left[1:2],
                        jnp.zeros((width - 4, rows), F32),
                        right[0:1],
                        right[1:2] - right_coef * right[0:1],
                    ],
                    axis=0,
                )
                o_ref[f, c, n * width:(n + 1) * width] = (value + extra).astype(BF)


def split_body(own_ref, got_ref, keep_ref, *send_refs):
    chips = len(send_refs) + 1
    blocks = lax.axis_size("row")
    probes = own_ref.shape[0] // 2
    block = probes // blocks
    size = block // chips
    chip = lax.div(lax.axis_index("col"), 2)
    me = lax.axis_index("row")
    for step, ref in enumerate((keep_ref,) + send_refs):
        target = xor(chip, step)
        at = 0
        for mate in range(2):
            for slot in range(blocks // 2):
                for c in range(2):
                    lo = c * probes + xor(me, mate ^ cross(slot)) * block + target * size
                    rows = part(lo, size)
                    ref[at:at + size] = (own_ref[rows, :] + got_ref[rows, :].astype(F32)).astype(ref.dtype)
                    at += size


def sum_body(keep_ref, d_ref, fence_ref, *refs):
    stay_ref, give_ref = refs[-2:]
    size = stay_ref.shape[0]
    total = keep_ref[...]
    for ref in refs[:-2]:
        total = total + ref[...].astype(F32)
    stay_ref[...] = total[:size].astype(BF)
    give_ref[:size] = total[size:].astype(BF)
    pad = jnp.zeros((13, d_ref.shape[1]), BF)
    give_ref[size:] = jnp.concatenate(three(d_ref[...]) + [pad], axis=0)


def pack_body(stay_ref, got_ref, fence_ref, o_ref):
    size = stay_ref.shape[0]
    o_ref[:size] = stay_ref[...]
    o_ref[size:] = got_ref[:size]


def join_body(mine_ref, *refs):
    out_ref = refs[-1]
    pieces = (mine_ref,) + refs[:-1]
    chips = len(pieces)
    groups = 2 * lax.axis_size("row")
    size = mine_ref.shape[0] // groups
    chip = lax.div(lax.axis_index("col"), 2)
    for step, ref in enumerate(pieces):
        source = xor(chip, step)
        for n in range(groups):
            lo = n * chips * size + source * size
            out_ref[part(lo, size), :] = ref[n * size:(n + 1) * size]


def predict(freq, a_ref, k_ref, targets):
    half = a_ref.shape[0] // 2
    width = a_ref.shape[1]
    size = targets[0].shape[0] // 2
    total = []
    for c in range(2):
        value = dot_nn(a_ref[:half], k_ref[freq, c, :width])
        total.append(value + dot_nn(a_ref[half:], k_ref[freq, c, width:]))
    by_real, by_imag = total
    for slot, ref in enumerate(targets):
        kind = F32 if slot == 0 else BF
        lo = 2 * slot * size
        mid = lo + size
        hi = mid + size
        ref[:size] = (by_real[lo:mid] - by_imag[mid:hi]).astype(kind)
        ref[size:] = (by_real[mid:hi] + by_imag[lo:mid]).astype(kind)


def predict_own_body(a_ref, k_ref, *outs):
    predict(parity(), a_ref, k_ref, outs)


def predict_other_body(peers, a_ref, k_ref, *refs):
    owns, keep_ref, sends = refs[:peers], refs[peers], refs[peers + 1:]
    size = keep_ref.shape[0]
    freq = parity()
    for own, send in zip(owns, sends):
        send[part(freq * size, size), :] = own[...]
    rest = part((1 - freq) * size, size)
    predict(1 - freq, a_ref, k_ref, (keep_ref,) + tuple(send.at[rest] for send in sends))


def final_body(x_ref, noise_ref, own_ref, other_ref, *refs):
    out_ref, s_ref = refs[-2:]
    size = out_ref.shape[0]
    rows = 4 * size
    half = 2 * size
    me = lax.axis_index("row")
    freq = parity()
    for which, keep_ref in enumerate((own_ref, other_ref)):
        f = freq if which == 0 else 1 - freq
        total = keep_ref[...]
        for ref in refs[:-2]:
            total = total + ref[part(f * half, half), :].astype(F32)
        for t in range(s_ref.shape[0]):
            at = slice(t * LANES, (t + 1) * LANES)
            s_ref[t, pl.ds(2 * f, size, stride=4), :] = total[:size, at]
            s_ref[t, pl.ds(2 * f + 1, size, stride=4), :] = total[size:, at]
    x = x_ref[part(me * rows, rows), :].astype(F32)
    kind = lax.rem(lax.broadcasted_iota(jnp.int32, x.shape, 0), 4)
    noise = jnp.where(kind < 2, noise_ref[0:1, :], noise_ref[1:2, :])
    values = jnp.concatenate([s_ref[t] for t in range(s_ref.shape[0])], axis=1) + noise * x
    out_ref[...] = values.reshape(out_ref.shape)


def wide_sum(own, got, coef, blocks):
    rows, width = own.shape
    a = parity()
    value = own + got.astype(F32)
    both = jnp.where(a == 0, jnp.stack([value, 0 * value]), jnp.stack([0 * value, value]))
    both = lax.psum(both, "col").astype(BF).reshape(2, 2, blocks, -1, width)
    slots = jnp.array([cross(slot) for slot in range(blocks // 2)])
    me = lax.axis_index("row")

    def chosen(freq, mate):
        value = lax.dynamic_index_in_dim(both, freq, 0, keepdims=False)
        value = jnp.take(value, xor(me, xor(mate, slots)), axis=1)
        return value.transpose(1, 0, 2, 3).reshape(-1, width)

    tail = jnp.concatenate(three(coef) + [jnp.zeros((13, width), BF)], axis=0)
    give = jnp.concatenate([chosen(0, 1), chosen(1, 1), tail], axis=0)
    give = lax.ppermute(give, "row", pair_perm("row", 1))
    fields = []
    for freq in (a, 1 - a):
        mate = lax.dynamic_slice_in_dim(give, freq * (rows // 2), rows // 2, 0)
        fields.append(jnp.concatenate([chosen(freq, 0), mate], axis=0))
    return (*fields, give)


def chip_sum(own, got, coef, chips):
    rows, width = own.shape
    size = rows // chips
    keep, *sends = call(split_body, (own, got), [((size, width), F32)] + [((size, width), BF)] * (chips - 1))
    fence = call(fence_body, (coef,), [((8, LANES), F32)])[0]
    got = [lax.ppermute(v, "col", pair_perm("col", hop(d + 1))) for d, v in enumerate(sends)]
    stay, give = call(sum_body, (keep, coef, fence, *got), [((size // 2, width), BF), ((size // 2 + 16, width), BF)])
    fence = call(fence_body, (coef,), [((8, LANES), F32)])[0]
    give = lax.ppermute(give, ("row", "col"), mate_perm())
    mine = call(pack_body, (stay, give, fence), [((size, width), BF)])[0]
    got = [lax.ppermute(mine, "col", pair_perm("col", hop(d + 1))) for d in range(chips - 1)]
    mine = call(join_body, (mine, *got), [((rows, width), BF)])[0]
    return mine, lax.ppermute(mine, "col", pair_perm("col", 1)), give


def apply(kernel, probes, noise_var, prior_diag):
    count = probes.shape[0]
    rows, width = kernel.shape[2:]
    blocks = lax.axis_size("row")
    chips = lax.axis_size("col") // 2
    coef = prior_diag[None, :]
    flat = (4 * count, rows)
    scratch = pltpu.VMEM((2 * width // LANES, 4 * count, LANES), F32)
    mate = lax.ppermute(kernel, "row", pair_perm("row", 1))
    other, x, kernel, coef, noise = call(
        adjoint_other_body,
        (),
        [((2 * count, width), BF), (flat, BF), (kernel.shape, BF), (coef.shape, F32), (noise_var.shape, F32)],
        (pltpu.VMEM(probes.shape, BF), scratch, pltpu.SemaphoreType.DMA((5,))),
        raw=(probes, kernel, coef, noise_var),
    )
    got = lax.ppermute(other, "col", pair_perm("col", 1))
    own = call(adjoint_own_body, (x, kernel), [((2 * count, width), F32)], (scratch,))[0]
    seam = call(seam_body, (kernel, coef), [((8, 4 * rows), BF)])[0]
    odd = [i for i in range(blocks) if i % 2]
    even = [i for i in range(blocks) if i % 2 == 0]
    near = [(i, i + 1) for i in odd if i + 1 < blocks] + [(i, i - 1) for i in even if i]
    far = [(i, i + 2 if i + 2 < blocks else 1) for i in odd] + [(i, i - 2 if i else blocks - 2) for i in even]
    near = lax.ppermute(seam, "row", near)
    far = lax.ppermute(seam, "row", far)
    if chips > 4:
        mine, other, give = wide_sum(own, got, coef, blocks)
    else:
        mine, other, give = chip_sum(own, got, coef, chips)
    operator = call(operator_body, (kernel, mate, coef, give, near, far), [((2, 2, 2 * width, rows), BF)])[0]
    size = count // blocks
    peers = blocks // 2 - 1
    half = (2 * size, rows)
    keep_own, *owns = call(predict_own_body, (mine, operator), [(half, F32)] + [(half, BF)] * peers)
    keep_other, *sends = call(
        functools.partial(predict_other_body, peers),
        (other, operator, *owns),
        [(half, F32)] + [((4 * size, rows), BF)] * peers,
    )
    got = [lax.ppermute(v, "row", pair_perm("row", cross(d + 1))) for d, v in enumerate(sends)]
    return call(
        final_body,
        (x, noise, keep_own, keep_other, *got),
        [((size,) + probes.shape[1:3] + (rows,), F32)],
        (pltpu.VMEM((rows // LANES, 4 * size, LANES), F32),),
    )[0]


def solution(mesh):
    in_specs = (P(None, None, "col", "row"), P(None, None, None, "col"), P(None, "col"), P("row"))
    out_specs = P("row", None, None, "col")
    return jax.shard_map(apply, mesh=mesh, in_specs=in_specs, out_specs=out_specs, check_vma=False)
```

```python
import functools

import jax
import jax.numpy as jnp
from jax import lax
from jax.experimental import pallas as pl
from jax.experimental.pallas import tpu as pltpu
from jax.sharding import PartitionSpec as P


BF = jnp.bfloat16
F32 = jnp.float32
LANES = 128
LIMIT = 24 * 2**20
VMEM = pl.BlockSpec(memory_space=pltpu.VMEM)
HBM = pl.BlockSpec(memory_space=pltpu.HBM)


def call(body, ins, outs, scratch=(), raw=()):
    return pl.pallas_call(
        body,
        in_specs=[HBM] * len(raw) + [VMEM] * len(ins),
        out_specs=[VMEM] * len(outs),
        out_shape=[pltpu.VMEM(*o) for o in outs],
        scratch_shapes=list(scratch),
        compiler_params=pltpu.CompilerParams(vmem_limit_bytes=LIMIT),
    )(*[pltpu.with_memory_space_constraint(v, pltpu.HBM) for v in raw], *[pltpu.with_memory_space_constraint(v, pltpu.VMEM) for v in ins])


def pair_perm(axis, step):
    return [(i, i ^ step) for i in range(lax.axis_size(axis))]


def parity():
    value = lax.axis_index("col")
    for shift in range(1, lax.axis_size("col").bit_length()):
        value = xor(value, lax.shift_right_logical(lax.axis_index("col"), jnp.int32(shift)))
    return lax.rem(xor(value, lax.axis_index("row")), 2)


def hop(step):
    return 2 * step + step.bit_count() % 2


def mate_perm():
    cols = lax.axis_size("col")
    return [(i * cols + j, (i ^ 1) * cols + (j ^ 1)) for i in range(lax.axis_size("row")) for j in range(cols)]


def xor(a, b):
    return jnp.bitwise_xor(a, b)


def cross(slot):
    return 2 * slot + 1 if slot else 0


def part(start, size):
    return pl.ds(pl.multiple_of(start, size), size)


def dot_nt(left, right):
    return lax.dot_general(left, right, (((1,), (1,)), ((), ())), preferred_element_type=F32)


def dot_nn(left, right):
    return jnp.dot(left, right, preferred_element_type=F32)


def three(value):
    pieces = []
    for _ in range(3):
        pieces.append(value.astype(BF))
        value = value - pieces[-1].astype(F32)
    return pieces


def adjoint(freq, x, k_ref, o_ref, u_ref):
    rows = x.shape[0] // 4
    width = k_ref.shape[3]
    tiles = width // LANES
    for c in range(2):
        y = dot_nn(x, k_ref[freq, c])
        for t in range(tiles):
            u_ref[c * tiles + t] = y[:, t * LANES:(t + 1) * LANES]
    real = pl.ds(2 * freq, rows, stride=4)
    imag = pl.ds(2 * freq + 1, rows, stride=4)
    for t in range(tiles):
        at = slice(t * LANES, (t + 1) * LANES)
        o_ref[:rows, at] = (u_ref[t, real, :] + u_ref[tiles + t, imag, :]).astype(o_ref.dtype)
        o_ref[rows:, at] = (u_ref[t, imag, :] - u_ref[tiles + t, real, :]).astype(o_ref.dtype)


def adjoint_other_body(v_hbm, k_hbm, d_hbm, n_hbm, o_ref, x_ref, k_ref, d_ref, n_ref, v_ref, u_ref, sems):
    freq = 1 - parity()
    copies = [
        pltpu.make_async_copy(v_hbm, v_ref, sems.at[0]),
        pltpu.make_async_copy(k_hbm.at[freq], k_ref.at[freq], sems.at[1]),
        pltpu.make_async_copy(k_hbm.at[1 - freq], k_ref.at[1 - freq], sems.at[2]),
        pltpu.make_async_copy(d_hbm, d_ref, sems.at[3]),
        pltpu.make_async_copy(n_hbm, n_ref, sems.at[4]),
    ]
    for copy in copies:
        copy.start()
    copies[0].wait()
    x = v_ref[...].reshape(x_ref.shape)
    x_ref[...] = x
    copies[1].wait()
    adjoint(freq, x, k_ref, o_ref, u_ref)
    for copy in copies[2:]:
        copy.wait()


def adjoint_own_body(x_ref, k_ref, o_ref, u_ref):
    adjoint(parity(), x_ref[...], k_ref, o_ref, u_ref)


def seam_body(k_ref, d_ref, o_ref):
    freqs, _, rows, width = k_ref.shape
    odd = lax.rem(lax.axis_index("row"), 2)
    at = lax.broadcasted_iota(jnp.int32, (8, width), 0)
    place = lax.broadcasted_iota(jnp.int32, (8, width), 1)
    pick = jnp.where((at < 2) & (place == at + odd * (width - 2)), 1.0, 0.0).astype(BF)
    for f in range(freqs):
        for c in range(2):
            lo = (f * 2 + c) * rows
            o_ref[:, lo:lo + rows] = dot_nt(pick, k_ref[f, c]).astype(BF)
    coef = d_ref[...]
    spot = lax.broadcasted_iota(jnp.int32, coef.shape, 1)
    edge = jnp.sum(jnp.where(spot == odd * (width - 1), coef, 0.0), axis=1, keepdims=True)
    for n, piece in enumerate(three(edge)):
        o_ref[2 + n:3 + n, :] = jnp.broadcast_to(piece, (1, o_ref.shape[1]))


def fence_body(d_ref, o_ref):
    o_ref[...] = jnp.zeros_like(o_ref)


def stencil_matrix(coef, block):
    width = coef.shape[1]
    row_at = lax.broadcasted_iota(jnp.int32, (width, width), 0)
    col_at = lax.broadcasted_iota(jnp.int32, (width, width), 1)
    wide = jnp.broadcast_to(coef, (width, width))
    tall = jnp.sum(jnp.where(row_at == col_at, wide, 0.0), axis=1, keepdims=True)
    gap = jnp.abs(row_at - col_at)
    first = (row_at == 0) & (block == 0)
    last = (row_at == width - 1) & (block == lax.axis_size("row") - 1)
    centre = wide * wide + jnp.where(first | last, 1.0, 2.0)
    matrix = jnp.where(gap == 0, centre, jnp.where(gap == 1, -(wide + tall), jnp.where(gap == 2, 1.0, 0.0)))
    upper = matrix.astype(BF)
    return upper, (matrix - upper.astype(F32)).astype(BF)


def operator_body(k_ref, mate_ref, d_ref, got_ref, near_ref, far_ref, o_ref):
    freqs, _, rows, width = k_ref.shape
    me = lax.axis_index("row")
    odd = lax.rem(me, 2)
    is_odd = odd == 1
    at = lax.broadcasted_iota(jnp.int32, (8, width), 0)
    place = lax.broadcasted_iota(jnp.int32, (8, width), 1)
    own_pick = jnp.where((at < 2) & (place == at + (1 - odd) * (width - 2)), 1.0, 0.0).astype(BF)
    mate_pick = jnp.where((at < 2) & (place == at + odd * (width - 2)), 1.0, 0.0).astype(BF)
    coef = d_ref[...]
    tail = got_ref[got_ref.shape[0] - 16:, :].astype(F32)
    mate_coef = tail[0:1] + tail[1:2] + tail[2:3]

    def last_or_first(value, last):
        return jnp.where(last, value[:, width - 1:], value[:, :1])

    def outer(ref, block):
        last = lax.axis_size("row") - 1
        there = jnp.where(lax.rem(block, 2) == 1, block < last, block > 0)
        full = jnp.where(there, ref[...].astype(F32), 0.0)
        return full[0:2], full[2:3, :1] + full[3:4, :1] + full[4:5, :1]

    near, near_coef = outer(near_ref, me)
    far, far_coef = outer(far_ref, xor(me, 1))
    sides = (
        (k_ref, coef, me, near, near_coef, mate_ref, mate_pick, last_or_first(mate_coef, is_odd), is_odd),
        (mate_ref, mate_coef, xor(me, 1), far, far_coef, k_ref, own_pick, last_or_first(coef, ~is_odd), ~is_odd),
    )
    for n, (ref, c_block, block, outside, outside_coef, inner_ref, pick, inside_coef, inner_left) in enumerate(sides):
        upper, lower = stencil_matrix(c_block, block)
        left_coef = jnp.where(inner_left, inside_coef, outside_coef) + c_block[:, :1]
        right_coef = jnp.where(inner_left, outside_coef, inside_coef) + c_block[:, width - 1:]
        for f in range(freqs):
            for c in range(2):
                own = ref[f, c]
                value = dot_nt(upper, own) + dot_nt(lower, own)
                inside = dot_nt(pick, inner_ref[f, c])[0:2]
                lo = (f * 2 + c) * rows
                beyond = outside[:, lo:lo + rows]
                left = jnp.where(inner_left, inside, beyond)
                right = jnp.where(inner_left, beyond, inside)
                extra = jnp.concatenate(
                    [
                        left[0:1] - left_coef * left[1:2],
                        left[1:2],
                        jnp.zeros((width - 4, rows), F32),
                        right[0:1],
                        right[1:2] - right_coef * right[0:1],
                    ],
                    axis=0,
                )
                o_ref[f, c, n * width:(n + 1) * width] = (value + extra).astype(BF)


def split_body(own_ref, got_ref, keep_ref, *send_refs):
    chips = len(send_refs) + 1
    blocks = lax.axis_size("row")
    probes = own_ref.shape[0] // 2
    block = probes // blocks
    size = block // chips
    chip = lax.div(lax.axis_index("col"), 2)
    me = lax.axis_index("row")
    for step, ref in enumerate((keep_ref,) + send_refs):
        target = xor(chip, step)
        at = 0
        for mate in range(2):
            for slot in range(blocks // 2):
                for c in range(2):
                    lo = c * probes + xor(me, mate ^ cross(slot)) * block + target * size
                    rows = part(lo, size)
                    ref[at:at + size] = (own_ref[rows, :] + got_ref[rows, :].astype(F32)).astype(ref.dtype)
                    at += size


def sum_body(keep_ref, d_ref, fence_ref, *refs):
    stay_ref, give_ref = refs[-2:]
    size = stay_ref.shape[0]
    total = keep_ref[...]
    for ref in refs[:-2]:
        total = total + ref[...].astype(F32)
    stay_ref[...] = total[:size].astype(BF)
    give_ref[:size] = total[size:].astype(BF)
    pad = jnp.zeros((13, d_ref.shape[1]), BF)
    give_ref[size:] = jnp.concatenate(three(d_ref[...]) + [pad], axis=0)


def pack_body(stay_ref, got_ref, fence_ref, o_ref):
    size = stay_ref.shape[0]
    o_ref[:size] = stay_ref[...]
    o_ref[size:] = got_ref[:size]


def join_body(mine_ref, *refs):
    away_ref, stay_ref = refs[-2:]
    pieces = (mine_ref,) + refs[:-2]
    chips = len(pieces)
    blocks = lax.axis_size("row")
    size = mine_ref.shape[0] // (2 * blocks)
    chip = lax.div(lax.axis_index("col"), 2)
    for step, ref in enumerate(pieces):
        source = xor(chip, step)
        for n in range(2 * blocks):
            block, inner = divmod(n, blocks)
            if inner < 2:
                out_ref, lo = stay_ref, block * 2 + inner
            else:
                out_ref, lo = away_ref, block * (blocks - 2) + inner - 2
            out_ref[part(lo * chips * size + source * size, size), :] = ref[n * size:(n + 1) * size]


def predict(freq, a_ref, k_ref, targets, kind):
    half = a_ref.shape[0] // 2
    width = a_ref.shape[1]
    size = half // (2 * len(targets))
    total = []
    for c in range(2):
        value = dot_nn(a_ref[:half], k_ref[freq, c, :width])
        total.append(value + dot_nn(a_ref[half:], k_ref[freq, c, width:]))
    by_real, by_imag = total
    for slot, ref in enumerate(targets):
        lo = 2 * slot * size
        mid = lo + size
        hi = mid + size
        ref[:size] = (by_real[lo:mid] - by_imag[mid:hi]).astype(kind)
        ref[size:] = (by_real[mid:hi] + by_imag[lo:mid]).astype(kind)


def predict_own_body(away_ref, stay_ref, k_ref, keep_ref, *owns):
    predict(parity(), away_ref, k_ref, owns, BF)
    predict(parity(), stay_ref, k_ref, (keep_ref,), F32)


def predict_away_body(peers, away_ref, k_ref, *refs):
    owns, sends = refs[:peers], refs[peers:]
    size = owns[0].shape[0]
    freq = parity()
    for own, send in zip(owns, sends):
        send[part(freq * size, size), :] = own[...]
    rest = part((1 - freq) * size, size)
    predict(1 - freq, away_ref, k_ref, tuple(send.at[rest] for send in sends), BF)


def predict_stay_body(stay_ref, k_ref, keep_ref):
    predict(1 - parity(), stay_ref, k_ref, (keep_ref,), F32)


def final_body(x_ref, noise_ref, own_ref, other_ref, *refs):
    out_ref, s_ref = refs[-2:]
    size = out_ref.shape[0]
    rows = 4 * size
    half = 2 * size
    me = lax.axis_index("row")
    freq = parity()
    for which, keep_ref in enumerate((own_ref, other_ref)):
        f = freq if which == 0 else 1 - freq
        total = keep_ref[...]
        for ref in refs[:-2]:
            total = total + ref[part(f * half, half), :].astype(F32)
        for t in range(s_ref.shape[0]):
            at = slice(t * LANES, (t + 1) * LANES)
            s_ref[t, pl.ds(2 * f, size, stride=4), :] = total[:size, at]
            s_ref[t, pl.ds(2 * f + 1, size, stride=4), :] = total[size:, at]
    x = x_ref[part(me * rows, rows), :].astype(F32)
    kind = lax.rem(lax.broadcasted_iota(jnp.int32, x.shape, 0), 4)
    noise = jnp.where(kind < 2, noise_ref[0:1, :], noise_ref[1:2, :])
    values = jnp.concatenate([s_ref[t] for t in range(s_ref.shape[0])], axis=1) + noise * x
    out_ref[...] = values.reshape(out_ref.shape)


def wide_sum(own, got, coef, blocks):
    rows, width = own.shape
    a = parity()
    value = own + got.astype(F32)
    both = jnp.where(a == 0, jnp.stack([value, 0 * value]), jnp.stack([0 * value, value]))
    both = lax.psum(both, "col").astype(BF).reshape(2, 2, blocks, -1, width)
    slots = jnp.array([cross(slot) for slot in range(blocks // 2)])
    me = lax.axis_index("row")

    def chosen(freq, mate):
        value = lax.dynamic_index_in_dim(both, freq, 0, keepdims=False)
        value = jnp.take(value, xor(me, xor(mate, slots)), axis=1)
        return value.transpose(1, 0, 2, 3).reshape(-1, width)

    tail = jnp.concatenate(three(coef) + [jnp.zeros((13, width), BF)], axis=0)
    give = jnp.concatenate([chosen(0, 1), chosen(1, 1), tail], axis=0)
    give = lax.ppermute(give, "row", pair_perm("row", 1))
    fields = []
    for freq in (a, 1 - a):
        mate = lax.dynamic_slice_in_dim(give, freq * (rows // 2), rows // 2, 0)
        field = jnp.stack([chosen(freq, 0), mate]).reshape(2, blocks // 2, -1, width)
        fields.append((field[:, 1:].reshape(-1, width), field[:, 0].reshape(-1, width)))
    return (*fields, give)


def chip_sum(own, got, coef, blocks, chips):
    rows, width = own.shape
    size = rows // chips
    keep, *sends = call(split_body, (own, got), [((size, width), F32)] + [((size, width), BF)] * (chips - 1))
    fence = call(fence_body, (coef,), [((8, LANES), F32)])[0]
    got = [lax.ppermute(v, "col", pair_perm("col", hop(d + 1))) for d, v in enumerate(sends)]
    stay, give = call(sum_body, (keep, coef, fence, *got), [((size // 2, width), BF), ((size // 2 + 16, width), BF)])
    fence = call(fence_body, (coef,), [((8, LANES), F32)])[0]
    give = lax.ppermute(give, ("row", "col"), mate_perm())
    mine = call(pack_body, (stay, give, fence), [((size, width), BF)])[0]
    got = [lax.ppermute(mine, "col", pair_perm("col", hop(d + 1))) for d in range(chips - 1)]
    stay = 4 * rows // (2 * blocks)
    mine = call(join_body, (mine, *got), [((rows - stay, width), BF), ((stay, width), BF)])
    other = [lax.ppermute(v, "col", pair_perm("col", 1)) for v in mine]
    return mine, other, give


def apply(kernel, probes, noise_var, prior_diag):
    count = probes.shape[0]
    rows, width = kernel.shape[2:]
    blocks = lax.axis_size("row")
    chips = lax.axis_size("col") // 2
    coef = prior_diag[None, :]
    flat = (4 * count, rows)
    scratch = pltpu.VMEM((2 * width // LANES, 4 * count, LANES), F32)
    mate = lax.ppermute(kernel, "row", pair_perm("row", 1))
    other, x, kernel, coef, noise = call(
        adjoint_other_body,
        (),
        [((2 * count, width), BF), (flat, BF), (kernel.shape, BF), (coef.shape, F32), (noise_var.shape, F32)],
        (pltpu.VMEM(probes.shape, BF), scratch, pltpu.SemaphoreType.DMA((5,))),
        raw=(probes, kernel, coef, noise_var),
    )
    got = lax.ppermute(other, "col", pair_perm("col", 1))
    own = call(adjoint_own_body, (x, kernel), [((2 * count, width), F32)], (scratch,))[0]
    seam = call(seam_body, (kernel, coef), [((8, 4 * rows), BF)])[0]
    odd = [i for i in range(blocks) if i % 2]
    even = [i for i in range(blocks) if i % 2 == 0]
    near = [(i, i + 1) for i in odd if i + 1 < blocks] + [(i, i - 1) for i in even if i]
    far = [(i, i + 2 if i + 2 < blocks else 1) for i in odd] + [(i, i - 2 if i else blocks - 2) for i in even]
    near = lax.ppermute(seam, "row", near)
    far = lax.ppermute(seam, "row", far)
    if chips > 4:
        mine, other, give = wide_sum(own, got, coef, blocks)
    else:
        mine, other, give = chip_sum(own, got, coef, blocks, chips)
    operator = call(operator_body, (kernel, mate, coef, give, near, far), [((2, 2, 2 * width, rows), BF)])[0]
    size = count // blocks
    peers = blocks // 2 - 1
    half = (2 * size, rows)
    keep_own, *owns = call(predict_own_body, (*mine, operator), [(half, F32)] + [(half, BF)] * peers)
    sends = call(
        functools.partial(predict_away_body, peers), (other[0], operator, *owns), [((4 * size, rows), BF)] * peers
    )
    got = [lax.ppermute(v, "row", pair_perm("row", cross(d + 1))) for d, v in enumerate(sends)]
    keep_other = call(predict_stay_body, (other[1], operator), [(half, F32)])[0]
    return call(
        final_body,
        (x, noise, keep_own, keep_other, *got),
        [((size,) + probes.shape[1:3] + (rows,), F32)],
        (pltpu.VMEM((rows // LANES, 4 * size, LANES), F32),),
    )[0]


def solution(mesh):
    in_specs = (P(None, None, "col", "row"), P(None, None, None, "col"), P(None, "col"), P("row"))
    out_specs = P("row", None, None, "col")
    return jax.shard_map(apply, mesh=mesh, in_specs=in_specs, out_specs=out_specs, check_vma=False)
```

```python
import functools

import jax
import jax.numpy as jnp
from jax import lax
from jax.experimental import pallas as pl
from jax.experimental.pallas import tpu as pltpu
from jax.sharding import PartitionSpec as P


BF = jnp.bfloat16
F32 = jnp.float32
LANES = 128
LIMIT = 24 * 2**20
VMEM = pl.BlockSpec(memory_space=pltpu.VMEM)
HBM = pl.BlockSpec(memory_space=pltpu.HBM)


def call(body, ins, outs, scratch=(), raw=()):
    return pl.pallas_call(
        body,
        in_specs=[HBM] * len(raw) + [VMEM] * len(ins),
        out_specs=[VMEM] * len(outs),
        out_shape=[pltpu.VMEM(*o) for o in outs],
        scratch_shapes=list(scratch),
        compiler_params=pltpu.CompilerParams(vmem_limit_bytes=LIMIT),
    )(*[pltpu.with_memory_space_constraint(v, pltpu.HBM) for v in raw], *[pltpu.with_memory_space_constraint(v, pltpu.VMEM) for v in ins])


def pair_perm(axis, step):
    return [(i, i ^ step) for i in range(lax.axis_size(axis))]


def parity():
    value = lax.axis_index("col")
    for shift in range(1, lax.axis_size("col").bit_length()):
        value = xor(value, lax.shift_right_logical(lax.axis_index("col"), jnp.int32(shift)))
    return lax.rem(xor(value, lax.axis_index("row")), 2)


def hop(step):
    return 2 * step + step.bit_count() % 2


def mate_perm():
    cols = lax.axis_size("col")
    return [(i * cols + j, (i ^ 1) * cols + (j ^ 1)) for i in range(lax.axis_size("row")) for j in range(cols)]


def xor(a, b):
    return jnp.bitwise_xor(a, b)


def cross(slot):
    return 2 * slot + 1 if slot else 0


def part(start, size):
    return pl.ds(pl.multiple_of(start, size), size)


def dot_nt(left, right):
    return lax.dot_general(left, right, (((1,), (1,)), ((), ())), preferred_element_type=F32)


def dot_nn(left, right):
    return jnp.dot(left, right, preferred_element_type=F32)


def three(value):
    pieces = []
    for _ in range(3):
        pieces.append(value.astype(BF))
        value = value - pieces[-1].astype(F32)
    return pieces


def adjoint(freq, v_ref, k_ref, o_ref, u_ref):
    rows = v_ref.shape[0]
    tiles = u_ref.shape[0] // 2
    x = v_ref[:, freq].reshape(2 * rows, v_ref.shape[3])
    for c in range(2):
        y = dot_nn(x, k_ref[c])
        for t in range(tiles):
            u_ref[c * tiles + t] = y[:, t * LANES:(t + 1) * LANES]
    real = pl.ds(0, rows, stride=2)
    imag = pl.ds(1, rows, stride=2)
    for t in range(tiles):
        at = slice(t * LANES, (t + 1) * LANES)
        o_ref[:rows, at] = (u_ref[t, real, :] + u_ref[tiles + t, imag, :]).astype(o_ref.dtype)
        o_ref[rows:, at] = (u_ref[t, imag, :] - u_ref[tiles + t, real, :]).astype(o_ref.dtype)


def adjoint_other_body(v_hbm, k_hbm, d_hbm, n_hbm, o_ref, v_ref, mine_ref, other_ref, d_ref, n_ref, u_ref, sems):
    freq = 1 - parity()
    pairs = (
        (v_hbm, v_ref),
        (k_hbm.at[freq], other_ref),
        (k_hbm.at[1 - freq], mine_ref),
        (d_hbm, d_ref),
        (n_hbm, n_ref),
    )
    copies = [pltpu.make_async_copy(*pair, sems.at[n]) for n, pair in enumerate(pairs)]
    for copy in copies:
        copy.start()
    copies[0].wait()
    copies[1].wait()
    adjoint(freq, v_ref, other_ref, o_ref, u_ref)
    for copy in copies[2:]:
        copy.wait()


def adjoint_own_body(v_ref, k_ref, o_ref, u_ref):
    adjoint(parity(), v_ref, k_ref, o_ref, u_ref)


def lanes_of(freq, c, rows):
    return part((freq * 2 + c) * rows, rows)


def seam_body(mine_ref, other_ref, d_ref, o_ref):
    _, rows, width = mine_ref.shape
    odd = lax.rem(lax.axis_index("row"), 2)
    at = lax.broadcasted_iota(jnp.int32, (8, width), 0)
    place = lax.broadcasted_iota(jnp.int32, (8, width), 1)
    pick = jnp.where((at < 2) & (place == at + odd * (width - 2)), 1.0, 0.0).astype(BF)
    coef = d_ref[...]
    spot = lax.broadcasted_iota(jnp.int32, coef.shape, 1)
    edge = jnp.sum(jnp.where(spot == odd * (width - 1), coef, 0.0), axis=1, keepdims=True)
    lines = [jnp.zeros((2, rows), F32)]
    lines += [jnp.broadcast_to(piece.astype(F32), (1, rows)) for piece in three(edge)]
    lines = jnp.concatenate(lines + [jnp.zeros((3, rows), F32)], axis=0)
    for freq, ref in ((parity(), mine_ref), (1 - parity(), other_ref)):
        for c in range(2):
            o_ref[:, lanes_of(freq, c, rows)] = (dot_nt(pick, ref[c]) + lines).astype(BF)


def fence_body(d_ref, o_ref):
    o_ref[...] = jnp.zeros_like(o_ref)


def stencil_matrix(coef, block):
    width = coef.shape[1]
    row_at = lax.broadcasted_iota(jnp.int32, (width, width), 0)
    col_at = lax.broadcasted_iota(jnp.int32, (width, width), 1)
    wide = jnp.broadcast_to(coef, (width, width))
    tall = jnp.sum(jnp.where(row_at == col_at, wide, 0.0), axis=1, keepdims=True)
    gap = jnp.abs(row_at - col_at)
    first = (row_at == 0) & (block == 0)
    last = (row_at == width - 1) & (block == lax.axis_size("row") - 1)
    centre = wide * wide + jnp.where(first | last, 1.0, 2.0)
    matrix = jnp.where(gap == 0, centre, jnp.where(gap == 1, -(wide + tall), jnp.where(gap == 2, 1.0, 0.0)))
    upper = matrix.astype(BF)
    return upper, (matrix - upper.astype(F32)).astype(BF)


def operator_body(swap, k_ref, mate_ref, d_ref, got_ref, near_ref, far_ref, o_ref):
    _, rows, width = k_ref.shape
    freq = 1 - parity() if swap else parity()
    me = lax.axis_index("row")
    odd = lax.rem(me, 2)
    is_odd = odd == 1
    at = lax.broadcasted_iota(jnp.int32, (8, width), 0)
    place = lax.broadcasted_iota(jnp.int32, (8, width), 1)
    own_pick = jnp.where((at < 2) & (place == at + (1 - odd) * (width - 2)), 1.0, 0.0).astype(BF)
    mate_pick = jnp.where((at < 2) & (place == at + odd * (width - 2)), 1.0, 0.0).astype(BF)
    coef = d_ref[...]
    tail = got_ref[got_ref.shape[0] - 16:, :].astype(F32)
    mate_coef = tail[0:1] + tail[1:2] + tail[2:3]

    def last_or_first(value, last):
        return jnp.where(last, value[:, width - 1:], value[:, :1])

    def outer(ref, block, c):
        last = lax.axis_size("row") - 1
        there = jnp.where(lax.rem(block, 2) == 1, block < last, block > 0)
        full = jnp.where(there, ref[:, lanes_of(freq, c, rows)].astype(F32), 0.0)
        return full[0:2], full[2:3, :1] + full[3:4, :1] + full[4:5, :1]

    sides = (
        (k_ref, coef, me, near_ref, mate_ref, mate_pick, last_or_first(mate_coef, is_odd), is_odd),
        (mate_ref, mate_coef, xor(me, 1), far_ref, k_ref, own_pick, last_or_first(coef, ~is_odd), ~is_odd),
    )
    for n, (ref, c_block, block, outer_ref, inner_ref, pick, inside_coef, inner_left) in enumerate(sides):
        upper, lower = stencil_matrix(c_block, block)
        for c in range(2):
            beyond, outside_coef = outer(outer_ref, block, c)
            left_coef = jnp.where(inner_left, inside_coef, outside_coef) + c_block[:, :1]
            right_coef = jnp.where(inner_left, outside_coef, inside_coef) + c_block[:, width - 1:]
            own = ref[c]
            value = dot_nt(upper, own) + dot_nt(lower, own)
            inside = dot_nt(pick, inner_ref[c])[0:2]
            left = jnp.where(inner_left, inside, beyond)
            right = jnp.where(inner_left, beyond, inside)
            extra = jnp.concatenate(
                [
                    left[0:1] - left_coef * left[1:2],
                    left[1:2],
                    jnp.zeros((width - 4, rows), F32),
                    right[0:1],
                    right[1:2] - right_coef * right[0:1],
                ],
                axis=0,
            )
            o_ref[c, n * width:(n + 1) * width] = (value + extra).astype(BF)


def split_body(own_ref, got_ref, keep_ref, *send_refs):
    chips = len(send_refs) + 1
    blocks = lax.axis_size("row")
    probes = own_ref.shape[0] // 2
    block = probes // blocks
    size = block // chips
    chip = lax.div(lax.axis_index("col"), 2)
    me = lax.axis_index("row")
    for step, ref in enumerate((keep_ref,) + send_refs):
        target = xor(chip, step)
        at = 0
        for mate in range(2):
            for slot in range(blocks // 2):
                for c in range(2):
                    lo = c * probes + xor(me, mate ^ cross(slot)) * block + target * size
                    rows = part(lo, size)
                    ref[at:at + size] = (own_ref[rows, :] + got_ref[rows, :].astype(F32)).astype(ref.dtype)
                    at += size


def sum_body(keep_ref, d_ref, fence_ref, *refs):
    stay_ref, give_ref = refs[-2:]
    size = stay_ref.shape[0]
    total = keep_ref[...]
    for ref in refs[:-2]:
        total = total + ref[...].astype(F32)
    stay_ref[...] = total[:size].astype(BF)
    give_ref[:size] = total[size:].astype(BF)
    pad = jnp.zeros((13, d_ref.shape[1]), BF)
    give_ref[size:] = jnp.concatenate(three(d_ref[...]) + [pad], axis=0)


def pack_body(stay_ref, got_ref, fence_ref, o_ref):
    size = stay_ref.shape[0]
    o_ref[:size] = stay_ref[...]
    o_ref[size:] = got_ref[:size]


def join_body(mine_ref, *refs):
    away_ref, stay_ref = refs[-2:]
    pieces = (mine_ref,) + refs[:-2]
    chips = len(pieces)
    blocks = lax.axis_size("row")
    size = mine_ref.shape[0] // (2 * blocks)
    chip = lax.div(lax.axis_index("col"), 2)
    for step, ref in enumerate(pieces):
        source = xor(chip, step)
        for n in range(2 * blocks):
            block, inner = divmod(n, blocks)
            if inner < 2:
                out_ref, lo = stay_ref, block * 2 + inner
            else:
                out_ref, lo = away_ref, block * (blocks - 2) + inner - 2
            out_ref[part(lo * chips * size + source * size, size), :] = ref[n * size:(n + 1) * size]


def predict(a_ref, k_ref, targets, kind):
    half = a_ref.shape[0] // 2
    width = a_ref.shape[1]
    size = half // (2 * len(targets))
    total = []
    for c in range(2):
        value = dot_nn(a_ref[:half], k_ref[c, :width])
        total.append(value + dot_nn(a_ref[half:], k_ref[c, width:]))
    by_real, by_imag = total
    for slot, ref in enumerate(targets):
        lo = 2 * slot * size
        mid = lo + size
        hi = mid + size
        ref[:size] = (by_real[lo:mid] - by_imag[mid:hi]).astype(kind)
        ref[size:] = (by_real[mid:hi] + by_imag[lo:mid]).astype(kind)


def predict_own_body(away_ref, stay_ref, k_ref, keep_ref, *owns):
    predict(away_ref, k_ref, owns, BF)
    predict(stay_ref, k_ref, (keep_ref,), F32)


def predict_away_body(peers, away_ref, k_ref, *refs):
    owns, sends = refs[:peers], refs[peers:]
    size = owns[0].shape[0]
    freq = parity()
    for own, send in zip(owns, sends):
        send[part(freq * size, size), :] = own[...]
    rest = part((1 - freq) * size, size)
    predict(away_ref, k_ref, tuple(send.at[rest] for send in sends), BF)


def predict_stay_body(stay_ref, k_ref, keep_ref):
    predict(stay_ref, k_ref, (keep_ref,), F32)


def final_body(v_ref, noise_ref, own_ref, other_ref, *refs):
    out_ref, s_ref = refs[-2:]
    size = out_ref.shape[0]
    rows = 4 * size
    half = 2 * size
    me = lax.axis_index("row")
    freq = parity()
    for which, keep_ref in enumerate((own_ref, other_ref)):
        f = freq if which == 0 else 1 - freq
        total = keep_ref[...]
        for ref in refs[:-2]:
            total = total + ref[part(f * half, half), :].astype(F32)
        for t in range(s_ref.shape[0]):
            at = slice(t * LANES, (t + 1) * LANES)
            s_ref[t, pl.ds(2 * f, size, stride=4), :] = total[:size, at]
            s_ref[t, pl.ds(2 * f + 1, size, stride=4), :] = total[size:, at]
    x = v_ref[part(me * size, size)].reshape(rows, v_ref.shape[3]).astype(F32)
    kind = lax.rem(lax.broadcasted_iota(jnp.int32, x.shape, 0), 4)
    noise = jnp.where(kind < 2, noise_ref[0:1, :], noise_ref[1:2, :])
    values = jnp.concatenate([s_ref[t] for t in range(s_ref.shape[0])], axis=1) + noise * x
    out_ref[...] = values.reshape(out_ref.shape)


def wide_sum(own, got, coef, blocks):
    rows, width = own.shape
    a = parity()
    value = own + got.astype(F32)
    both = jnp.where(a == 0, jnp.stack([value, 0 * value]), jnp.stack([0 * value, value]))
    both = lax.psum(both, "col").astype(BF).reshape(2, 2, blocks, -1, width)
    slots = jnp.array([cross(slot) for slot in range(blocks // 2)])
    me = lax.axis_index("row")

    def chosen(freq, mate):
        value = lax.dynamic_index_in_dim(both, freq, 0, keepdims=False)
        value = jnp.take(value, xor(me, xor(mate, slots)), axis=1)
        return value.transpose(1, 0, 2, 3).reshape(-1, width)

    tail = jnp.concatenate(three(coef) + [jnp.zeros((13, width), BF)], axis=0)
    give = jnp.concatenate([chosen(0, 1), chosen(1, 1), tail], axis=0)
    give = lax.ppermute(give, "row", pair_perm("row", 1))
    fields = []
    for freq in (a, 1 - a):
        mate = lax.dynamic_slice_in_dim(give, freq * (rows // 2), rows // 2, 0)
        field = jnp.stack([chosen(freq, 0), mate]).reshape(2, blocks // 2, -1, width)
        fields.append((field[:, 1:].reshape(-1, width), field[:, 0].reshape(-1, width)))
    return (*fields, give)


def chip_sum(own, got, coef, blocks, chips):
    rows, width = own.shape
    size = rows // chips
    keep, *sends = call(split_body, (own, got), [((size, width), F32)] + [((size, width), BF)] * (chips - 1))
    fence = call(fence_body, (coef,), [((8, LANES), F32)])[0]
    got = [lax.ppermute(v, "col", pair_perm("col", hop(d + 1))) for d, v in enumerate(sends)]
    stay, give = call(sum_body, (keep, coef, fence, *got), [((size // 2, width), BF), ((size // 2 + 16, width), BF)])
    fence = call(fence_body, (coef,), [((8, LANES), F32)])[0]
    give = lax.ppermute(give, ("row", "col"), mate_perm())
    mine = call(pack_body, (stay, give, fence), [((size, width), BF)])[0]
    got = [lax.ppermute(mine, "col", pair_perm("col", hop(d + 1))) for d in range(chips - 1)]
    stay = 4 * rows // (2 * blocks)
    mine = call(join_body, (mine, *got), [((rows - stay, width), BF), ((stay, width), BF)])
    other = [lax.ppermute(v, "col", pair_perm("col", 1)) for v in mine]
    return mine, other, give


def apply(kernel, probes, noise_var, prior_diag):
    count = probes.shape[0]
    rows, width = kernel.shape[2:]
    blocks = lax.axis_size("row")
    chips = lax.axis_size("col") // 2
    coef = prior_diag[None, :]
    scratch = pltpu.VMEM((2 * width // LANES, 2 * count, LANES), F32)
    block = kernel.shape[1:]
    other, probes, k_own, k_other, coef, noise = call(
        adjoint_other_body,
        (),
        [
            ((2 * count, width), BF),
            (probes.shape, BF),
            (block, BF),
            (block, BF),
            (coef.shape, F32),
            (noise_var.shape, F32),
        ],
        (scratch, pltpu.SemaphoreType.DMA((5,))),
        raw=(probes, kernel, coef, noise_var),
    )
    got = lax.ppermute(other, "col", pair_perm("col", 1))
    mate_own = lax.ppermute(k_other, "row", pair_perm("row", 1))
    mate_other = lax.ppermute(k_own, "row", pair_perm("row", 1))
    own = call(adjoint_own_body, (probes, k_own), [((2 * count, width), F32)], (scratch,))[0]
    seam = call(seam_body, (k_own, k_other, coef), [((8, 4 * rows), BF)])[0]
    odd = [i for i in range(blocks) if i % 2]
    even = [i for i in range(blocks) if i % 2 == 0]
    near = [(i, i + 1) for i in odd if i + 1 < blocks] + [(i, i - 1) for i in even if i]
    far = [(i, i + 2 if i + 2 < blocks else 1) for i in odd] + [(i, i - 2 if i else blocks - 2) for i in even]
    near = lax.ppermute(seam, "row", near)
    far = lax.ppermute(seam, "row", far)
    if chips > 4:
        mine, other, give = wide_sum(own, got, coef, blocks)
    else:
        mine, other, give = chip_sum(own, got, coef, blocks, chips)
    operators = [
        call(
            functools.partial(operator_body, swap), (block_k, mate, coef, give, near, far), [((2, 2 * width, rows), BF)]
        )[0]
        for swap, block_k, mate in ((False, k_own, mate_own), (True, k_other, mate_other))
    ]
    size = count // blocks
    peers = blocks // 2 - 1
    half = (2 * size, rows)
    keep_own, *owns = call(predict_own_body, (*mine, operators[0]), [(half, F32)] + [(half, BF)] * peers)
    sends = call(
        functools.partial(predict_away_body, peers), (other[0], operators[1], *owns), [((4 * size, rows), BF)] * peers
    )
    got = [lax.ppermute(v, "row", pair_perm("row", cross(d + 1))) for d, v in enumerate(sends)]
    keep_other = call(predict_stay_body, (other[1], operators[1]), [(half, F32)])[0]
    return call(
        final_body,
        (probes, noise, keep_own, keep_other, *got),
        [((size,) + probes.shape[1:3] + (rows,), F32)],
        (pltpu.VMEM((rows // LANES, 4 * size, LANES), F32),),
    )[0]


def solution(mesh):
    in_specs = (P(None, None, "col", "row"), P(None, None, None, "col"), P(None, "col"), P("row"))
    out_specs = P("row", None, None, "col")
    return jax.shard_map(apply, mesh=mesh, in_specs=in_specs, out_specs=out_specs, check_vma=False)
```

```python
import functools

import jax
import jax.numpy as jnp
from jax import lax
from jax.experimental import pallas as pl
from jax.experimental.pallas import tpu as pltpu
from jax.sharding import PartitionSpec as P


BF = jnp.bfloat16
F32 = jnp.float32
LANES = 128
LIMIT = 24 * 2**20
VMEM = pl.BlockSpec(memory_space=pltpu.VMEM)
HBM = pl.BlockSpec(memory_space=pltpu.HBM)


def call(body, ins, outs, scratch=(), raw=()):
    return pl.pallas_call(
        body,
        in_specs=[HBM] * len(raw) + [VMEM] * len(ins),
        out_specs=[VMEM] * len(outs),
        out_shape=[pltpu.VMEM(*o) for o in outs],
        scratch_shapes=list(scratch),
        compiler_params=pltpu.CompilerParams(vmem_limit_bytes=LIMIT),
    )(*[pltpu.with_memory_space_constraint(v, pltpu.HBM) for v in raw], *[pltpu.with_memory_space_constraint(v, pltpu.VMEM) for v in ins])


def pair_perm(axis, step):
    return [(i, i ^ step) for i in range(lax.axis_size(axis))]


def parity():
    value = lax.axis_index("col")
    for shift in range(1, lax.axis_size("col").bit_length()):
        value = xor(value, lax.shift_right_logical(lax.axis_index("col"), jnp.int32(shift)))
    return lax.rem(xor(value, lax.axis_index("row")), 2)


def hop(step):
    return 2 * step + step.bit_count() % 2


def mate_perm():
    cols = lax.axis_size("col")
    return [(i * cols + j, (i ^ 1) * cols + (j ^ 1)) for i in range(lax.axis_size("row")) for j in range(cols)]


def xor(a, b):
    return jnp.bitwise_xor(a, b)


def cross(slot):
    return 2 * slot + 1 if slot else 0


def part(start, size):
    return pl.ds(pl.multiple_of(start, size), size)


def dot_nt(left, right):
    return lax.dot_general(left, right, (((1,), (1,)), ((), ())), preferred_element_type=F32)


def dot_nn(left, right):
    return jnp.dot(left, right, preferred_element_type=F32)


def three(value):
    pieces = []
    for _ in range(3):
        pieces.append(value.astype(BF))
        value = value - pieces[-1].astype(F32)
    return pieces


def adjoint(freq, v_ref, k_ref, o_ref, u_ref):
    rows = v_ref.shape[0]
    tiles = u_ref.shape[0] // 2
    x = v_ref[:, freq].reshape(2 * rows, v_ref.shape[3])
    for c in range(2):
        y = dot_nn(x, k_ref[c])
        for t in range(tiles):
            u_ref[c * tiles + t] = y[:, t * LANES:(t + 1) * LANES]
    real = pl.ds(0, rows, stride=2)
    imag = pl.ds(1, rows, stride=2)
    for t in range(tiles):
        at = slice(t * LANES, (t + 1) * LANES)
        o_ref[:rows, at] = (u_ref[t, real, :] + u_ref[tiles + t, imag, :]).astype(o_ref.dtype)
        o_ref[rows:, at] = (u_ref[t, imag, :] - u_ref[tiles + t, real, :]).astype(o_ref.dtype)


def adjoint_other_body(v_hbm, k_hbm, d_hbm, n_hbm, o_ref, v_ref, mine_ref, other_ref, d_ref, n_ref, u_ref, sems):
    freq = 1 - parity()
    pairs = (
        (v_hbm, v_ref),
        (k_hbm.at[freq], other_ref),
        (k_hbm.at[1 - freq], mine_ref),
        (d_hbm, d_ref),
        (n_hbm, n_ref),
    )
    copies = [pltpu.make_async_copy(*pair, sems.at[n]) for n, pair in enumerate(pairs)]
    for copy in copies:
        copy.start()
    copies[0].wait()
    copies[1].wait()
    adjoint(freq, v_ref, other_ref, o_ref, u_ref)
    for copy in copies[2:]:
        copy.wait()


def adjoint_own_body(v_ref, k_ref, o_ref, u_ref):
    adjoint(parity(), v_ref, k_ref, o_ref, u_ref)


def lanes_of(freq, c, rows):
    return part((freq * 2 + c) * rows, rows)


def seam_body(mine_ref, other_ref, d_ref, o_ref):
    _, rows, width = mine_ref.shape
    odd = lax.rem(lax.axis_index("row"), 2)
    at = lax.broadcasted_iota(jnp.int32, (8, width), 0)
    place = lax.broadcasted_iota(jnp.int32, (8, width), 1)
    pick = jnp.where((at < 2) & (place == at + odd * (width - 2)), 1.0, 0.0).astype(BF)
    coef = d_ref[...]
    spot = lax.broadcasted_iota(jnp.int32, coef.shape, 1)
    edge = jnp.sum(jnp.where(spot == odd * (width - 1), coef, 0.0), axis=1, keepdims=True)
    lines = [jnp.zeros((2, rows), F32)]
    lines += [jnp.broadcast_to(piece.astype(F32), (1, rows)) for piece in three(edge)]
    lines = jnp.concatenate(lines + [jnp.zeros((3, rows), F32)], axis=0)
    for freq, ref in ((parity(), mine_ref), (1 - parity(), other_ref)):
        for c in range(2):
            o_ref[:, lanes_of(freq, c, rows)] = (dot_nt(pick, ref[c]) + lines).astype(BF)


def fence_body(d_ref, o_ref):
    o_ref[...] = jnp.zeros_like(o_ref)


def stencil_matrix(coef, block):
    width = coef.shape[1]
    row_at = lax.broadcasted_iota(jnp.int32, (width, width), 0)
    col_at = lax.broadcasted_iota(jnp.int32, (width, width), 1)
    wide = jnp.broadcast_to(coef, (width, width))
    tall = jnp.sum(jnp.where(row_at == col_at, wide, 0.0), axis=1, keepdims=True)
    gap = jnp.abs(row_at - col_at)
    first = (row_at == 0) & (block == 0)
    last = (row_at == width - 1) & (block == lax.axis_size("row") - 1)
    centre = wide * wide + jnp.where(first | last, 1.0, 2.0)
    matrix = jnp.where(gap == 0, centre, jnp.where(gap == 1, -(wide + tall), jnp.where(gap == 2, 1.0, 0.0)))
    upper = matrix.astype(BF)
    return upper, (matrix - upper.astype(F32)).astype(BF)


def operator_body(swap, k_ref, mate_ref, d_ref, got_ref, near_ref, far_ref, o_ref):
    _, rows, width = k_ref.shape
    freq = 1 - parity() if swap else parity()
    me = lax.axis_index("row")
    odd = lax.rem(me, 2)
    is_odd = odd == 1
    at = lax.broadcasted_iota(jnp.int32, (8, width), 0)
    place = lax.broadcasted_iota(jnp.int32, (8, width), 1)
    own_pick = jnp.where((at < 2) & (place == at + (1 - odd) * (width - 2)), 1.0, 0.0).astype(BF)
    mate_pick = jnp.where((at < 2) & (place == at + odd * (width - 2)), 1.0, 0.0).astype(BF)
    coef = d_ref[...]
    tail = got_ref[got_ref.shape[0] - 16:, :].astype(F32)
    mate_coef = tail[0:1] + tail[1:2] + tail[2:3]

    def last_or_first(value, last):
        return jnp.where(last, value[:, width - 1:], value[:, :1])

    def outer(ref, block, c):
        last = lax.axis_size("row") - 1
        there = jnp.where(lax.rem(block, 2) == 1, block < last, block > 0)
        full = jnp.where(there, ref[:, lanes_of(freq, c, rows)].astype(F32), 0.0)
        return full[0:2], full[2:3, :1] + full[3:4, :1] + full[4:5, :1]

    sides = (
        (k_ref, coef, me, near_ref, mate_ref, mate_pick, last_or_first(mate_coef, is_odd), is_odd),
        (mate_ref, mate_coef, xor(me, 1), far_ref, k_ref, own_pick, last_or_first(coef, ~is_odd), ~is_odd),
    )
    for n, (ref, c_block, block, outer_ref, inner_ref, pick, inside_coef, inner_left) in enumerate(sides):
        upper, lower = stencil_matrix(c_block, block)
        for c in range(2):
            beyond, outside_coef = outer(outer_ref, block, c)
            left_coef = jnp.where(inner_left, inside_coef, outside_coef) + c_block[:, :1]
            right_coef = jnp.where(inner_left, outside_coef, inside_coef) + c_block[:, width - 1:]
            own = ref[c]
            value = dot_nt(upper, own) + dot_nt(lower, own)
            inside = dot_nt(pick, inner_ref[c])[0:2]
            left = jnp.where(inner_left, inside, beyond)
            right = jnp.where(inner_left, beyond, inside)
            extra = jnp.concatenate(
                [
                    left[0:1] - left_coef * left[1:2],
                    left[1:2],
                    jnp.zeros((width - 4, rows), F32),
                    right[0:1],
                    right[1:2] - right_coef * right[0:1],
                ],
                axis=0,
            )
            o_ref[c, n * width:(n + 1) * width] = (value + extra).astype(BF)


def split_body(own_ref, got_ref, keep_ref, *send_refs):
    chips = len(send_refs) + 1
    blocks = lax.axis_size("row")
    probes = own_ref.shape[0] // 2
    block = probes // blocks
    size = block // chips
    chip = lax.div(lax.axis_index("col"), 2)
    me = lax.axis_index("row")
    for step, ref in enumerate((keep_ref,) + send_refs):
        target = xor(chip, step)
        at = 0
        for mate in range(2):
            for slot in range(blocks // 2):
                for c in range(2):
                    lo = c * probes + xor(me, mate ^ cross(slot)) * block + target * size
                    rows = part(lo, size)
                    ref[at:at + size] = (own_ref[rows, :] + got_ref[rows, :].astype(F32)).astype(ref.dtype)
                    at += size


def sum_body(keep_ref, d_ref, fence_ref, *refs):
    stay_ref, give_ref = refs[-2:]
    size = stay_ref.shape[0]
    total = keep_ref[...]
    for ref in refs[:-2]:
        total = total + ref[...].astype(F32)
    stay_ref[...] = total[:size].astype(BF)
    give_ref[:size] = total[size:].astype(BF)
    pad = jnp.zeros((13, d_ref.shape[1]), BF)
    give_ref[size:] = jnp.concatenate(three(d_ref[...]) + [pad], axis=0)


def pack_body(stay_ref, got_ref, fence_ref, o_ref):
    size = stay_ref.shape[0]
    o_ref[:size] = stay_ref[...]
    o_ref[size:] = got_ref[:size]


def join_body(mine_ref, *refs):
    away_ref, stay_ref = refs[-2:]
    pieces = (mine_ref,) + refs[:-2]
    chips = len(pieces)
    blocks = lax.axis_size("row")
    size = mine_ref.shape[0] // (2 * blocks)
    chip = lax.div(lax.axis_index("col"), 2)
    for step, ref in enumerate(pieces):
        source = xor(chip, step)
        for n in range(2 * blocks):
            block, inner = divmod(n, blocks)
            if inner < 2:
                out_ref, lo = stay_ref, block * 2 + inner
            else:
                out_ref, lo = away_ref, block * (blocks - 2) + inner - 2
            out_ref[part(lo * chips * size + source * size, size), :] = ref[n * size:(n + 1) * size]


def predict(a_ref, k_ref, targets, kind):
    half = a_ref.shape[0] // 2
    width = a_ref.shape[1]
    size = half // (2 * len(targets))
    total = []
    for c in range(2):
        value = dot_nn(a_ref[:half], k_ref[c, :width])
        total.append(value + dot_nn(a_ref[half:], k_ref[c, width:]))
    by_real, by_imag = total
    for slot, ref in enumerate(targets):
        lo = 2 * slot * size
        mid = lo + size
        hi = mid + size
        ref[:size] = (by_real[lo:mid] - by_imag[mid:hi]).astype(kind)
        ref[size:] = (by_real[mid:hi] + by_imag[lo:mid]).astype(kind)


def predict_own_body(away_ref, stay_ref, k_ref, keep_ref, *owns):
    predict(away_ref, k_ref, owns, BF)
    predict(stay_ref, k_ref, (keep_ref,), F32)


def predict_away_body(peers, away_ref, k_ref, *refs):
    owns, sends = refs[:peers], refs[peers:]
    size = owns[0].shape[0]
    freq = parity()
    for own, send in zip(owns, sends):
        send[part(freq * size, size), :] = own[...]
    rest = part((1 - freq) * size, size)
    predict(away_ref, k_ref, tuple(send.at[rest] for send in sends), BF)


def predict_stay_body(stay_ref, k_ref, keep_ref):
    predict(stay_ref, k_ref, (keep_ref,), F32)


def final_body(v_ref, noise_ref, own_ref, other_ref, *refs):
    out_ref, s_ref = refs[-2:]
    size = out_ref.shape[0]
    rows = 4 * size
    half = 2 * size
    me = lax.axis_index("row")
    freq = parity()
    for which, keep_ref in enumerate((own_ref, other_ref)):
        f = freq if which == 0 else 1 - freq
        total = keep_ref[...]
        for ref in refs[:-2]:
            total = total + ref[part(f * half, half), :].astype(F32)
        for t in range(s_ref.shape[0]):
            at = slice(t * LANES, (t + 1) * LANES)
            s_ref[t, pl.ds(2 * f, size, stride=4), :] = total[:size, at]
            s_ref[t, pl.ds(2 * f + 1, size, stride=4), :] = total[size:, at]
    x = v_ref[part(me * size, size)].reshape(rows, v_ref.shape[3]).astype(F32)
    kind = lax.rem(lax.broadcasted_iota(jnp.int32, x.shape, 0), 4)
    noise = jnp.where(kind < 2, noise_ref[0:1, :], noise_ref[1:2, :])
    values = jnp.concatenate([s_ref[t] for t in range(s_ref.shape[0])], axis=1) + noise * x
    out_ref[...] = values.reshape(out_ref.shape)


def wide_sum(own, got, coef, blocks):
    rows, width = own.shape
    a = parity()
    value = own + got.astype(F32)
    both = jnp.where(a == 0, jnp.stack([value, 0 * value]), jnp.stack([0 * value, value]))
    both = lax.psum(both, "col").astype(BF).reshape(2, 2, blocks, -1, width)
    slots = jnp.array([cross(slot) for slot in range(blocks // 2)])
    me = lax.axis_index("row")

    def chosen(freq, mate):
        value = lax.dynamic_index_in_dim(both, freq, 0, keepdims=False)
        value = jnp.take(value, xor(me, xor(mate, slots)), axis=1)
        return value.transpose(1, 0, 2, 3).reshape(-1, width)

    tail = jnp.concatenate(three(coef) + [jnp.zeros((13, width), BF)], axis=0)
    give = jnp.concatenate([chosen(0, 1), chosen(1, 1), tail], axis=0)
    give = lax.ppermute(give, "row", pair_perm("row", 1))
    fields = []
    for freq in (a, 1 - a):
        mate = lax.dynamic_slice_in_dim(give, freq * (rows // 2), rows // 2, 0)
        field = jnp.stack([chosen(freq, 0), mate]).reshape(2, blocks // 2, -1, width)
        fields.append((field[:, 1:].reshape(-1, width), field[:, 0].reshape(-1, width)))
    return (*fields, give)


def chip_sum(own, got, coef, blocks, chips):
    rows, width = own.shape
    size = rows // chips
    keep, *sends = call(split_body, (own, got), [((size, width), F32)] + [((size, width), BF)] * (chips - 1))
    fence = call(fence_body, (coef,), [((8, LANES), F32)])[0]
    got = [lax.ppermute(v, "col", pair_perm("col", hop(d + 1))) for d, v in enumerate(sends)]
    stay, give = call(sum_body, (keep, coef, fence, *got), [((size // 2, width), BF), ((size // 2 + 16, width), BF)])
    fence = call(fence_body, (coef,), [((8, LANES), F32)])[0]
    give = lax.ppermute(give, ("row", "col"), mate_perm())
    mine = call(pack_body, (stay, give, fence), [((size, width), BF)])[0]
    got = [lax.ppermute(mine, "col", pair_perm("col", hop(d + 1))) for d in range(chips - 1)]
    stay = 4 * rows // (2 * blocks)
    mine = call(join_body, (mine, *got), [((rows - stay, width), BF), ((stay, width), BF)])
    other = [lax.ppermute(v, "col", pair_perm("col", 1)) for v in mine]
    return mine, other, give


def apply(kernel, probes, noise_var, prior_diag):
    count = probes.shape[0]
    rows, width = kernel.shape[2:]
    blocks = lax.axis_size("row")
    chips = lax.axis_size("col") // 2
    coef = prior_diag[None, :]
    scratch = pltpu.VMEM((2 * width // LANES, 2 * count, LANES), F32)
    block = kernel.shape[1:]
    other, probes, k_own, k_other, coef, noise = call(
        adjoint_other_body,
        (),
        [
            ((2 * count, width), BF),
            (probes.shape, BF),
            (block, BF),
            (block, BF),
            (coef.shape, F32),
            (noise_var.shape, F32),
        ],
        (scratch, pltpu.SemaphoreType.DMA((5,))),
        raw=(probes, kernel, coef, noise_var),
    )
    got = lax.ppermute(other, "col", pair_perm("col", 1))
    mate_own = lax.ppermute(k_other, "row", pair_perm("row", 1))
    mate_other = lax.ppermute(k_own, "row", pair_perm("row", 1))
    own = call(adjoint_own_body, (probes, k_own), [((2 * count, width), F32)], (scratch,))[0]
    seam = call(seam_body, (k_own, k_other, coef), [((8, 4 * rows), BF)])[0]
    odd = [i for i in range(blocks) if i % 2]
    even = [i for i in range(blocks) if i % 2 == 0]
    near = [(i, (i + 1) % blocks) for i in odd] + [(i, (i - 1) % blocks) for i in even]
    near = lax.ppermute(seam, "row", near)
    far = lax.ppermute(near, "row", pair_perm("row", 1))
    if chips > 4:
        mine, other, give = wide_sum(own, got, coef, blocks)
    else:
        mine, other, give = chip_sum(own, got, coef, blocks, chips)
    operators = [
        call(
            functools.partial(operator_body, swap), (block_k, mate, coef, give, near, far), [((2, 2 * width, rows), BF)]
        )[0]
        for swap, block_k, mate in ((False, k_own, mate_own), (True, k_other, mate_other))
    ]
    size = count // blocks
    peers = blocks // 2 - 1
    half = (2 * size, rows)
    keep_own, *owns = call(predict_own_body, (*mine, operators[0]), [(half, F32)] + [(half, BF)] * peers)
    sends = call(
        functools.partial(predict_away_body, peers), (other[0], operators[1], *owns), [((4 * size, rows), BF)] * peers
    )
    got = [lax.ppermute(v, "row", pair_perm("row", cross(d + 1))) for d, v in enumerate(sends)]
    keep_other = call(predict_stay_body, (other[1], operators[1]), [(half, F32)])[0]
    return call(
        final_body,
        (probes, noise, keep_own, keep_other, *got),
        [((size,) + probes.shape[1:3] + (rows,), F32)],
        (pltpu.VMEM((rows // LANES, 4 * size, LANES), F32),),
    )[0]


def solution(mesh):
    in_specs = (P(None, None, "col", "row"), P(None, None, None, "col"), P(None, "col"), P("row"))
    out_specs = P("row", None, None, "col")
    return jax.shard_map(apply, mesh=mesh, in_specs=in_specs, out_specs=out_specs, check_vma=False)
```

```python
import functools

import jax
import jax.numpy as jnp
from jax import lax
from jax.experimental import pallas as pl
from jax.experimental.pallas import tpu as pltpu
from jax.sharding import PartitionSpec as P


BF = jnp.bfloat16
F32 = jnp.float32
LANES = 128
PIECES = 2
LIMIT = 24 * 2**20
VMEM = pl.BlockSpec(memory_space=pltpu.VMEM)
HBM = pl.BlockSpec(memory_space=pltpu.HBM)


def call(body, ins, outs, scratch=(), raw=()):
    return pl.pallas_call(
        body,
        in_specs=[HBM] * len(raw) + [VMEM] * len(ins),
        out_specs=[VMEM] * len(outs),
        out_shape=[pltpu.VMEM(*o) for o in outs],
        scratch_shapes=list(scratch),
        compiler_params=pltpu.CompilerParams(vmem_limit_bytes=LIMIT),
    )(*[pltpu.with_memory_space_constraint(v, pltpu.HBM) for v in raw], *[pltpu.with_memory_space_constraint(v, pltpu.VMEM) for v in ins])


def pair_perm(axis, step):
    return [(i, i ^ step) for i in range(lax.axis_size(axis))]


def parity():
    value = lax.axis_index("col")
    for shift in range(1, lax.axis_size("col").bit_length()):
        value = xor(value, lax.shift_right_logical(lax.axis_index("col"), jnp.int32(shift)))
    return lax.rem(xor(value, lax.axis_index("row")), 2)


def hop(step):
    return 2 * step + step.bit_count() % 2


def mate_perm():
    cols = lax.axis_size("col")
    return [(i * cols + j, (i ^ 1) * cols + (j ^ 1)) for i in range(lax.axis_size("row")) for j in range(cols)]


def xor(a, b):
    return jnp.bitwise_xor(a, b)


def cross(slot):
    return 2 * slot + 1 if slot else 0


def part(start, size):
    return pl.ds(pl.multiple_of(start, size), size)


def dot_nt(left, right):
    return lax.dot_general(left, right, (((1,), (1,)), ((), ())), preferred_element_type=F32)


def dot_nn(left, right):
    return jnp.dot(left, right, preferred_element_type=F32)


def three(value):
    pieces = []
    for _ in range(3):
        pieces.append(value.astype(BF))
        value = value - pieces[-1].astype(F32)
    return pieces


def adjoint(freq, v_ref, k_ref, o_ref, u_ref):
    rows = v_ref.shape[0]
    tiles = u_ref.shape[0] // 2
    x = v_ref[:, freq].reshape(2 * rows, v_ref.shape[3])
    for c in range(2):
        y = dot_nn(x, k_ref[c])
        for t in range(tiles):
            u_ref[c * tiles + t] = y[:, t * LANES:(t + 1) * LANES]
    real = pl.ds(0, rows, stride=2)
    imag = pl.ds(1, rows, stride=2)
    for t in range(tiles):
        at = slice(t * LANES, (t + 1) * LANES)
        o_ref[:rows, at] = (u_ref[t, real, :] + u_ref[tiles + t, imag, :]).astype(o_ref.dtype)
        o_ref[rows:, at] = (u_ref[t, imag, :] - u_ref[tiles + t, real, :]).astype(o_ref.dtype)


def adjoint_other_body(v_hbm, k_hbm, d_hbm, n_hbm, o_ref, v_ref, other_ref, d_ref, n_ref, u_ref, sems):
    freq = 1 - parity()
    pairs = (
        (v_hbm, v_ref),
        (k_hbm.at[freq], other_ref),
        (d_hbm, d_ref),
        (n_hbm, n_ref),
    )
    copies = [pltpu.make_async_copy(*pair, sems.at[n]) for n, pair in enumerate(pairs)]
    for copy in copies:
        copy.start()
    copies[0].wait()
    copies[1].wait()
    adjoint(freq, v_ref, other_ref, o_ref, u_ref)
    for copy in copies[2:]:
        copy.wait()


def adjoint_own_body(k_hbm, v_ref, o_ref, k_ref, u_ref, sem):
    freq = parity()
    copy = pltpu.make_async_copy(k_hbm.at[freq], k_ref, sem)
    copy.start()
    copy.wait()
    adjoint(freq, v_ref, k_ref, o_ref, u_ref)


def lanes_of(freq, c, rows):
    return part((freq * 2 + c) * rows, rows)


def seam_body(mine_ref, other_ref, d_ref, o_ref):
    _, rows, width = mine_ref.shape
    odd = lax.rem(lax.axis_index("row"), 2)
    at = lax.broadcasted_iota(jnp.int32, (8, width), 0)
    place = lax.broadcasted_iota(jnp.int32, (8, width), 1)
    pick = jnp.where((at < 2) & (place == at + odd * (width - 2)), 1.0, 0.0).astype(BF)
    coef = d_ref[...]
    spot = lax.broadcasted_iota(jnp.int32, coef.shape, 1)
    edge = jnp.sum(jnp.where(spot == odd * (width - 1), coef, 0.0), axis=1, keepdims=True)
    lines = [jnp.zeros((2, rows), F32)]
    lines += [jnp.broadcast_to(piece.astype(F32), (1, rows)) for piece in three(edge)]
    lines = jnp.concatenate(lines + [jnp.zeros((3, rows), F32)], axis=0)
    for freq, ref in ((parity(), mine_ref), (1 - parity(), other_ref)):
        for c in range(2):
            o_ref[:, lanes_of(freq, c, rows)] = (dot_nt(pick, ref[c]) + lines).astype(BF)


def fence_body(d_ref, o_ref):
    o_ref[...] = jnp.zeros_like(o_ref)


def stencil_matrix(coef, block):
    width = coef.shape[1]
    row_at = lax.broadcasted_iota(jnp.int32, (width, width), 0)
    col_at = lax.broadcasted_iota(jnp.int32, (width, width), 1)
    wide = jnp.broadcast_to(coef, (width, width))
    tall = jnp.sum(jnp.where(row_at == col_at, wide, 0.0), axis=1, keepdims=True)
    gap = jnp.abs(row_at - col_at)
    first = (row_at == 0) & (block == 0)
    last = (row_at == width - 1) & (block == lax.axis_size("row") - 1)
    centre = wide * wide + jnp.where(first | last, 1.0, 2.0)
    matrix = jnp.where(gap == 0, centre, jnp.where(gap == 1, -(wide + tall), jnp.where(gap == 2, 1.0, 0.0)))
    upper = matrix.astype(BF)
    return upper, (matrix - upper.astype(F32)).astype(BF)


def operator_body(swap, k_ref, mate_ref, d_ref, got_ref, near_ref, far_ref, o_ref):
    _, rows, width = k_ref.shape
    freq = 1 - parity() if swap else parity()
    me = lax.axis_index("row")
    odd = lax.rem(me, 2)
    is_odd = odd == 1
    at = lax.broadcasted_iota(jnp.int32, (8, width), 0)
    place = lax.broadcasted_iota(jnp.int32, (8, width), 1)
    own_pick = jnp.where((at < 2) & (place == at + (1 - odd) * (width - 2)), 1.0, 0.0).astype(BF)
    mate_pick = jnp.where((at < 2) & (place == at + odd * (width - 2)), 1.0, 0.0).astype(BF)
    coef = d_ref[...]
    tail = got_ref[got_ref.shape[0] - 16:, :].astype(F32)
    mate_coef = tail[0:1] + tail[1:2] + tail[2:3]

    def last_or_first(value, last):
        return jnp.where(last, value[:, width - 1:], value[:, :1])

    def outer(ref, block, c):
        last = lax.axis_size("row") - 1
        there = jnp.where(lax.rem(block, 2) == 1, block < last, block > 0)
        full = jnp.where(there, ref[:, lanes_of(freq, c, rows)].astype(F32), 0.0)
        return full[0:2], full[2:3, :1] + full[3:4, :1] + full[4:5, :1]

    sides = (
        (k_ref, coef, me, near_ref, mate_ref, mate_pick, last_or_first(mate_coef, is_odd), is_odd),
        (mate_ref, mate_coef, xor(me, 1), far_ref, k_ref, own_pick, last_or_first(coef, ~is_odd), ~is_odd),
    )
    for n, (ref, c_block, block, outer_ref, inner_ref, pick, inside_coef, inner_left) in enumerate(sides):
        upper, lower = stencil_matrix(c_block, block)
        for c in range(2):
            beyond, outside_coef = outer(outer_ref, block, c)
            left_coef = jnp.where(inner_left, inside_coef, outside_coef) + c_block[:, :1]
            right_coef = jnp.where(inner_left, outside_coef, inside_coef) + c_block[:, width - 1:]
            own = ref[c]
            value = dot_nt(upper, own) + dot_nt(lower, own)
            inside = dot_nt(pick, inner_ref[c])[0:2]
            left = jnp.where(inner_left, inside, beyond)
            right = jnp.where(inner_left, beyond, inside)
            extra = jnp.concatenate(
                [
                    left[0:1] - left_coef * left[1:2],
                    left[1:2],
                    jnp.zeros((width - 4, rows), F32),
                    right[0:1],
                    right[1:2] - right_coef * right[0:1],
                ],
                axis=0,
            )
            o_ref[c, n * width:(n + 1) * width] = (value + extra).astype(BF)


def split_body(own_ref, got_ref, keep_ref, *send_refs):
    chips = len(send_refs) + 1
    blocks = lax.axis_size("row")
    probes = own_ref.shape[0] // 2
    block = probes // blocks
    size = block // chips
    chip = lax.div(lax.axis_index("col"), 2)
    me = lax.axis_index("row")
    for step, ref in enumerate((keep_ref,) + send_refs):
        target = xor(chip, step)
        at = 0
        for mate in range(2):
            for slot in range(blocks // 2):
                for c in range(2):
                    lo = c * probes + xor(me, mate ^ cross(slot)) * block + target * size
                    rows = part(lo, size)
                    ref[at:at + size] = (own_ref[rows, :] + got_ref[rows, :].astype(F32)).astype(ref.dtype)
                    at += size


def sum_body(keep_ref, d_ref, fence_ref, *refs):
    stay_ref, give_ref = refs[-2:]
    size = stay_ref.shape[0]
    total = keep_ref[...]
    for ref in refs[:-2]:
        total = total + ref[...].astype(F32)
    stay_ref[...] = total[:size].astype(BF)
    give_ref[:size] = total[size:].astype(BF)
    pad = jnp.zeros((13, d_ref.shape[1]), BF)
    give_ref[size:] = jnp.concatenate(three(d_ref[...]) + [pad], axis=0)


def pack_body(stay_ref, got_ref, fence_ref, o_ref):
    size = stay_ref.shape[0]
    o_ref[:size] = stay_ref[...]
    o_ref[size:] = got_ref[:size]


def join_body(mine_ref, *refs):
    away_ref, stay_ref = refs[-2:]
    pieces = (mine_ref,) + refs[:-2]
    chips = len(pieces)
    blocks = lax.axis_size("row")
    size = mine_ref.shape[0] // (2 * blocks)
    chip = lax.div(lax.axis_index("col"), 2)
    for step, ref in enumerate(pieces):
        source = xor(chip, step)
        for n in range(2 * blocks):
            block, inner = divmod(n, blocks)
            if inner < 2:
                out_ref, lo = stay_ref, block * 2 + inner
            else:
                out_ref, lo = away_ref, block * (blocks - 2) + inner - 2
            out_ref[part(lo * chips * size + source * size, size), :] = ref[n * size:(n + 1) * size]


def predict(a_ref, k_ref, targets, kind):
    half = a_ref.shape[0] // 2
    width = a_ref.shape[1]
    size = half // (2 * len(targets))
    total = []
    for c in range(2):
        value = dot_nn(a_ref[:half], k_ref[c, :width])
        total.append(value + dot_nn(a_ref[half:], k_ref[c, width:]))
    by_real, by_imag = total
    for slot, ref in enumerate(targets):
        lo = 2 * slot * size
        mid = lo + size
        hi = mid + size
        ref[:size] = (by_real[lo:mid] - by_imag[mid:hi]).astype(kind)
        ref[size:] = (by_real[mid:hi] + by_imag[lo:mid]).astype(kind)


def predict_own_body(away_ref, stay_ref, k_ref, keep_ref, *owns):
    predict(away_ref, k_ref, owns, BF)
    predict(stay_ref, k_ref, (keep_ref,), F32)


def predict_away_body(peers, away_ref, k_ref, *refs):
    owns, sends = refs[:peers], refs[peers:]
    size = owns[0].shape[0]
    freq = parity()
    for own, send in zip(owns, sends):
        send[part(freq * size, size), :] = own[...]
    rest = part((1 - freq) * size, size)
    predict(away_ref, k_ref, tuple(send.at[rest] for send in sends), BF)


def predict_stay_body(stay_ref, k_ref, keep_ref):
    predict(stay_ref, k_ref, (keep_ref,), F32)


def final_body(v_ref, noise_ref, own_ref, other_ref, *refs):
    out_hbm, s_ref, y_ref, sems = refs[-4:]
    size = y_ref.shape[0]
    half = 2 * size
    step = size // PIECES
    me = lax.axis_index("row")
    freq = parity()
    copies = []
    for n in range(PIECES):
        lo = n * step
        for which, keep_ref in enumerate((own_ref, other_ref)):
            f = freq if which == 0 else 1 - freq
            for c in range(2):
                at = c * size + lo
                total = keep_ref[at:at + step]
                for ref in refs[:-4]:
                    total = total + ref[part(f * half + at, step), :].astype(F32)
                for t in range(s_ref.shape[0]):
                    s_ref[t, pl.ds(4 * lo + 2 * f + c, step, stride=4), :] = total[:, t * LANES:(t + 1) * LANES]
        x = v_ref[part(me * size + lo, step)].reshape(4 * step, v_ref.shape[3]).astype(F32)
        kind = lax.rem(lax.broadcasted_iota(jnp.int32, x.shape, 0), 4)
        noise = jnp.where(kind < 2, noise_ref[0:1, :], noise_ref[1:2, :])
        sums = [s_ref[t, 4 * lo:4 * (lo + step)] for t in range(s_ref.shape[0])]
        values = jnp.concatenate(sums, axis=1) + noise * x
        y_ref[lo:lo + step] = values.reshape((step,) + y_ref.shape[1:])
        rows = pl.ds(lo, step)
        copies.append(pltpu.make_async_copy(y_ref.at[rows], out_hbm.at[rows], sems.at[n]))
        copies[-1].start()
    for copy in copies:
        copy.wait()


def finish(ins, shape):
    ins = [pltpu.with_memory_space_constraint(v, pltpu.VMEM) for v in ins]
    return pl.pallas_call(
        final_body,
        name="final",
        in_specs=[VMEM] * len(ins),
        out_specs=HBM,
        out_shape=jax.ShapeDtypeStruct(shape, F32),
        scratch_shapes=[
            pltpu.VMEM((shape[3] // LANES, 4 * shape[0], LANES), F32),
            pltpu.VMEM(shape, F32),
            pltpu.SemaphoreType.DMA((PIECES,)),
        ],
        compiler_params=pltpu.CompilerParams(vmem_limit_bytes=LIMIT),
    )(*ins)


def wide_sum(own, got, coef, blocks):
    rows, width = own.shape
    a = parity()
    value = own + got.astype(F32)
    both = jnp.where(a == 0, jnp.stack([value, 0 * value]), jnp.stack([0 * value, value]))
    both = lax.psum(both, "col").astype(BF).reshape(2, 2, blocks, -1, width)
    slots = jnp.array([cross(slot) for slot in range(blocks // 2)])
    me = lax.axis_index("row")

    def chosen(freq, mate):
        value = lax.dynamic_index_in_dim(both, freq, 0, keepdims=False)
        value = jnp.take(value, xor(me, xor(mate, slots)), axis=1)
        return value.transpose(1, 0, 2, 3).reshape(-1, width)

    tail = jnp.concatenate(three(coef) + [jnp.zeros((13, width), BF)], axis=0)
    give = jnp.concatenate([chosen(0, 1), chosen(1, 1), tail], axis=0)
    give = lax.ppermute(give, "row", pair_perm("row", 1))
    fields = []
    for freq in (a, 1 - a):
        mate = lax.dynamic_slice_in_dim(give, freq * (rows // 2), rows // 2, 0)
        field = jnp.stack([chosen(freq, 0), mate]).reshape(2, blocks // 2, -1, width)
        fields.append((field[:, 1:].reshape(-1, width), field[:, 0].reshape(-1, width)))
    return (*fields, give)


def chip_sum(own, got, coef, blocks, chips):
    rows, width = own.shape
    size = rows // chips
    keep, *sends = call(split_body, (own, got), [((size, width), F32)] + [((size, width), BF)] * (chips - 1))
    fence = call(fence_body, (coef,), [((8, LANES), F32)])[0]
    got = [lax.ppermute(v, "col", pair_perm("col", hop(d + 1))) for d, v in enumerate(sends)]
    stay, give = call(sum_body, (keep, coef, fence, *got), [((size // 2, width), BF), ((size // 2 + 16, width), BF)])
    fence = call(fence_body, (coef,), [((8, LANES), F32)])[0]
    give = lax.ppermute(give, ("row", "col"), mate_perm())
    mine = call(pack_body, (stay, give, fence), [((size, width), BF)])[0]
    got = [lax.ppermute(mine, "col", pair_perm("col", hop(d + 1))) for d in range(chips - 1)]
    stay = 4 * rows // (2 * blocks)
    mine = call(join_body, (mine, *got), [((rows - stay, width), BF), ((stay, width), BF)])
    other = [lax.ppermute(v, "col", pair_perm("col", 1)) for v in mine]
    return mine, other, give


def apply(kernel, probes, noise_var, prior_diag):
    count = probes.shape[0]
    rows, width = kernel.shape[2:]
    blocks = lax.axis_size("row")
    chips = lax.axis_size("col") // 2
    coef = prior_diag[None, :]
    scratch = pltpu.VMEM((2 * width // LANES, 2 * count, LANES), F32)
    block = kernel.shape[1:]
    other, probes, k_other, coef, noise = call(
        adjoint_other_body,
        (),
        [
            ((2 * count, width), BF),
            (probes.shape, BF),
            (block, BF),
            (coef.shape, F32),
            (noise_var.shape, F32),
        ],
        (scratch, pltpu.SemaphoreType.DMA((4,))),
        raw=(probes, kernel, coef, noise_var),
    )
    got = lax.ppermute(other, "col", pair_perm("col", 1))
    mate_own = lax.ppermute(k_other, "row", pair_perm("row", 1))
    own, k_own = call(
        adjoint_own_body,
        (probes,),
        [((2 * count, width), F32), (block, BF)],
        (scratch, pltpu.SemaphoreType.DMA),
        raw=(kernel,),
    )
    mate_other = lax.ppermute(k_own, "row", pair_perm("row", 1))
    seam = call(seam_body, (k_own, k_other, coef), [((8, 4 * rows), BF)])[0]
    odd = [i for i in range(blocks) if i % 2]
    even = [i for i in range(blocks) if i % 2 == 0]
    near = [(i, (i + 1) % blocks) for i in odd] + [(i, (i - 1) % blocks) for i in even]
    far = [(i, i + 2 if i + 2 < blocks else 1) for i in odd] + [(i, i - 2 if i else blocks - 2) for i in even]
    near = lax.ppermute(seam, "row", near)
    far = lax.ppermute(seam, "row", far)
    if chips > 4:
        mine, other, give = wide_sum(own, got, coef, blocks)
    else:
        mine, other, give = chip_sum(own, got, coef, blocks, chips)
    operators = [
        call(
            functools.partial(operator_body, swap), (block_k, mate, coef, give, near, far), [((2, 2 * width, rows), BF)]
        )[0]
        for swap, block_k, mate in ((False, k_own, mate_own), (True, k_other, mate_other))
    ]
    size = count // blocks
    peers = blocks // 2 - 1
    half = (2 * size, rows)
    keep_own, *owns = call(predict_own_body, (*mine, operators[0]), [(half, F32)] + [(half, BF)] * peers)
    sends = call(
        functools.partial(predict_away_body, peers), (other[0], operators[1], *owns), [((4 * size, rows), BF)] * peers
    )
    got = [lax.ppermute(v, "row", pair_perm("row", cross(d + 1))) for d, v in enumerate(sends)]
    keep_other = call(predict_stay_body, (other[1], operators[1]), [(half, F32)])[0]
    shape = (size,) + probes.shape[1:3] + (rows,)
    return finish((probes, noise, keep_own, keep_other, *got), shape)


def solution(mesh):
    in_specs = (P(None, None, "col", "row"), P(None, None, None, "col"), P(None, "col"), P("row"))
    out_specs = P("row", None, None, "col")
    return jax.shard_map(apply, mesh=mesh, in_specs=in_specs, out_specs=out_specs, check_vma=False)
```

```python
import functools

import jax
import jax.numpy as jnp
from jax import lax
from jax.experimental import pallas as pl
from jax.experimental.pallas import tpu as pltpu
from jax.sharding import PartitionSpec as P


BF = jnp.bfloat16
F32 = jnp.float32
LANES = 128
PIECES = 4
LIMIT = 24 * 2**20
VMEM = pl.BlockSpec(memory_space=pltpu.VMEM)
HBM = pl.BlockSpec(memory_space=pltpu.HBM)


def call(body, ins, outs, scratch=(), raw=()):
    return pl.pallas_call(
        body,
        in_specs=[HBM] * len(raw) + [VMEM] * len(ins),
        out_specs=[VMEM] * len(outs),
        out_shape=[pltpu.VMEM(*o) for o in outs],
        scratch_shapes=list(scratch),
        compiler_params=pltpu.CompilerParams(vmem_limit_bytes=LIMIT),
    )(*[pltpu.with_memory_space_constraint(v, pltpu.HBM) for v in raw], *[pltpu.with_memory_space_constraint(v, pltpu.VMEM) for v in ins])


def pair_perm(axis, step):
    return [(i, i ^ step) for i in range(lax.axis_size(axis))]


def parity():
    value = lax.axis_index("col")
    for shift in range(1, lax.axis_size("col").bit_length()):
        value = xor(value, lax.shift_right_logical(lax.axis_index("col"), jnp.int32(shift)))
    return lax.rem(xor(value, lax.axis_index("row")), 2)


def hop(step):
    return 2 * step + step.bit_count() % 2


def mate_perm():
    cols = lax.axis_size("col")
    return [(i * cols + j, (i ^ 1) * cols + (j ^ 1)) for i in range(lax.axis_size("row")) for j in range(cols)]


def xor(a, b):
    return jnp.bitwise_xor(a, b)


def cross(slot):
    return 2 * slot + 1 if slot else 0


def part(start, size):
    return pl.ds(pl.multiple_of(start, size), size)


def dot_nt(left, right):
    return lax.dot_general(left, right, (((1,), (1,)), ((), ())), preferred_element_type=F32)


def dot_nn(left, right):
    return jnp.dot(left, right, preferred_element_type=F32)


def three(value):
    pieces = []
    for _ in range(3):
        pieces.append(value.astype(BF))
        value = value - pieces[-1].astype(F32)
    return pieces


def adjoint(freq, v_ref, k_ref, o_ref, u_ref):
    rows = v_ref.shape[0]
    tiles = u_ref.shape[0] // 2
    x = v_ref[:, freq].reshape(2 * rows, v_ref.shape[3])
    for c in range(2):
        y = dot_nn(x, k_ref[c])
        for t in range(tiles):
            u_ref[c * tiles + t] = y[:, t * LANES:(t + 1) * LANES]
    real = pl.ds(0, rows, stride=2)
    imag = pl.ds(1, rows, stride=2)
    for t in range(tiles):
        at = slice(t * LANES, (t + 1) * LANES)
        o_ref[:rows, at] = (u_ref[t, real, :] + u_ref[tiles + t, imag, :]).astype(o_ref.dtype)
        o_ref[rows:, at] = (u_ref[t, imag, :] - u_ref[tiles + t, real, :]).astype(o_ref.dtype)


def adjoint_other_body(v_hbm, k_hbm, d_hbm, n_hbm, o_ref, v_ref, mine_ref, other_ref, d_ref, n_ref, u_ref, sems):
    freq = 1 - parity()
    pairs = (
        (v_hbm, v_ref),
        (k_hbm.at[freq], other_ref),
        (k_hbm.at[1 - freq], mine_ref),
        (d_hbm, d_ref),
        (n_hbm, n_ref),
    )
    copies = [pltpu.make_async_copy(*pair, sems.at[n]) for n, pair in enumerate(pairs)]
    for copy in copies:
        copy.start()
    copies[0].wait()
    copies[1].wait()
    adjoint(freq, v_ref, other_ref, o_ref, u_ref)
    for copy in copies[2:]:
        copy.wait()


def adjoint_own_body(v_ref, k_ref, o_ref, u_ref):
    adjoint(parity(), v_ref, k_ref, o_ref, u_ref)


def lanes_of(freq, c, rows):
    return part((freq * 2 + c) * rows, rows)


def seam_body(mine_ref, other_ref, d_ref, o_ref):
    _, rows, width = mine_ref.shape
    odd = lax.rem(lax.axis_index("row"), 2)
    at = lax.broadcasted_iota(jnp.int32, (8, width), 0)
    place = lax.broadcasted_iota(jnp.int32, (8, width), 1)
    pick = jnp.where((at < 2) & (place == at + odd * (width - 2)), 1.0, 0.0).astype(BF)
    coef = d_ref[...]
    spot = lax.broadcasted_iota(jnp.int32, coef.shape, 1)
    edge = jnp.sum(jnp.where(spot == odd * (width - 1), coef, 0.0), axis=1, keepdims=True)
    lines = [jnp.zeros((2, rows), F32)]
    lines += [jnp.broadcast_to(piece.astype(F32), (1, rows)) for piece in three(edge)]
    lines = jnp.concatenate(lines + [jnp.zeros((3, rows), F32)], axis=0)
    for freq, ref in ((parity(), mine_ref), (1 - parity(), other_ref)):
        for c in range(2):
            o_ref[:, lanes_of(freq, c, rows)] = (dot_nt(pick, ref[c]) + lines).astype(BF)


def fence_body(d_ref, o_ref):
    o_ref[...] = jnp.zeros_like(o_ref)


def stencil_matrix(coef, block):
    width = coef.shape[1]
    row_at = lax.broadcasted_iota(jnp.int32, (width, width), 0)
    col_at = lax.broadcasted_iota(jnp.int32, (width, width), 1)
    wide = jnp.broadcast_to(coef, (width, width))
    tall = jnp.sum(jnp.where(row_at == col_at, wide, 0.0), axis=1, keepdims=True)
    gap = jnp.abs(row_at - col_at)
    first = (row_at == 0) & (block == 0)
    last = (row_at == width - 1) & (block == lax.axis_size("row") - 1)
    centre = wide * wide + jnp.where(first | last, 1.0, 2.0)
    matrix = jnp.where(gap == 0, centre, jnp.where(gap == 1, -(wide + tall), jnp.where(gap == 2, 1.0, 0.0)))
    upper = matrix.astype(BF)
    return upper, (matrix - upper.astype(F32)).astype(BF)


def operator_body(swap, k_ref, mate_ref, d_ref, got_ref, near_ref, far_ref, o_ref):
    _, rows, width = k_ref.shape
    freq = 1 - parity() if swap else parity()
    me = lax.axis_index("row")
    odd = lax.rem(me, 2)
    is_odd = odd == 1
    at = lax.broadcasted_iota(jnp.int32, (8, width), 0)
    place = lax.broadcasted_iota(jnp.int32, (8, width), 1)
    own_pick = jnp.where((at < 2) & (place == at + (1 - odd) * (width - 2)), 1.0, 0.0).astype(BF)
    mate_pick = jnp.where((at < 2) & (place == at + odd * (width - 2)), 1.0, 0.0).astype(BF)
    coef = d_ref[...]
    tail = got_ref[got_ref.shape[0] - 16:, :].astype(F32)
    mate_coef = tail[0:1] + tail[1:2] + tail[2:3]

    def last_or_first(value, last):
        return jnp.where(last, value[:, width - 1:], value[:, :1])

    def outer(ref, block, c):
        last = lax.axis_size("row") - 1
        there = jnp.where(lax.rem(block, 2) == 1, block < last, block > 0)
        full = jnp.where(there, ref[:, lanes_of(freq, c, rows)].astype(F32), 0.0)
        return full[0:2], full[2:3, :1] + full[3:4, :1] + full[4:5, :1]

    sides = (
        (k_ref, coef, me, near_ref, mate_ref, mate_pick, last_or_first(mate_coef, is_odd), is_odd),
        (mate_ref, mate_coef, xor(me, 1), far_ref, k_ref, own_pick, last_or_first(coef, ~is_odd), ~is_odd),
    )
    for n, (ref, c_block, block, outer_ref, inner_ref, pick, inside_coef, inner_left) in enumerate(sides):
        upper, lower = stencil_matrix(c_block, block)
        for c in range(2):
            beyond, outside_coef = outer(outer_ref, block, c)
            left_coef = jnp.where(inner_left, inside_coef, outside_coef) + c_block[:, :1]
            right_coef = jnp.where(inner_left, outside_coef, inside_coef) + c_block[:, width - 1:]
            own = ref[c]
            value = dot_nt(upper, own) + dot_nt(lower, own)
            inside = dot_nt(pick, inner_ref[c])[0:2]
            left = jnp.where(inner_left, inside, beyond)
            right = jnp.where(inner_left, beyond, inside)
            extra = jnp.concatenate(
                [
                    left[0:1] - left_coef * left[1:2],
                    left[1:2],
                    jnp.zeros((width - 4, rows), F32),
                    right[0:1],
                    right[1:2] - right_coef * right[0:1],
                ],
                axis=0,
            )
            o_ref[c, n * width:(n + 1) * width] = (value + extra).astype(BF)


def split_body(own_ref, got_ref, keep_ref, *send_refs):
    chips = len(send_refs) + 1
    blocks = lax.axis_size("row")
    probes = own_ref.shape[0] // 2
    block = probes // blocks
    size = block // chips
    chip = lax.div(lax.axis_index("col"), 2)
    me = lax.axis_index("row")
    for step, ref in enumerate((keep_ref,) + send_refs):
        target = xor(chip, step)
        at = 0
        for mate in range(2):
            for slot in range(blocks // 2):
                for c in range(2):
                    lo = c * probes + xor(me, mate ^ cross(slot)) * block + target * size
                    rows = part(lo, size)
                    ref[at:at + size] = (own_ref[rows, :] + got_ref[rows, :].astype(F32)).astype(ref.dtype)
                    at += size


def sum_body(keep_ref, d_ref, fence_ref, *refs):
    stay_ref, give_ref = refs[-2:]
    size = stay_ref.shape[0]
    total = keep_ref[...]
    for ref in refs[:-2]:
        total = total + ref[...].astype(F32)
    stay_ref[...] = total[:size].astype(BF)
    give_ref[:size] = total[size:].astype(BF)
    pad = jnp.zeros((13, d_ref.shape[1]), BF)
    give_ref[size:] = jnp.concatenate(three(d_ref[...]) + [pad], axis=0)


def pack_body(stay_ref, got_ref, fence_ref, o_ref):
    size = stay_ref.shape[0]
    o_ref[:size] = stay_ref[...]
    o_ref[size:] = got_ref[:size]


def join_body(mine_ref, *refs):
    away_ref, stay_ref = refs[-2:]
    pieces = (mine_ref,) + refs[:-2]
    chips = len(pieces)
    blocks = lax.axis_size("row")
    size = mine_ref.shape[0] // (2 * blocks)
    chip = lax.div(lax.axis_index("col"), 2)
    for step, ref in enumerate(pieces):
        source = xor(chip, step)
        for n in range(2 * blocks):
            block, inner = divmod(n, blocks)
            if inner < 2:
                out_ref, lo = stay_ref, block * 2 + inner
            else:
                out_ref, lo = away_ref, block * (blocks - 2) + inner - 2
            out_ref[part(lo * chips * size + source * size, size), :] = ref[n * size:(n + 1) * size]


def predict(a_ref, k_ref, targets, kind):
    half = a_ref.shape[0] // 2
    width = a_ref.shape[1]
    size = half // (2 * len(targets))
    total = []
    for c in range(2):
        value = dot_nn(a_ref[:half], k_ref[c, :width])
        total.append(value + dot_nn(a_ref[half:], k_ref[c, width:]))
    by_real, by_imag = total
    for slot, ref in enumerate(targets):
        lo = 2 * slot * size
        mid = lo + size
        hi = mid + size
        ref[:size] = (by_real[lo:mid] - by_imag[mid:hi]).astype(kind)
        ref[size:] = (by_real[mid:hi] + by_imag[lo:mid]).astype(kind)


def predict_own_body(away_ref, stay_ref, k_ref, keep_ref, *owns):
    predict(away_ref, k_ref, owns, BF)
    predict(stay_ref, k_ref, (keep_ref,), F32)


def predict_away_body(peers, away_ref, k_ref, *refs):
    owns, sends = refs[:peers], refs[peers:]
    size = owns[0].shape[0]
    freq = parity()
    for own, send in zip(owns, sends):
        send[part(freq * size, size), :] = own[...]
    rest = part((1 - freq) * size, size)
    predict(away_ref, k_ref, tuple(send.at[rest] for send in sends), BF)


def predict_stay_body(stay_ref, k_ref, keep_ref):
    predict(stay_ref, k_ref, (keep_ref,), F32)


def final_body(v_ref, noise_ref, own_ref, other_ref, *refs):
    out_hbm, s_ref, y_ref, sems = refs[-4:]
    size = y_ref.shape[0]
    half = 2 * size
    step = size // PIECES
    me = lax.axis_index("row")
    freq = parity()
    copies = []
    for n in range(PIECES):
        lo = n * step
        for which, keep_ref in enumerate((own_ref, other_ref)):
            f = freq if which == 0 else 1 - freq
            for c in range(2):
                at = c * size + lo
                total = keep_ref[at:at + step]
                for ref in refs[:-4]:
                    total = total + ref[part(f * half + at, step), :].astype(F32)
                for t in range(s_ref.shape[0]):
                    s_ref[t, pl.ds(4 * lo + 2 * f + c, step, stride=4), :] = total[:, t * LANES:(t + 1) * LANES]
        x = v_ref[part(me * size + lo, step)].reshape(4 * step, v_ref.shape[3]).astype(F32)
        kind = lax.rem(lax.broadcasted_iota(jnp.int32, x.shape, 0), 4)
        noise = jnp.where(kind < 2, noise_ref[0:1, :], noise_ref[1:2, :])
        sums = [s_ref[t, 4 * lo:4 * (lo + step)] for t in range(s_ref.shape[0])]
        values = jnp.concatenate(sums, axis=1) + noise * x
        y_ref[lo:lo + step] = values.reshape((step,) + y_ref.shape[1:])
        rows = pl.ds(lo, step)
        copies.append(pltpu.make_async_copy(y_ref.at[rows], out_hbm.at[rows], sems.at[n]))
        copies[-1].start()
    for copy in copies:
        copy.wait()


def finish(ins, shape):
    ins = [pltpu.with_memory_space_constraint(v, pltpu.VMEM) for v in ins]
    return pl.pallas_call(
        final_body,
        name="final",
        in_specs=[VMEM] * len(ins),
        out_specs=HBM,
        out_shape=jax.ShapeDtypeStruct(shape, F32),
        scratch_shapes=[
            pltpu.VMEM((shape[3] // LANES, 4 * shape[0], LANES), F32),
            pltpu.VMEM(shape, F32),
            pltpu.SemaphoreType.DMA((PIECES,)),
        ],
        compiler_params=pltpu.CompilerParams(vmem_limit_bytes=LIMIT),
    )(*ins)


def wide_sum(own, got, coef, blocks):
    rows, width = own.shape
    a = parity()
    value = own + got.astype(F32)
    both = jnp.where(a == 0, jnp.stack([value, 0 * value]), jnp.stack([0 * value, value]))
    both = lax.psum(both, "col").astype(BF).reshape(2, 2, blocks, -1, width)
    slots = jnp.array([cross(slot) for slot in range(blocks // 2)])
    me = lax.axis_index("row")

    def chosen(freq, mate):
        value = lax.dynamic_index_in_dim(both, freq, 0, keepdims=False)
        value = jnp.take(value, xor(me, xor(mate, slots)), axis=1)
        return value.transpose(1, 0, 2, 3).reshape(-1, width)

    tail = jnp.concatenate(three(coef) + [jnp.zeros((13, width), BF)], axis=0)
    give = jnp.concatenate([chosen(0, 1), chosen(1, 1), tail], axis=0)
    give = lax.ppermute(give, "row", pair_perm("row", 1))
    fields = []
    for freq in (a, 1 - a):
        mate = lax.dynamic_slice_in_dim(give, freq * (rows // 2), rows // 2, 0)
        field = jnp.stack([chosen(freq, 0), mate]).reshape(2, blocks // 2, -1, width)
        fields.append((field[:, 1:].reshape(-1, width), field[:, 0].reshape(-1, width)))
    return (*fields, give)


def chip_sum(own, got, coef, blocks, chips):
    rows, width = own.shape
    size = rows // chips
    keep, *sends = call(split_body, (own, got), [((size, width), F32)] + [((size, width), BF)] * (chips - 1))
    fence = call(fence_body, (coef,), [((8, LANES), F32)])[0]
    got = [lax.ppermute(v, "col", pair_perm("col", hop(d + 1))) for d, v in enumerate(sends)]
    stay, give = call(sum_body, (keep, coef, fence, *got), [((size // 2, width), BF), ((size // 2 + 16, width), BF)])
    fence = call(fence_body, (coef,), [((8, LANES), F32)])[0]
    give = lax.ppermute(give, ("row", "col"), mate_perm())
    mine = call(pack_body, (stay, give, fence), [((size, width), BF)])[0]
    got = [lax.ppermute(mine, "col", pair_perm("col", hop(d + 1))) for d in range(chips - 1)]
    stay = 4 * rows // (2 * blocks)
    mine = call(join_body, (mine, *got), [((rows - stay, width), BF), ((stay, width), BF)])
    other = [lax.ppermute(v, "col", pair_perm("col", 1)) for v in mine]
    return mine, other, give


def apply(kernel, probes, noise_var, prior_diag):
    count = probes.shape[0]
    rows, width = kernel.shape[2:]
    blocks = lax.axis_size("row")
    chips = lax.axis_size("col") // 2
    coef = prior_diag[None, :]
    scratch = pltpu.VMEM((2 * width // LANES, 2 * count, LANES), F32)
    block = kernel.shape[1:]
    other, probes, k_own, k_other, coef, noise = call(
        adjoint_other_body,
        (),
        [
            ((2 * count, width), BF),
            (probes.shape, BF),
            (block, BF),
            (block, BF),
            (coef.shape, F32),
            (noise_var.shape, F32),
        ],
        (scratch, pltpu.SemaphoreType.DMA((5,))),
        raw=(probes, kernel, coef, noise_var),
    )
    got = lax.ppermute(other, "col", pair_perm("col", 1))
    mate_own = lax.ppermute(k_other, "row", pair_perm("row", 1))
    mate_other = lax.ppermute(k_own, "row", pair_perm("row", 1))
    own = call(adjoint_own_body, (probes, k_own), [((2 * count, width), F32)], (scratch,))[0]
    seam = call(seam_body, (k_own, k_other, coef), [((8, 4 * rows), BF)])[0]
    odd = [i for i in range(blocks) if i % 2]
    even = [i for i in range(blocks) if i % 2 == 0]
    near = [(i, (i + 1) % blocks) for i in odd] + [(i, (i - 1) % blocks) for i in even]
    far = [(i, i + 2 if i + 2 < blocks else 1) for i in odd] + [(i, i - 2 if i else blocks - 2) for i in even]
    near = lax.ppermute(seam, "row", near)
    far = lax.ppermute(seam, "row", far)
    if chips > 4:
        mine, other, give = wide_sum(own, got, coef, blocks)
    else:
        mine, other, give = chip_sum(own, got, coef, blocks, chips)
    operators = [
        call(
            functools.partial(operator_body, swap), (block_k, mate, coef, give, near, far), [((2, 2 * width, rows), BF)]
        )[0]
        for swap, block_k, mate in ((False, k_own, mate_own), (True, k_other, mate_other))
    ]
    size = count // blocks
    peers = blocks // 2 - 1
    half = (2 * size, rows)
    keep_own, *owns = call(predict_own_body, (*mine, operators[0]), [(half, F32)] + [(half, BF)] * peers)
    sends = call(
        functools.partial(predict_away_body, peers), (other[0], operators[1], *owns), [((4 * size, rows), BF)] * peers
    )
    got = [lax.ppermute(v, "row", pair_perm("row", cross(d + 1))) for d, v in enumerate(sends)]
    keep_other = call(predict_stay_body, (other[1], operators[1]), [(half, F32)])[0]
    shape = (size,) + probes.shape[1:3] + (rows,)
    return finish((probes, noise, keep_own, keep_other, *got), shape)


def solution(mesh):
    in_specs = (P(None, None, "col", "row"), P(None, None, None, "col"), P(None, "col"), P("row"))
    out_specs = P("row", None, None, "col")
    return jax.shard_map(apply, mesh=mesh, in_specs=in_specs, out_specs=out_specs, check_vma=False)
```
